32 devices in a mesh: dp: 16 (over z, y, x), mp: 2 (over core).
Axes of the slice: x: 2, y: 2, z: 4, core: 2. Of those that a mesh axis runs over, the one named last changes fastest.
Arguments:
- tokens: bfloat16 [16384, 768], P('dp'), may hold values from -6 to 6
- embed_table: bfloat16 [16384, 768], P('dp'), may hold values from -6 to 6
- qkv_weight: bfloat16 [768, 3, 768], P('dp', None, 'mp'), may hold values from -0.21875 to 0.21875
- qv_bias: float32 [2, 768], P(None, 'mp'), may hold values from -3 to 3
- out_weight: bfloat16 [768, 768], P('mp', 'dp'), may hold values from -0.625 to 0.625
- out_bias: float32 [768], replicated, may hold values from -3 to 3
- norm1_gain: float32 [768], replicated, may hold values from 0.5 to 1.5
- norm1_bias: float32 [768], replicated, may hold values from -3 to 3
- in_weight: bfloat16 [768, 3072], P('dp', 'mp'), may hold values from -0.21875 to 0.21875
- in_bias: float32 [3072], P('mp'), may hold values from -3 to 3
- down_weight: bfloat16 [3072, 768], P('mp', 'dp'), may hold values from -0.109375 to 0.109375
- down_bias: float32 [768], replicated, may hold values from -3 to 3
- norm2_gain: float32 [768], replicated, may hold values from 0.5 to 1.5
- norm2_bias: float32 [768], replicated, may hold values from -3 to 3
- masked_pos: int32 [32, 96], P('dp'), may hold values from 0 to 511, as said below
- replace_ids: int32 [32, 96], P('dp'), may hold values from 0 to 16383
- masked_count: int32 [32], P('dp'), may hold values from 48 to 96, as said below
- cotangent: bfloat16 [32, 96, 768], P('dp'), may hold values from -6 to 6
Outputs:
- output: bfloat16 [16384, 768], P('dp')
- grad_input: float32 [16384, 768], P('dp')
- grad_table: float32 [16384, 768], P('dp')
- grad_qkv: float32 [768, 3, 768], P('dp', None, 'mp')
- grad_qv_bias: float32 [2, 2, 384], P(None, 'mp', 'dp')
- grad_out_weight: float32 [768, 768], P('mp', 'dp')
- grad_out_bias: float32 [768], P('dp')
- grad_norm1_gain: float32 [768], P('dp')
- grad_norm1_bias: float32 [768], P('dp')
- grad_in_weight: float32 [768, 3072], P('dp', 'mp')
- grad_in_bias: float32 [2, 1536], P('mp', 'dp')
- grad_down_weight: float32 [3072, 768], P('mp', 'dp')
- grad_down_bias: float32 [768], P('dp')
- grad_norm2_gain: float32 [768], P('dp')
- grad_norm2_bias: float32 [768], P('dp')
The draws below stay inside these ranges and needn't reach their ends.
Inputs may be any that keep to these rules, and one draw needn't show every extreme that they name: `masked_pos`: within each page the 96 positions are distinct. Slots 0 to masked_count - 1 of a page are used; some page uses all 96.
All inputs are finite; a program needn't handle non-finite values.
Results may differ from the reference program's by a relative error of at most 0.015.
The reference program's roundings to bfloat16 on the way count: a program that leaves them out, or rounds other values in their place, can miss the bound.
Values may be sent and summed in bfloat16 or wider, within the bound.
No kernel may reach another device: no remote copies, remote signals or barrier semaphores. Data moves between devices by JAX's collectives and lax.ppermute only.
A program may use at most 192 MiB of HBM per device.

```python
import jax
import jax.numpy as jnp
from jax import lax

D = 768
HEADS = 12
HEAD = 64
FF = 3072
VOCAB = 16384
LEN = 512
CAP = 96
PAGES = 32
TOKENS = 16384
N_MP = 2


def draw_masked_pos(key, part):
    page_keys = jax.random.split(key, PAGES)
    return jax.vmap(lambda single: jax.random.permutation(single, LEN)[:CAP])(page_keys).astype(jnp.int32)


def draw_masked_count(key, part):
    count_key, pick_key = jax.random.split(jax.random.fold_in(key, 7))
    counts = jax.random.randint(count_key, (PAGES,), CAP // 2, CAP + 1)
    fullest = jax.random.randint(pick_key, (), 0, PAGES)
    return jnp.where(jnp.arange(PAGES) == fullest, CAP, counts).astype(jnp.int32)


def touch_ends(entries, own_key, least, high):
    place = [jax.random.randint(jax.random.fold_in(own_key, axis), (), 0, length) for axis, length in enumerate(entries.shape)]
    longest = entries.shape.index(max(entries.shape))
    beside = place[:longest] + [(place[longest] + 1) % entries.shape[longest]] + place[longest + 1:]
    return entries.at[tuple(place)].set(least).at[tuple(beside)].set(high)


def block_levels(key, shape, cuts, low, largest):
    factor_of, own = 1.0, jax.random.fold_in(key, 6)
    for position, parts in cuts:
        steps = jnp.exp(jax.random.uniform(jax.random.fold_in(own, position), (parts,), jnp.float32, low / len(cuts), largest / len(cuts)))
        factor_of = factor_of * jnp.repeat(steps, shape[position] // parts).reshape([-1 if axis == position else 1 for axis in range(len(shape))])
    return factor_of


def scatter_about(key, extent, scale, bound, shards=(), held_as=jnp.bfloat16):
    gain = block_levels(key, extent, shards, -0.22, 0.18) if shards else 1.0
    entries = jax.random.normal(key, extent, jnp.float32) * scale * gain
    return jnp.minimum(jnp.maximum(entries, -bound), bound).astype(held_as)


def setup_inputs(seed: int = 0) -> dict:
    keys = jax.random.split(jax.random.key(seed), 19)
    return {
        "tokens": scatter_about(keys[0], (TOKENS, D), 1.0, 6.0, ((0, 16),)),
        "embed_table": scatter_about(keys[1], (VOCAB, D), 1.0, 6.0, ((0, 16),)),
        "qkv_weight": scatter_about(keys[2], (D, 3, D), D ** -0.5, 0.21875, ((0, 16), (2, 2))),
        "qv_bias": scatter_about(keys[3], (2, D), 0.5, 3.0, ((1, 2),), jnp.float32),
        "out_weight": scatter_about(keys[4], (D, D), (D // 8) ** -0.5, 0.625, ((0, 2), (1, 16))),
        "out_bias": scatter_about(keys[5], (D,), 0.5, 3.0, (), jnp.float32),
        "norm1_gain": jnp.clip(jax.random.uniform(keys[6], (D,), jnp.float32, 0.5, 1.5), 0.5, 1.5),
        "norm1_bias": scatter_about(keys[7], (D,), 0.5, 3.0, (), jnp.float32),
        "in_weight": scatter_about(keys[8], (D, FF), D ** -0.5, 0.21875, ((0, 16), (1, 2))),
        "in_bias": scatter_about(keys[9], (FF,), 0.5, 3.0, ((0, 2),), jnp.float32),
        "down_weight": scatter_about(keys[10], (FF, D), FF ** -0.5, 0.109375, ((0, 2), (1, 16))),
        "down_bias": scatter_about(keys[11], (D,), 0.5, 3.0, (), jnp.float32),
        "norm2_gain": jnp.clip(jax.random.uniform(keys[12], (D,), jnp.float32, 0.5, 1.5), 0.5, 1.5),
        "norm2_bias": scatter_about(keys[13], (D,), 0.5, 3.0, (), jnp.float32),
        "masked_pos": draw_masked_pos(jax.random.fold_in(keys[18], 71), 0),
        "replace_ids": touch_ends(jax.random.randint(keys[15], (PAGES, CAP), 0, VOCAB), jax.random.fold_in(keys[15], 1), 0, VOCAB - 1).astype(jnp.int32),
        "masked_count": draw_masked_count(jax.random.fold_in(keys[18], 71), 0),
        "cotangent": scatter_about(keys[17], (PAGES, CAP, D), 1.0, 6.0, ((0, 16),)),
    }


EPSILON = 1e-05
HIGHEST = lax.Precision.HIGHEST

@jax.custom_vjp
def low(v):
    return lax.optimization_barrier(v.astype(jnp.bfloat16)).astype(jnp.float32)

@jax.custom_vjp
def low_back(v):
    return v

def low_keep(v):
    return (low(v), None)

def low_pass(kept, grad):
    return (grad,)

def back_keep(v):
    return (v, None)

def back_low(kept, grad):
    return (low(grad),)
low.defvjp(low_keep, low_pass)
low_back.defvjp(back_keep, back_low)

def layer_norm(values, norm_gain, norm_bias):
    row_mean = lax.optimization_barrier(jnp.mean(values, axis=-1, keepdims=True))
    centered = values - row_mean
    variance = lax.optimization_barrier(jnp.mean(centered * centered, axis=-1, keepdims=True))
    return centered * lax.rsqrt(variance + EPSILON) * norm_gain + norm_bias

def layer(inputs, embed_table, qkv_weight, qv_bias, out_weight, out_bias, norm1_gain, norm1_bias, in_weight, in_bias, down_weight, down_bias, norm2_gain, norm2_bias, placed, ids_here, is_valid):
    group = inputs.shape[0]
    repl_rows = jnp.take(embed_table, ids_here, axis=0) * is_valid[:, :, None]
    embedded = inputs + jnp.einsum('gcl,gcd->gld', placed, repl_rows, precision=HIGHEST)
    embedded_low = low(embedded)
    project = jnp.einsum('gld,dke->glke', embedded_low, qkv_weight, precision=HIGHEST)
    query_rows = low(low_back(project[:, :, 0] + qv_bias[0]))
    key_rows = low(low_back(project[:, :, 1]))
    value_rows = low(low_back(project[:, :, 2] + qv_bias[1]))
    split_shape = (group, LEN, HEADS, HEAD)
    query_rows = query_rows.reshape(split_shape)
    key_rows = key_rows.reshape(split_shape)
    value_rows = value_rows.reshape(split_shape)
    score_scale = HEAD ** (-0.5)
    scores = low_back(jnp.einsum('gqhe,gkhe->ghqk', query_rows, key_rows, precision=HIGHEST) * score_scale)
    row_max = lax.optimization_barrier(jnp.max(scores, axis=-1, keepdims=True))
    powers = jnp.exp(scores - row_max)
    attn_prob = low(powers / lax.optimization_barrier(jnp.sum(powers, axis=-1, keepdims=True)))
    attended = jnp.einsum('ghqk,gkhe->gqhe', attn_prob, value_rows, precision=HIGHEST).reshape(group, LEN, D)
    attended = low(low_back(attended))
    attn_out = low_back(jnp.einsum('gle,ed->gld', attended, out_weight, precision=HIGHEST) + out_bias)
    middle = layer_norm(embedded + attn_out, norm1_gain, norm1_bias)
    hidden_in = low_back(jnp.einsum('gld,df->glf', low(middle), in_weight, precision=HIGHEST) + in_bias)
    hidden = low(jax.nn.gelu(hidden_in, approximate=False))
    ffn_out = low_back(jnp.einsum('glf,fd->gld', hidden, down_weight, precision=HIGHEST) + down_bias)
    return layer_norm(middle + ffn_out, norm2_gain, norm2_bias)

def reference(tokens, embed_table, qkv_weight, qv_bias, out_weight, out_bias, norm1_gain, norm1_bias, in_weight, in_bias, down_weight, down_bias, norm2_gain, norm2_bias, masked_pos, replace_ids, masked_count, cotangent):
    params = tuple((item.astype(jnp.float32) for item in (embed_table, qkv_weight, qv_bias, out_weight, out_bias, norm1_gain, norm1_bias, in_weight, in_bias, down_weight, down_bias, norm2_gain, norm2_bias)))
    groups = PAGES // 8
    group_inputs = tokens.astype(jnp.float32).reshape(groups, 8, LEN, D)
    group_pos = masked_pos.reshape(groups, 8, CAP)
    group_ids = replace_ids.reshape(groups, 8, CAP)
    group_count = masked_count.reshape(groups, 8)
    group_cot = cotangent.reshape(groups, 8, CAP, D)

    def group_step(totals, group_data):
        inputs, positions, ids_here, counts, incoming = group_data
        is_valid = (jnp.arange(CAP)[None, :] < counts[:, None]).astype(jnp.float32)
        placed = (positions[:, :, None] == jnp.arange(LEN)[None, None, :]).astype(jnp.float32)
        weighted = incoming.astype(jnp.float32) * is_valid[:, :, None]
        page_index = jnp.arange(8, dtype=jnp.int32)[:, None]
        grad_final = jnp.zeros((8, LEN, D), jnp.float32).at[page_index, positions.astype(jnp.int32)].add(weighted)

        def forward(inputs, *weights):
            return layer(inputs, *weights, placed, ids_here, is_valid)
        final, pull = jax.vjp(forward, inputs, *params)
        grads = pull(grad_final)
        totals = tuple((left + right for left, right in zip(totals, grads[1:])))
        return (totals, (final.astype(jnp.bfloat16), grads[0]))
    start = tuple((jnp.zeros_like(item) for item in params))
    totals, (finals, grad_inputs) = lax.scan(group_step, start, (group_inputs, group_pos, group_ids, group_count, group_cot))
    output = finals.reshape(TOKENS, D)
    grad_input = grad_inputs.reshape(TOKENS, D)
    return (output, grad_input, totals[0], totals[1], totals[2].reshape(2, N_MP, D // N_MP), totals[3], totals[4], totals[5], totals[6], totals[7], totals[8].reshape(N_MP, FF // N_MP), totals[9], totals[10], totals[11], totals[12])
```

```python
import jax
import jax.numpy as jnp
from jax import lax
from jax.sharding import PartitionSpec as P

HEAD = 64
EPSILON = 1e-05
ROOM = 24
EXTRA = 8

BF = jnp.bfloat16
F32 = jnp.float32


def dot(a, b, dims=((1,), (0,)), **kw):
    return lax.dot_general(a, b, (dims, ((), ())), preferred_element_type=F32, **kw)


def nt(a, b):
    return dot(a, b, ((1,), (1,)))


def tn(a, b):
    return dot(a, b, ((0,), (0,)))


def split_two(values):
    high = values.astype(BF)
    return high, (values - high.astype(F32)).astype(BF)


def far_digits(size):
    found = []
    stride, rest = 4, size // 4
    while rest > 1:
        radix = next(r for r in (4, 2, 3, 5, 7, rest) if rest % r == 0)
        found.append((radix, stride))
        stride, rest = stride * radix, rest // radix
    return found


NEAR = ((2, 1), (2, 2))


def shift(size, digit, step):
    radix, stride = digit
    pairs = []
    for src in range(size):
        own = (src // stride) % radix
        pairs.append((src, src + ((own + step) % radix - own) * stride))
    return pairs


def send(values, size, digit, step):
    return lax.ppermute(values, "dp", shift(size, digit, step))


def gather_far(shard, size):
    blocks = [shard]
    rows = shard.shape[0]
    for digit in far_digits(size):
        packed = blocks[0] if len(blocks) == 1 else jnp.concatenate(blocks, axis=0)
        count = len(blocks)
        for step in range(1, digit[0]):
            got = send(packed, size, digit, step)
            blocks = blocks + [got[k * rows : (k + 1) * rows] for k in range(count)]
    return blocks


def gather_near(blocks, size, half):
    order = NEAR if half == 0 else NEAR[::-1]
    packed = jnp.concatenate(blocks, axis=0)
    for digit in order:
        packed = jnp.concatenate([packed, send(packed, size, digit, 1)], axis=0)
    return packed


def held_order(size, rows, me):
    half_rows = rows // 2
    far = far_digits(size)
    place = jnp.arange(size * rows)
    second = place >= size * half_rows
    count = jnp.where(second, rows - half_rows, half_rows)
    within = place - jnp.where(second, size * half_rows, 0)
    slot, row = within // count, within % count + jnp.where(second, half_rows, 0)
    owner = jnp.zeros_like(place)
    for radix, stride in far:
        step = slot % radix
        slot = slot // radix
        owner = owner + ((me // stride - step) % radix) * stride
    low, high = slot % 2, slot // 2
    x_step, y_step = jnp.where(second, high, low), jnp.where(second, low, high)
    owner = owner + (me - x_step) % 2 + ((me // 2 - y_step) % 2) * 2
    return owner * rows + row


def scatter_sum(parts, size):
    far = far_digits(size)
    kept = []
    for half, part in enumerate(parts):
        order = (NEAR if half == 0 else NEAR[::-1])[::-1]
        for digit in order:
            middle = part.shape[0] // 2
            got = send(part[middle:], size, digit, 1)
            part = (part[:middle].astype(F32) + got.astype(F32)).astype(BF)
        kept.append(part)
    count = size // 4
    rows = [part.shape[0] // count for part in kept]
    blocks = [
        jnp.concatenate([part[k * r : (k + 1) * r] for part, r in zip(kept, rows)], axis=0)
        for k in range(count)
    ]
    for digit in far[::-1]:
        radix = digit[0]
        inner = len(blocks) // radix
        groups = [blocks[k * inner : (k + 1) * inner] for k in range(radix)]
        total = [block.astype(F32) for block in groups[0]]
        for step in range(1, radix):
            packed = groups[step][0] if inner == 1 else jnp.concatenate(groups[step], axis=0)
            got = send(packed, size, digit, radix - step).astype(F32)
            high = got.shape[0] // inner
            total = [t + got[k * high : (k + 1) * high] for k, t in enumerate(total)]
        blocks = total if inner == 1 else [t.astype(BF) for t in total]
    return blocks[0].astype(F32)


def norm_stats(values):
    row_mean = jnp.mean(values, axis=-1, keepdims=True)
    centered = values - row_mean
    scale = lax.rsqrt(jnp.mean(centered * centered, axis=-1, keepdims=True) + EPSILON)
    return centered * scale, scale


def norm_back(grad, unit, scale, gain):
    inner = grad * gain
    mean_inner = jnp.mean(inner, axis=-1, keepdims=True)
    mean_unit = jnp.mean(inner * unit, axis=-1, keepdims=True)
    return (
        scale * (inner - mean_inner - unit * mean_unit),
        jnp.sum(grad * unit, axis=0),
        jnp.sum(grad, axis=0),
    )


def gelu(values):
    return values * (0.5 + 0.5 * lax.erf(values * (0.5**0.5)))


def gelu_slope(values):
    bell = jnp.exp(-0.5 * values * values) * (0.5 / jnp.pi) ** 0.5
    return 0.5 + 0.5 * lax.erf(values * (0.5**0.5)) + values * bell


def probabilities(query, key):
    scores = jnp.einsum("gqhe,gkhe->ghqk", query, key, preferred_element_type=F32) * HEAD**-0.5
    powers = jnp.exp(scores - jnp.max(scores, axis=-1, keepdims=True))
    return powers / jnp.sum(powers, axis=-1, keepdims=True)


def attend(query, key, value):
    prob = probabilities(query, key).astype(BF)
    out = jnp.einsum("ghqk,gkhe->gqhe", prob, value, preferred_element_type=F32)
    return out.astype(BF)


def attend_back(query, key, value, grad):
    prob = probabilities(query, key)
    low = prob.astype(BF)
    grad_value = jnp.einsum("ghqk,gqhe->gkhe", low, grad, preferred_element_type=F32)
    grad_prob = jnp.einsum("gqhe,gkhe->ghqk", grad, value, preferred_element_type=F32)
    grad_scores = prob * (grad_prob - jnp.sum(prob * grad_prob, axis=-1, keepdims=True))
    grad_scores = grad_scores.astype(BF)
    grad_query = jnp.einsum("ghqk,gkhe->gqhe", grad_scores, key, preferred_element_type=F32)
    grad_key = jnp.einsum("ghqk,gqhe->gkhe", grad_scores, query, preferred_element_type=F32)
    scale = HEAD**-0.5
    return (
        (grad_query * scale).astype(BF),
        (grad_key * scale).astype(BF),
        grad_value.astype(BF),
    )


def per_device(
    tokens,
    embed_table,
    qkv_weight,
    qv_bias,
    out_weight,
    out_bias,
    norm1_gain,
    norm1_bias,
    in_weight,
    in_bias,
    down_weight,
    down_bias,
    norm2_gain,
    norm2_bias,
    masked_pos,
    replace_ids,
    masked_count,
    cotangent,
):
    size, cores = lax.axis_size("dp"), lax.axis_size("mp")
    me, core = lax.axis_index("dp"), lax.axis_index("mp")
    page_count, slot_count = masked_pos.shape
    length = tokens.shape[0] // page_count
    width = tokens.shape[1]
    shard_rows = width // size
    table_rows = embed_table.shape[0]
    pages = page_count // cores
    rows = pages * length
    slots = pages * slot_count
    head_cols = qkv_weight.shape[2]
    hidden_cols = in_weight.shape[1]

    def to_core(values, step):
        pairs = [(c, (c + step) % cores) for c in range(cores)]
        return lax.ppermute(values, "mp", pairs)

    def from_cores(values):
        return [values] + [to_core(values, k) for k in range(1, cores)]

    def own_pages(values):
        per = values.shape[0] // cores
        return lax.dynamic_slice_in_dim(values, core * per, per, 0)

    pad = -(slot_count + 1) % 128
    packed_ids = jnp.concatenate(
        [replace_ids, masked_count[:, None], jnp.zeros((page_count, pad), jnp.int32)], axis=1
    )
    all_ids = lax.all_to_all(
        jnp.broadcast_to(packed_ids[None], (size, *packed_ids.shape)), "dp", 0, 0
    )
    slot_ids = all_ids[:, :, :slot_count]
    slot_used = jnp.arange(slot_count)[None, None, :] < all_ids[:, :, slot_count : slot_count + 1]
    slot_ids = slot_ids.reshape(size * cores, slots)
    slot_used = slot_used.reshape(size * cores, slots)
    before = (jnp.arange(slots)[:, None] < jnp.arange(slots)[None, :]).astype(BF)
    slot_mine = slot_used & (slot_ids // table_rows == me)
    slot_rank = dot(slot_mine.astype(BF), before).astype(jnp.int32)
    slot_local = slot_ids - me * table_rows
    owners = jnp.arange(size)
    fullest = jnp.max(
        jnp.sum(
            (slot_used[:, :, None] & (slot_ids[:, :, None] // table_rows == owners)).astype(
                jnp.int32
            ),
            axis=1,
        )
    )
    rounds = (fullest + ROOM - 1) // ROOM

    def wanted(turn):
        place = (slot_rank - turn * ROOM)[:, None, :] == jnp.arange(ROOM)[None, :, None]
        place = place & slot_mine[:, None, :]
        asked = jnp.sum(jnp.where(place, slot_local[:, None, :] + 1, 0), axis=2) - 1
        hot = asked[:, :, None] == jnp.arange(table_rows)[None, None, :]
        return hot.astype(BF).reshape(size, cores, ROOM, table_rows)

    pos = own_pages(masked_pos)
    ids = own_pages(replace_ids).reshape(slots)
    used = (jnp.arange(slot_count)[None, :] < own_pages(masked_count)[:, None]).reshape(slots)
    row_of = (pos + jnp.arange(pages)[:, None] * length).reshape(slots)
    slot_owner = ids // table_rows
    to_owner = used[:, None] & (slot_owner[:, None] == owners[None, :])
    owner_rank = tn(before, to_owner.astype(BF)).astype(jnp.int32)

    def sent(turn):
        place = (owner_rank - turn * ROOM)[:, :, None] == jnp.arange(ROOM)[None, None, :]
        place = place & to_owner[:, :, None]
        return place.astype(BF).reshape(slots, size * ROOM)

    first_wanted, first_sent = wanted(0), sent(0)

    def core_wanted(hot, which):
        return lax.dynamic_index_in_dim(hot, which % cores, 1, keepdims=False).reshape(
            size * ROOM, table_rows
        )

    def fetch(hot, sent_hot):
        found = dot(core_wanted(hot, core), embed_table).astype(BF)
        found = lax.all_to_all(found.reshape(size, ROOM, width), "dp", 0, 0)
        return dot(sent_hot, found.reshape(size * ROOM, width))

    new_rows = fetch(first_wanted, first_sent)
    new_rows = lax.fori_loop(
        1, rounds, lambda turn, held: held + fetch(wanted(turn), sent(turn)), new_rows
    ).astype(BF)

    out_turned, down_turned = out_weight.T, down_weight.T

    def gathered(blocks):
        halves = []
        for half in range(2):
            cut = shard_rows // 2
            halves.append([b[:cut] if half == 0 else b[cut:] for b in blocks])
        whole = jnp.concatenate(
            [gather_near(halves[0], size, 0), gather_near(halves[1], size, 1)], axis=0
        )
        return from_cores(whole)

    first = gather_far(qkv_weight.reshape(shard_rows, 3 * head_cols), size)
    second_shard = jnp.concatenate([out_turned, in_weight], axis=1)
    second_shard, *first = lax.optimization_barrier((second_shard, *first))
    second = gather_far(second_shard, size)
    third_shard, *second = lax.optimization_barrier((down_turned, *second))
    third = gather_far(third_shard, size)
    qkv_full = gathered(first)
    out_in_full = gathered(second)
    down_full = gathered(third)
    out_full = [w[:, :head_cols] for w in out_in_full]
    in_full = [w[:, head_cols:] for w in out_in_full]
    biases = from_cores(jnp.concatenate([qv_bias.reshape(-1), in_bias]))
    query_bias = jnp.concatenate([b[:head_cols] for b in biases])
    value_bias = jnp.concatenate([b[head_cols : 2 * head_cols] for b in biases])
    hidden_bias = jnp.concatenate([b[2 * head_cols :] for b in biases])

    order = held_order(size, shard_rows, me)
    turn_in = (jnp.arange(width)[:, None] == order[None, :]).astype(BF)
    vectors = jnp.stack([out_bias, norm1_gain, norm1_bias, down_bias, norm2_gain, norm2_bias])
    vectors = dot(vectors, turn_in.astype(F32), precision=lax.Precision.HIGHEST)
    out_bias, norm1_gain, norm1_bias, down_bias, norm2_gain, norm2_bias = vectors

    placed = (row_of[None, :] == jnp.arange(rows)[:, None]).astype(BF)
    embedded = dot(own_pages(tokens), turn_in) + dot(placed, dot(new_rows, turn_in).astype(BF))
    embedded_low = embedded.astype(BF)
    slot_embedded = jnp.take(embedded, row_of, axis=0)
    slot_low = slot_embedded.astype(BF)

    def cat(parts):
        return jnp.concatenate(parts, axis=1)

    def heads(values):
        return values.reshape(pages, -1, values.shape[1] // HEAD, HEAD)

    key = cat([dot(embedded_low, w[:, head_cols : 2 * head_cols]) for w in qkv_full]).astype(BF)
    value = cat([dot(embedded_low, w[:, 2 * head_cols :]) for w in qkv_full]) + value_bias
    value = value.astype(BF)
    key, value = heads(key), heads(value)

    def front(low, exact):
        query = cat([dot(low, w[:, :head_cols]) for w in qkv_full]) + query_bias
        query = heads(query.astype(BF))
        attended = attend(query, key, value).reshape(low.shape[0], -1)
        parts = [attended[:, k * head_cols : (k + 1) * head_cols] for k in range(cores)]
        attn_out = sum(nt(p, w) for p, w in zip(parts, out_full)) + out_bias
        unit1, scale1 = norm_stats(exact + attn_out)
        middle = unit1 * norm1_gain + norm1_bias
        middle_low = middle.astype(BF)
        hidden_in = [dot(middle_low, w) for w in in_full]
        hidden_in = [
            h + hidden_bias[k * hidden_cols : (k + 1) * hidden_cols]
            for k, h in enumerate(hidden_in)
        ]
        hidden = [gelu(h).astype(BF) for h in hidden_in]
        ffn_out = sum(nt(h, w) for h, w in zip(hidden, down_full)) + down_bias
        unit2, scale2 = norm_stats(middle + ffn_out)
        return query, parts, unit1, scale1, middle_low, hidden_in, hidden, unit2, scale2

    query, attended, unit1, scale1, middle_low, hidden_in, hidden, unit2, scale2 = front(
        slot_low, slot_embedded
    )

    def summed(grads):
        total = grads[0].astype(BF).astype(F32)
        for k in range(1, cores):
            total = total + to_core(grads[k].astype(BF), cores - k).astype(F32)
        total = total.astype(BF)
        cut = size * (shard_rows // 2)
        return scatter_sum([total[:cut], total[cut:]], size)

    incoming = jnp.where(used[:, None], own_pages(cotangent).reshape(slots, width), 0.0)
    grad_final = dot(incoming.astype(BF), turn_in)
    grad_r2, grad_gain2, grad_bias2 = norm_back(grad_final, unit2, scale2, norm2_gain)
    grad_ffn = grad_r2.astype(BF)
    grad_down_bias = jnp.sum(grad_ffn.astype(F32), axis=0)
    down_share = summed([tn(grad_ffn, h) for h in hidden])
    grad_hidden_in = [
        (dot(grad_ffn, w) * gelu_slope(h)).astype(BF) for w, h in zip(down_full, hidden_in)
    ]
    grad_in_bias = [jnp.sum(g.astype(F32), axis=0) for g in grad_hidden_in]
    in_share = summed([tn(middle_low, g) for g in grad_hidden_in])
    grad_middle = sum(nt(g, w) for g, w in zip(grad_hidden_in, in_full)) + grad_r2
    grad_r1, grad_gain1, grad_bias1 = norm_back(grad_middle, unit1, scale1, norm1_gain)
    grad_attn = grad_r1.astype(BF)
    grad_out_bias = jnp.sum(grad_attn.astype(F32), axis=0)
    out_share = summed([tn(grad_attn, a) for a in attended])
    grad_attended = heads(cat([dot(grad_attn, w) for w in out_full]).astype(BF))
    grad_query, grad_key, grad_value = attend_back(query, key, value, grad_attended)
    grad_query = grad_query.reshape(slots, -1)
    grad_key = grad_key.reshape(rows, -1)
    grad_value = grad_value.reshape(rows, -1)

    def part(values, k):
        return values[:, k * head_cols : (k + 1) * head_cols]

    qkv_share = summed(
        [
            cat(
                [
                    tn(slot_low, part(grad_query, k)),
                    tn(embedded_low, part(grad_key, k)),
                    tn(embedded_low, part(grad_value, k)),
                ]
            )
            for k in range(cores)
        ]
    )
    grad_query_bias = jnp.sum(grad_query.astype(F32), axis=0)
    grad_value_bias = jnp.sum(grad_value.astype(F32), axis=0)

    at_slots = grad_r1
    everywhere = 0.0
    for k, w in enumerate(qkv_full):
        at_slots = at_slots + nt(part(grad_query, k), w[:, :head_cols])
        everywhere = everywhere + nt(part(grad_key, k), w[:, head_cols : 2 * head_cols])
        everywhere = everywhere + nt(part(grad_value, k), w[:, 2 * head_cols :])
    slot_high, slot_rest = split_two(at_slots)
    everywhere = everywhere + dot(placed, slot_high) + dot(placed, slot_rest)
    high, rest = split_two(everywhere)
    grad_rows = nt(high, turn_in) + nt(rest, turn_in)

    slot_grad = jnp.take(grad_rows, row_of, axis=0).astype(BF)
    small = jnp.stack(
        [grad_out_bias, grad_gain1, grad_bias1, grad_down_bias, grad_gain2, grad_bias2]
    )
    small = dot(small, turn_in.T.astype(F32), precision=lax.Precision.HIGHEST)
    per_owner = [v.reshape(size, shard_rows) for v in small]
    for k in range(cores):
        per_owner.append(part(grad_query_bias[None], k).reshape(size, -1))
        per_owner.append(part(grad_value_bias[None], k).reshape(size, -1))
        per_owner.append(grad_in_bias[k].reshape(size, -1))
    lengths = [v.shape[1] for v in per_owner]
    small = cat(per_owner)
    small_rows = -(-small.shape[1] // width)
    small = jnp.pad(small, ((0, 0), (0, small_rows * width - small.shape[1])))
    small = small.reshape(size, small_rows, width)
    small_high, small_rest = split_two(small)
    spare = jnp.zeros((size, EXTRA - 2 * small_rows, width), BF)

    def give(hot, sent_hot, tail):
        moved = tn(sent_hot, slot_grad).astype(BF).reshape(size, ROOM, width)
        if tail is not None:
            moved = jnp.concatenate([moved, *tail], axis=1)
        got = from_cores(lax.all_to_all(moved, "dp", 0, 0))
        table = 0.0
        for k, block in enumerate(got):
            table = table + tn(
                core_wanted(hot, core + cores - k),
                block[:, :ROOM].reshape(size * ROOM, width),
            )
        return table, got

    grad_table, got = give(first_wanted, first_sent, (small_high, small_rest, spare))
    grad_table = lax.fori_loop(
        1,
        rounds,
        lambda turn, held: held + give(wanted(turn), sent(turn), None)[0],
        grad_table,
    )
    totals = [
        jnp.sum(block[:, ROOM : ROOM + 2 * small_rows].astype(F32), axis=0) for block in got
    ]
    totals = [(t[:small_rows] + t[small_rows:]).reshape(-1) for t in totals]
    starts = [sum(lengths[:k]) for k in range(len(lengths))]

    def piece(k, index):
        return totals[k][starts[index] : starts[index] + lengths[index]]

    vec = [sum(piece(k, index) for k in range(cores)) for index in range(6)]
    own = [sum(piece(k, 6 + 3 * k + j) for k in range(cores)) for j in range(3)]

    *_, full_unit2, _ = front(embedded_low, embedded)
    final = (full_unit2 * norm2_gain + norm2_bias).astype(BF)
    final = nt(final, turn_in).astype(BF)

    def all_pages(values):
        whole = jnp.zeros((cores * values.shape[0], values.shape[1]), values.dtype)
        for k, block in enumerate(from_cores(values)):
            whole = lax.dynamic_update_slice_in_dim(
                whole, block, ((core + cores - k) % cores) * values.shape[0], 0
            )
        return whole

    return (
        all_pages(final),
        all_pages(grad_rows),
        grad_table,
        qkv_share.reshape(shard_rows, 3, head_cols),
        jnp.stack([own[0], own[1]])[:, None, :],
        out_share.T,
        vec[0],
        vec[1],
        vec[2],
        in_share,
        own[2][None],
        down_share.T,
        vec[3],
        vec[4],
        vec[5],
    )


def solution(mesh):
    in_specs = (
        P("dp", None),
        P("dp", None),
        P("dp", None, "mp"),
        P(None, "mp"),
        P("mp", "dp"),
        P(),
        P(),
        P(),
        P("dp", "mp"),
        P("mp"),
        P("mp", "dp"),
        P(),
        P(),
        P(),
        P("dp", None),
        P("dp", None),
        P("dp"),
        P("dp", None, None),
    )
    out_specs = (
        P("dp", None),
        P("dp", None),
        P("dp", None),
        P("dp", None, "mp"),
        P(None, "mp", "dp"),
        P("mp", "dp"),
        P("dp"),
        P("dp"),
        P("dp"),
        P("dp", "mp"),
        P("mp", "dp"),
        P("mp", "dp"),
        P("dp"),
        P("dp"),
        P("dp"),
    )
    return jax.shard_map(
        per_device, mesh=mesh, in_specs=in_specs, out_specs=out_specs, check_vma=False
    )
```

```python
import jax
import jax.numpy as jnp
import numpy as np
from jax import lax
from jax.experimental import pallas as pl
from jax.experimental.pallas import tpu as pltpu
from jax.sharding import PartitionSpec as P

HEAD = 64
EPSILON = 1e-05
ROOM = 24
EXTRA = 8

BF = jnp.bfloat16
F32 = jnp.float32


def dot(a, b, dims=((1,), (0,)), **kw):
    return lax.dot_general(a, b, (dims, ((), ())), preferred_element_type=F32, **kw)


def nt(a, b):
    return dot(a, b, ((1,), (1,)))


def tn(a, b):
    return dot(a, b, ((0,), (0,)))


def split_two(values):
    high = values.astype(BF)
    return high, (values - high.astype(F32)).astype(BF)


def far_digits(size):
    found = []
    stride, rest = 4, size // 4
    while rest > 1:
        radix = next(r for r in (4, 2, 3, 5, 7, rest) if rest % r == 0)
        found.append((radix, stride))
        stride, rest = stride * radix, rest // radix
    return found


NEAR = ((2, 1), (2, 2))


def shift(size, digit, step):
    radix, stride = digit
    pairs = []
    for src in range(size):
        own = (src // stride) % radix
        pairs.append((src, src + ((own + step) % radix - own) * stride))
    return pairs


def send(values, size, digit, step):
    return lax.ppermute(values, "dp", shift(size, digit, step))


def held_order(size, rows, me):
    half_rows = rows // 2
    far = far_digits(size)
    place = jnp.arange(size * rows)
    second = place >= size * half_rows
    count = jnp.where(second, rows - half_rows, half_rows)
    within = place - jnp.where(second, size * half_rows, 0)
    slot, row = within // count, within % count + jnp.where(second, half_rows, 0)
    owner = jnp.zeros_like(place)
    for radix, stride in far:
        step = slot % radix
        slot = slot // radix
        owner = owner + ((me // stride - step) % radix) * stride
    low, high = slot % 2, slot // 2
    x_step, y_step = jnp.where(second, high, low), jnp.where(second, low, high)
    owner = owner + (me - x_step) % 2 + ((me // 2 - y_step) % 2) * 2
    return owner * rows + row


VMEM_LIMIT = 56 * 1024 * 1024


def kernel_call(body, outs, inputs, far_count=0, scratch=(), flops=0, grid=None, specs=None):
    near = len(inputs) - far_count
    in_specs, out_specs = specs or (
        [pl.BlockSpec(memory_space=pltpu.VMEM)] * near,
        [pl.BlockSpec(memory_space=pltpu.VMEM)] * len(outs),
    )
    return pl.pallas_call(
        body,
        grid=grid or (),
        out_shape=outs,
        in_specs=[*in_specs, *([pl.BlockSpec(memory_space=pl.ANY)] * far_count)],
        out_specs=out_specs,
        scratch_shapes=scratch,
        compiler_params=pltpu.CompilerParams(vmem_limit_bytes=VMEM_LIMIT),
        cost_estimate=pl.CostEstimate(flops=1, bytes_accessed=1, transcendentals=0),
    )(*inputs)


def shape(rows, cols, dtype):
    return jax.ShapeDtypeStruct((rows, cols), dtype)


def fill(pieces, held, sems, start=0):
    copies, at = [], 0
    for i, piece in enumerate(pieces):
        rows = piece.shape[0]
        source = piece.at[:, pl.ds(start, held.shape[1])]
        copy = pltpu.make_async_copy(source, held.at[pl.ds(at, rows)], sems.at[i])
        copy.start()
        copies.append(copy)
        at += rows

    def wait():
        for copy in copies:
            copy.wait()

    return wait


def held_scratch(pieces, cols=None):
    rows = sum(p.shape[0] for p in pieces)
    return [
        pltpu.VMEM((rows, cols or pieces[0].shape[1]), BF),
        pltpu.SemaphoreType.DMA((len(pieces),)),
    ]


def norm_stats(values):
    row_mean = jnp.mean(values, axis=-1, keepdims=True)
    centered = values - row_mean
    scale = lax.rsqrt(jnp.mean(centered * centered, axis=-1, keepdims=True) + EPSILON)
    return centered * scale, scale


def norm_back(grad, unit, scale, gain):
    inner = grad * gain
    mean_inner = jnp.mean(inner, axis=-1, keepdims=True)
    mean_unit = jnp.mean(inner * unit, axis=-1, keepdims=True)
    return (
        scale * (inner - mean_inner - unit * mean_unit),
        jnp.sum(grad * unit, axis=0, keepdims=True),
        jnp.sum(grad, axis=0, keepdims=True),
    )


def gelu(values):
    return values * (0.5 + 0.5 * lax.erf(values * (0.5**0.5)))


def gelu_both(values):
    normal = 0.5 + 0.5 * lax.erf(values * (0.5**0.5))
    bell = jnp.exp(-0.5 * values * values) * (0.5 / np.pi) ** 0.5
    return values * normal, normal + values * bell


def head_masks(dtype):
    lane = lax.broadcasted_iota(jnp.int32, (1, 2 * HEAD), 1)
    return [(lane // HEAD == h).astype(dtype) for h in range(2)]


def attend_pair(query, key, value):
    outs = []
    for mask in head_masks(BF):
        scores = nt(query * mask, key)
        powers = jnp.exp(scores - jnp.max(scores, axis=-1, keepdims=True))
        prob = powers * (1.0 / jnp.sum(powers, axis=-1, keepdims=True))
        outs.append(dot(prob.astype(BF), value))
    first, second = head_masks(F32)
    return (outs[0] * first + outs[1] * second).astype(BF)


def one_hot_rows(row_of_line, rows):
    at = lax.broadcasted_iota(jnp.int32, (rows, row_of_line.shape[1]), 0)
    return (at == row_of_line).astype(F32).astype(BF)


def one_hot_slots(row_of_column, rows):
    at = lax.broadcasted_iota(jnp.int32, (row_of_column.shape[0], rows), 1)
    return (at == row_of_column).astype(F32).astype(BF)


def as_column(line):
    count = line.shape[1]
    square = (count, count)
    same = lax.broadcasted_iota(jnp.int32, square, 0) == lax.broadcasted_iota(jnp.int32, square, 1)
    return jnp.sum(jnp.where(same, line.astype(F32), 0.0), axis=1, keepdims=True)


def floor_by(values, divisor):
    return jnp.floor((values + 0.5) * (1.0 / divisor))


def iota(dims, axis):
    return lax.broadcasted_iota(jnp.int32, dims, axis).astype(F32)


def serve(places, codes, table, size, cores):
    table_rows, width = table.shape
    devices, slots = codes.shape
    count = size * ROOM

    def body(place, code, tab, *outs):
        *hots, found, most = outs
        me, core = place[0], place[1]
        line = code[...].astype(F32)
        local = line - (me * table_rows).astype(F32)
        mine = (local >= 0) & (local < table_rows)
        before = (iota((slots, slots), 0) < iota((slots, slots), 1)).astype(BF)
        rank = dot(mine.astype(F32).astype(BF), before)
        rank = jnp.where(mine & (rank < ROOM), rank, 255.0).astype(BF)
        local = jnp.where(mine, local, 0.0)
        local_high = floor_by(local, 256)
        local_low = (local - 256 * local_high).astype(BF)
        local_high = local_high.astype(BF)
        source = floor_by(iota((count, 1), 0), ROOM)
        room = iota((count, 1), 0) - ROOM * source
        for k in range(cores):
            which = lax.rem(core + cores - k, cores).astype(F32)
            pick = (iota((count, devices), 1) == source * cores + which).astype(F32).astype(BF)
            hit = dot(pick, rank) == room
            at = 256 * dot(pick, local_high) + dot(pick, local_low) + 1.0
            asked = jnp.sum(jnp.where(hit, at, 0.0), axis=1, keepdims=True) - 1.0
            hots[k][...] = (iota((count, table_rows), 1) == asked).astype(F32).astype(BF)
        found[...] = dot(hots[0][...], tab[...]).astype(BF)
        owner = floor_by(line, table_rows)
        fullest = jnp.zeros((devices, 1), F32)
        for o in range(size):
            here = jnp.sum(jnp.where(owner == o, 1.0, 0.0), axis=1, keepdims=True)
            fullest = jnp.maximum(fullest, here)
        fullest = jnp.max(fullest, axis=0, keepdims=True)
        most[...] = jnp.broadcast_to(fullest, most.shape).astype(jnp.int32)

    smem, vmem = pl.BlockSpec(memory_space=pltpu.SMEM), pl.BlockSpec(memory_space=pltpu.VMEM)
    return kernel_call(
        body,
        [
            *[shape(count, table_rows, BF)] * cores,
            shape(count, width, BF),
            shape(8, 128, jnp.int32),
        ],
        [places, codes, table],
        flops=2 * count * table_rows * width,
        specs=([smem, vmem, vmem], [vmem] * (cores + 2)),
    )


def by_owner(values, owner, place, size):
    count = values.shape[1]
    hit = (iota((size, count), 0) == owner).astype(F32)
    rows = jnp.concatenate([hit * values[r : r + 1] for r in range(values.shape[0])], axis=0)
    hot = (iota((128, count), 0) == place).astype(F32).astype(BF)
    total, rest = 0.0, rows
    for _ in range(3):
        high = rest.astype(BF)
        rest = rest - high.astype(F32)
        total = total + nt(high, hot)
    return total


def prepare(tokens, order, codes, size, table_rows):
    rows, width = tokens.shape
    slots = codes.shape[1]

    def body(tok, order_, code, turn, tok_out, sent):
        turn[...] = (
            (lax.broadcasted_iota(jnp.int32, (width, width), 0) == order_[...])
            .astype(F32)
            .astype(BF)
        )
        line = code[...].astype(F32)
        column = as_column(line)
        owner_line, owner = floor_by(line, table_rows), floor_by(column, table_rows)
        square = (slots, slots)
        earlier = (iota(square, 1) < iota(square, 0)) & (owner_line == owner)
        rank = jnp.sum(jnp.where(earlier, 1.0, 0.0), axis=1, keepdims=True)
        target = jnp.where((column >= 0) & (rank < ROOM), owner * ROOM + rank, -1.0)
        sent[...] = (iota((slots, size * ROOM), 1) == target).astype(F32).astype(BF)
        tok_out[...] = dot(tok[...], turn[...]).astype(BF)

    return kernel_call(
        body,
        [shape(width, width, BF), shape(rows, width, BF), shape(slots, size * ROOM, BF)],
        [tokens, order, codes],
    )


def turn_small(cotangent, codes, vectors, turn):
    slots, width = cotangent.shape

    def body(cot, code, vec, turn_, cot_out, vec_out):
        used = (as_column(code[...].astype(F32)) >= 0).astype(F32).astype(BF)
        cot_out[...] = dot(cot[...] * used, turn_[...]).astype(BF)
        rest, total = vec[...], 0.0
        for _ in range(3):
            high = rest.astype(BF)
            rest = rest - high.astype(F32)
            total = total + dot(high, turn_[...])
        vec_out[...] = total

    return kernel_call(
        body,
        [shape(slots, width, BF), shape(vectors.shape[0], width, F32)],
        [cotangent, codes, vectors, turn],
    )


def enter(tokens, new_rows, turn, line, column, bias, pieces, pages):
    rows, width = tokens.shape
    slots = new_rows.shape[0]
    cols = pieces[0].shape[1] // 3
    length, per = rows // pages, slots // pages

    def body(*refs):
        tok, found, turn_, line_, column_, bias_ = refs[:6]
        piece_refs = refs[6 : 6 + len(pieces)]
        emb, low, q, k, v, s_emb, s_low, s_q, s_att, held, sems = refs[6 + len(pieces) :]
        wait = fill(piece_refs, held, sems)
        new = dot(found[...].astype(BF), turn_[...]).astype(BF)
        hots = []
        for g in range(pages):
            page, here = slice(g * length, (g + 1) * length), slice(g * per, (g + 1) * per)
            placed = one_hot_rows(line_[:, here] - g * length, length)
            hot = one_hot_slots(column_[here] - g * length, length)
            hots.append(hot)
            exact = tok[page].astype(F32) + dot(placed, new[here])
            emb[page] = exact
            low[page] = exact.astype(BF)
            s_emb[here] = dot(hot, tok[page]) + new[here].astype(F32)
        s_low[...] = s_emb[...].astype(BF)
        wait()
        for g in range(pages):
            page, here = slice(g * length, (g + 1) * length), slice(g * per, (g + 1) * per)
            q[page] = (dot(low[page], held[:, :cols]) + bias_[:, :cols]).astype(BF)
            k[page] = dot(low[page], held[:, cols : 2 * cols]).astype(BF)
            v[page] = (dot(low[page], held[:, 2 * cols :]) + bias_[:, cols : 2 * cols]).astype(BF)
            s_q[here] = dot(hots[g], q[page]).astype(BF)
            for j in range(0, cols, 2 * HEAD):
                at = slice(j, j + 2 * HEAD)
                s_att[here, at] = attend_pair(s_q[here, at] * HEAD**-0.5, k[page, at], v[page, at])

    outs = [
        shape(rows, width, F32),
        shape(rows, width, BF),
        *[shape(rows, cols, BF)] * 3,
        shape(slots, width, F32),
        shape(slots, width, BF),
        *[shape(slots, cols, BF)] * 2,
    ]
    return kernel_call(
        body,
        outs,
        [tokens, new_rows, turn, line, column, bias, *pieces],
        len(pieces),
        held_scratch(pieces),
    )


def attend_all(query, key, value, pages):
    rows, cols = query.shape
    length = rows // pages

    def body(q, k, v, out):
        half = length // 2
        for part in range(2):
            here = slice(part * half, (part + 1) * half)
            out[here] = attend_pair(q[here] * HEAD**-0.5, k[...], v[...])

    spec = pl.BlockSpec((length, 2 * HEAD), lambda g, j: (g, j))
    return kernel_call(
        body,
        [shape(rows, cols, BF)],
        [query, key, value],
        grid=(pages, cols // (2 * HEAD)),
        specs=([spec] * 3, [spec]),
    )[0]


def out_part(attended, pieces, dtype):
    rows, cols = attended.shape
    width = sum(p.shape[0] for p in pieces)

    def body(att, *refs):
        out, held, sems = refs[len(pieces) :]
        fill(refs[: len(pieces)], held, sems)()
        out[...] = nt(att[...], held[...]).astype(dtype)

    return kernel_call(
        body,
        [shape(rows, width, dtype)],
        [attended, *pieces],
        len(pieces),
        held_scratch(pieces, cols),
    )[0]


def slot_forward(parts, embedded, vectors, bias, out_in, down):
    slots, width = embedded.shape
    wide = down[0].shape[1]
    skip = out_in[0].shape[1] - wide
    count = len(out_in)

    def body(first, second, emb, vec, bias_, *refs):
        unit1, scale1, mid_low, hid, slope, part, held, sems, held2, sems2 = refs[2 * count :]
        wait = fill(refs[:count], held, sems, skip)
        wait2 = fill(refs[count : 2 * count], held2, sems2)
        unit, scale = norm_stats(emb[...] + vec[0:1] + (first[...] + second[...]))
        unit1[...] = unit
        scale1[...] = jnp.broadcast_to(scale, scale1.shape)
        mid_low[...] = (unit * vec[1:2] + vec[2:3]).astype(BF)
        wait()
        value, rate = gelu_both(dot(mid_low[...], held[...]) + bias_[:, 2 * skip :])
        hid[...] = value.astype(BF)
        slope[...] = rate
        wait2()
        part[...] = nt(hid[...], held2[...])

    outs = [
        shape(slots, width, F32),
        shape(slots, 128, F32),
        shape(slots, width, BF),
        shape(slots, wide, BF),
        shape(slots, wide, F32),
        shape(slots, width, F32),
    ]
    return kernel_call(
        body,
        outs,
        [*parts, embedded, vectors, bias, *out_in, *down],
        2 * count,
        [*held_scratch(out_in, wide), *held_scratch(down)],
    )


def put_rows(outs, start, values):
    at = 0
    for out in outs:
        rows = out.shape[0]
        out[:, start : start + values.shape[1]] = values[at : at + rows].astype(BF)
        at += rows


def slot_turn(parts, hidden, slope, unit1, grad_final, vectors, out_in, down):
    slots, width = unit1.shape
    wide = hidden.shape[1]
    skip = out_in[0].shape[1] - wide
    count = len(down)

    def body(first, second, hid, slp, un1, final, vec, *refs):
        (*grads, grad2, ghin, small, in_small, mid, held, sems, held2, sems2) = refs[2 * count :]
        wait = fill(refs[:count], held, sems, skip)
        wait2 = fill(refs[count : 2 * count], held2, sems2)
        total = un1[...] * vec[1:2] + vec[2:3] + vec[3:4] + (first[...] + second[...])
        unit, scale = norm_stats(total)
        grad, gain, bias = norm_back(final[...].astype(F32), unit, scale, vec[4:5])
        grad2[...] = grad
        grad_low = grad.astype(BF)
        small[0:1] = jnp.sum(grad_low.astype(F32), axis=0, keepdims=True)
        small[1:2] = gain
        small[2:3] = bias
        small[3:8] = jnp.zeros((5, width), F32)
        wait2()
        back = (dot(grad_low, held2[...]) * slp[...]).astype(BF)
        ghin[...] = back
        in_small[...] = jnp.sum(back.astype(F32), axis=0, keepdims=True)
        wait()
        mid[...] = nt(back, held[...])
        put_rows(grads, 0, tn(grad_low, hid[...]))

    outs = [
        *[shape(p.shape[0], wide, BF) for p in down],
        shape(slots, width, F32),
        shape(slots, wide, BF),
        shape(8, width, F32),
        shape(1, wide, F32),
        shape(slots, width, F32),
    ]
    return kernel_call(
        body,
        outs,
        [*parts, hidden, slope, unit1, grad_final, vectors, *out_in, *down],
        2 * count,
        [*held_scratch(out_in, wide), *held_scratch(down)],
    )


def in_grad(mid_low, ghin, heights):
    def body(mid, gh, *grads):
        put_rows(grads, 0, tn(mid[...], gh[...]))

    return kernel_call(body, [shape(r, ghin.shape[1], BF) for r in heights], [mid_low, ghin])


def slot_back(parts, grad2, unit1, scale1, attended, s_query, key, value, s_low, low, vectors, pieces, pages):
    slots, width = unit1.shape
    rows, cols = key.shape
    length, per = rows // pages, slots // pages
    scale = HEAD**-0.5

    def body(first, second, g2, un1, sc1, att, sq, k, v, sl, lo, vec, *refs):
        (*grads, grad1, gq, gk, gv, small, small_heads, held, sems) = refs[len(pieces) :]
        wait = fill(refs[: len(pieces)], held, sems)
        total = g2[...] + (first[...] + second[...])
        grad, gain, bias = norm_back(total, un1[...], sc1[:, :1], vec[1:2])
        grad1[...] = grad
        grad_low = grad.astype(BF)
        small[0:1] = jnp.sum(grad_low.astype(F32), axis=0, keepdims=True)
        small[1:2] = gain
        small[2:3] = bias
        small[3:8] = jnp.zeros((5, width), F32)
        put_rows(grads, 3 * cols, tn(grad_low, att[...]))
        wait()
        gatt = dot(grad_low, held[...]).astype(BF)
        masks = head_masks(BF)
        left_lanes, right_lanes = head_masks(F32)
        for g in range(pages):
            here, page = slice(g * per, (g + 1) * per), slice(g * length, (g + 1) * length)
            for j in range(0, cols, 2 * HEAD):
                at = slice(j, j + 2 * HEAD)
                query, back = sq[here, at], gatt[here, at]
                keys, values = k[page, at], v[page, at]
                got = []
                for mask in masks:
                    scores = nt(query * mask * scale, keys)
                    powers = jnp.exp(scores - jnp.max(scores, axis=-1, keepdims=True))
                    prob = powers * (1.0 / jnp.sum(powers, axis=-1, keepdims=True))
                    grad_prob = nt(back * mask, values)
                    inner = jnp.sum(prob * grad_prob, axis=-1, keepdims=True)
                    grad_scores = (prob * (grad_prob - inner)).astype(BF)
                    got.append(
                        (
                            dot(grad_scores, keys),
                            tn(grad_scores, query),
                            tn(prob.astype(BF), back),
                        )
                    )
                left, right = got
                gq[here, at] = ((left[0] * left_lanes + right[0] * right_lanes) * scale).astype(BF)
                gk[page, at] = ((left[1] * left_lanes + right[1] * right_lanes) * scale).astype(BF)
                gv[page, at] = (left[2] * left_lanes + right[2] * right_lanes).astype(BF)
        small_heads[0:1] = jnp.sum(gq[...].astype(F32), axis=0, keepdims=True)
        small_heads[1:2] = jnp.sum(gv[...].astype(F32), axis=0, keepdims=True)
        small_heads[2:8] = jnp.zeros((6, cols), F32)
        put_rows(grads, 0, tn(sl[...], gq[...]))
        put_rows(grads, cols, tn(lo[...], gk[...]))
        put_rows(grads, 2 * cols, tn(lo[...], gv[...]))

    outs = [
        *[shape(p.shape[0], 4 * cols, BF) for p in pieces],
        shape(slots, width, F32),
        shape(slots, cols, BF),
        *[shape(rows, cols, BF)] * 2,
        shape(8, width, F32),
        shape(8, cols, F32),
    ]
    return kernel_call(
        body,
        outs,
        [*parts, grad2, unit1, scale1, attended, s_query, key, value, s_low, low, vectors, *pieces],
        len(pieces),
        held_scratch(pieces, cols),
    )


def leave_part(gq, gk, gv, line, pieces, pages):
    slots, cols = gq.shape
    rows = gk.shape[0]
    width = sum(p.shape[0] for p in pieces)
    length, per = rows // pages, slots // pages

    def body(q, k, v, line_, *refs):
        out, held, sems = refs[len(pieces) :]
        fill(refs[: len(pieces)], held, sems)()
        high, low = split_two(nt(q[...], held[:, :cols]))
        for g in range(pages):
            page, here = slice(g * length, (g + 1) * length), slice(g * per, (g + 1) * per)
            placed = one_hot_rows(line_[:, here] - g * length, length)
            total = nt(k[page], held[:, cols : 2 * cols]) + nt(v[page], held[:, 2 * cols :])
            total = total + dot(placed, high[here]) + dot(placed, low[here])
            out[page] = total.astype(BF)

    return kernel_call(
        body,
        [shape(rows, width, BF)],
        [gq, gk, gv, line, *pieces],
        len(pieces),
        held_scratch(pieces),
    )[0]


def leave(parts, grad1, line, own_column, turn, order, sent_hot, smalls, size, pages):
    rows, width = parts[0].shape
    slots = grad1.shape[0]
    length, per = rows // pages, slots // pages
    cols, wide = smalls[2].shape[1], smalls[3].shape[1]

    def body(first, second, g1, line_, column_, turn_, order_, hot, sm1, sm2, smq, smh, out, moved):
        high, low = split_two(g1[...])
        for g in range(pages):
            page, here = slice(g * length, (g + 1) * length), slice(g * per, (g + 1) * per)
            placed = one_hot_rows(line_[:, here] - g * length, length)
            total = first[page].astype(F32) + second[page].astype(F32)
            total = total + dot(placed, high[here]) + dot(placed, low[here])
            near, rest = split_two(total)
            out[page] = nt(near, turn_[...]) + nt(rest, turn_[...])

        place = order_[...].astype(F32)
        owner = floor_by(place, width // size)
        vec = jnp.concatenate([sm1[0:3], sm2[0:3]], axis=0)
        vec = by_owner(vec, owner, place - owner * (width // size), size)
        vec = jnp.concatenate([vec[r * size : (r + 1) * size] for r in range(6)], axis=1)
        at = iota((1, cols), 1)
        owner = floor_by(at, cols // size)
        head = by_owner(smq[0:2], owner, at - owner * (cols // size), size)
        at = iota((1, wide), 1)
        owner = floor_by(at, wide // size)
        unit = by_owner(smh[...], owner, at - owner * (wide // size), size)
        own = jnp.concatenate([head[:size], head[size:], unit], axis=1)
        own = jnp.concatenate([own, jnp.zeros((size, width - own.shape[1]), F32)], axis=1)
        tails = [p.astype(F32) for values in (vec, own) for p in split_two(values)]
        slot_hot = one_hot_slots(column_[...], rows)
        going = tn(hot[...], dot(slot_hot, out[...].astype(BF)).astype(BF))
        for s in range(size):
            moved[s, :ROOM] = going[s * ROOM : (s + 1) * ROOM].astype(BF)
            tail = [t[s : s + 1] for t in tails] + [jnp.zeros((EXTRA - len(tails), width), F32)]
            moved[s, ROOM:] = jnp.concatenate(tail, axis=0).astype(BF)

    return kernel_call(
        body,
        [shape(rows, width, F32), jax.ShapeDtypeStruct((size, ROOM + EXTRA, width), BF)],
        [*parts, grad1, line, own_column, turn, order, sent_hot, *smalls],
    )


def collect(hots, gots):
    cores, (count, table_rows) = len(hots), hots[0].shape
    size, held, width = gots[0].shape

    def body(*refs):
        hot, got = refs[:cores], refs[cores : 2 * cores]
        table, sums = refs[2 * cores :]
        value = 0.0
        for k in range(cores):
            rows = jnp.concatenate([got[k][s, :ROOM] for s in range(size)], axis=0)
            value = value + tn(hot[k][...], rows)
        table[...] = value
        tail = jnp.zeros((held - ROOM, width), F32)
        for s in range(size):
            tail = tail + got[0][s, ROOM:].astype(F32)
        sums[...] = jnp.concatenate(
            [tail[0:1] + tail[1:2], tail[2:3] + tail[3:4], jnp.zeros((6, width), F32)], axis=0
        )

    return kernel_call(
        body,
        [shape(table_rows, width, F32), shape(8, width, F32)],
        [*hots, *gots],
    )


def rows_forward(parts, embedded, vectors, bias, out_in, down):
    rows, width = embedded.shape
    wide = down[0].shape[1]
    skip = out_in[0].shape[1] - wide
    block = 256 if rows % 256 == 0 else rows
    count = len(out_in)

    def body(first, second, emb, vec, bias_, *refs):
        middle, part, held, sems, held2, sems2 = refs[2 * count :]

        @pl.when(pl.program_id(0) == 0)
        def _():
            wait = fill(refs[:count], held, sems, skip)
            wait2 = fill(refs[count : 2 * count], held2, sems2)
            wait()
            wait2()

        total = emb[...] + vec[0:1] + (first[...].astype(F32) + second[...].astype(F32))
        value = norm_stats(total)[0] * vec[1:2] + vec[2:3]
        middle[...] = value
        hidden = dot(value.astype(BF), held[...]) + bias_[:, 2 * skip :]
        part[...] = nt(gelu(hidden).astype(BF), held2[...]).astype(BF)

    whole = pl.BlockSpec(memory_space=pltpu.VMEM)
    by_rows = pl.BlockSpec((block, width), lambda i: (i, 0))
    return kernel_call(
        body,
        [shape(rows, width, F32), shape(rows, width, BF)],
        [*parts, embedded, vectors, bias, *out_in, *down],
        2 * count,
        [*held_scratch(out_in, wide), *held_scratch(down)],
        grid=(rows // block,),
        specs=([by_rows, by_rows, by_rows, whole, whole], [by_rows, by_rows]),
    )


def rows_end(parts, middle, vectors, turn):
    rows, width = middle.shape
    block = 256 if rows % 256 == 0 else rows

    def body(first, second, mid, vec, turn_, out):
        total = mid[...] + vec[3:4] + (first[...].astype(F32) + second[...].astype(F32))
        final = norm_stats(total)[0] * vec[4:5] + vec[5:6]
        out[...] = nt(final.astype(BF), turn_[...]).astype(BF)

    whole = pl.BlockSpec(memory_space=pltpu.VMEM)
    by_rows = pl.BlockSpec((block, width), lambda i: (i, 0))
    return kernel_call(
        body,
        [shape(rows, width, BF)],
        [*parts, middle, vectors, turn],
        grid=(rows // block,),
        specs=([by_rows, by_rows, by_rows, whole, whole], [by_rows]),
    )[0]


def together(*values):
    return lax.optimization_barrier(values)


def per_device(
    tokens,
    embed_table,
    qkv_weight,
    qv_bias,
    out_weight,
    out_bias,
    norm1_gain,
    norm1_bias,
    in_weight,
    in_bias,
    down_weight,
    down_bias,
    norm2_gain,
    norm2_bias,
    masked_pos,
    replace_ids,
    masked_count,
    cotangent,
):
    size, cores = lax.axis_size("dp"), lax.axis_size("mp")
    me, core = lax.axis_index("dp"), lax.axis_index("mp")
    page_count, slot_count = masked_pos.shape
    length = tokens.shape[0] // page_count
    width = tokens.shape[1]
    shard_rows = width // size
    cut = shard_rows // 2
    table_rows = embed_table.shape[0]
    pages = page_count
    rows = pages * length
    own_slots = page_count // cores * slot_count
    slots = pages * slot_count
    head_cols = qkv_weight.shape[2]
    hidden_cols = in_weight.shape[1]
    far = far_digits(size)

    def to_core(values, step):
        pairs = [(c, (c + step) % cores) for c in range(cores)]
        return lax.ppermute(values, "mp", pairs)

    def from_cores(values):
        return [values] + [to_core(values, k) for k in range(1, cores)]

    def in_core_order(parts):
        whole = jnp.concatenate([parts[-k % cores] for k in range(cores)], axis=0)
        for at in range(1, cores):
            turned = jnp.concatenate([parts[(at - k) % cores] for k in range(cores)], axis=0)
            whole = jnp.where(core == at, turned, whole)
        return whole

    def own_pages(values):
        per = values.shape[0] // cores
        return lax.dynamic_slice_in_dim(values, core * per, per, 0)

    def spread_far(shard):
        blocks = [shard]
        for digit in far:
            packed = blocks[0] if len(blocks) == 1 else jnp.concatenate(blocks, axis=0)
            count = len(blocks)
            for step in range(1, digit[0]):
                got = send(packed, size, digit, step)
                blocks = blocks + [
                    got[k * shard_rows : (k + 1) * shard_rows] for k in range(count)
                ]
        return blocks

    def spread_near(blocks):
        halves = []
        for half, digit in enumerate(NEAR):
            packed = jnp.concatenate([b[:cut] if half == 0 else b[cut:] for b in blocks], axis=0)
            halves.append((packed, send(packed, size, digit, 1)))
        return halves

    def spread_last(halves):
        here, there = [], []
        for half, pair in enumerate(halves):
            packed = jnp.concatenate(pair, axis=0)
            here.append(packed)
            there.append(send(packed, size, NEAR[1 - half], 1))
        return here, there

    def in_order(here, there):
        return [p for pair in zip(here, there) for p in pair]

    def halved(parts):
        middle = parts[0].shape[0] // 2
        sums = []
        for at in (slice(0, middle), slice(middle, None)):
            total = parts[0][at].astype(F32)
            for part in parts[1:]:
                total = total + part[at].astype(F32)
            sums.append(total.astype(BF))
        return sums

    def sum_first(pieces):
        return [
            (pieces[2 * half], send(pieces[2 * half + 1], size, NEAR[1 - half], 1))
            for half in range(2)
        ]

    def sum_second(halves):
        done = []
        for half, pair in enumerate(halves):
            stay, leave_ = halved(pair)
            done.append((stay, send(leave_, size, NEAR[half], 1)))
        return done

    def sum_far(halves):
        kept = [(stay.astype(F32) + came.astype(F32)).astype(BF) for stay, came in halves]
        count = size // 4
        per = [part.shape[0] // count for part in kept]
        blocks = [
            jnp.concatenate([part[k * r : (k + 1) * r] for part, r in zip(kept, per)], axis=0)
            for k in range(count)
        ]
        for digit in far[:0:-1]:
            blocks = [add_up(terms).astype(BF) for terms in spread_fold(blocks, digit)]
        return spread_fold(blocks, far[0])[0]

    def spread_fold(blocks, digit):
        radix = digit[0]
        inner = len(blocks) // radix
        terms = [[block] for block in blocks[:inner]]
        for step in range(1, radix):
            group = blocks[step * inner : (step + 1) * inner]
            packed = group[0] if inner == 1 else jnp.concatenate(group, axis=0)
            got = send(packed, size, digit, radix - step)
            for k in range(inner):
                terms[k].append(got[k * shard_rows : (k + 1) * shard_rows])
        return terms

    def add_up(terms):
        total = terms[0].astype(F32)
        for term in terms[1:]:
            total = total + term.astype(F32)
        return total

    pad = -(slot_count + 1) % 128
    packed_ids = jnp.concatenate(
        [replace_ids, masked_count[:, None], jnp.zeros((page_count, pad), jnp.int32)], axis=1
    )
    packed_ids = jnp.broadcast_to(packed_ids[None], (size, *packed_ids.shape))
    all_ids = lax.all_to_all(packed_ids, "dp", 0, 0)
    qkv_far = spread_far(qkv_weight.reshape(shard_rows, 3 * head_cols))

    places = jnp.stack([me, core])
    row_of = masked_pos + jnp.arange(pages)[:, None] * length
    used = jnp.arange(slot_count)[None, :] < masked_count[:, None]
    page_codes = jnp.where(used, replace_ids, -1)
    codes = page_codes.reshape(1, slots)
    own_codes = own_pages(page_codes).reshape(1, own_slots)
    own_column = own_pages(row_of).reshape(own_slots, 1)
    line, column = row_of.reshape(1, slots), row_of.reshape(slots, 1)
    held_rows = held_order(size, shard_rows, me)[None, :]
    turn, turned_tokens, sent_hot = prepare(tokens, held_rows, own_codes, size, table_rows)
    out_in_shard = jnp.concatenate([out_weight.T, in_weight], axis=1)
    all_ids, turned_tokens, sent_hot, out_in_shard, *qkv_far = together(
        all_ids, turned_tokens, sent_hot, out_in_shard, *qkv_far
    )

    def device_codes(got):
        is_used = jnp.arange(slot_count)[None, None, :] < got[:, :, slot_count : slot_count + 1]
        return jnp.where(is_used, got[:, :, :slot_count], -1).reshape(size * cores, own_slots)

    all_codes = device_codes(all_ids)
    *hots, found, fullest = serve(places, all_codes, embed_table, size, cores)
    found = lax.all_to_all(found.reshape(size, ROOM, width), "dp", 0, 0)
    found = found.reshape(size * ROOM, width)
    qkv_near = spread_near(qkv_far)
    out_in_far = spread_far(out_in_shard)
    vectors = jnp.stack(
        [out_bias, norm1_gain, norm1_bias, down_bias, norm2_gain, norm2_bias] + [out_bias] * 2
    )
    grad_final, vectors = turn_small(cotangent.reshape(slots, width), codes, vectors, turn)
    bias = jnp.concatenate([qv_bias.reshape(-1), in_bias])[None]
    down_shard = down_weight.T
    found, fullest, hots, qkv_near, out_in_far, grad_final, down_shard = together(
        found, fullest, hots, qkv_near, out_in_far, grad_final, down_shard
    )

    rounds = (fullest[0, 0] + ROOM - 1) // ROOM

    def round_of(turn_, held):
        own, every, held = lax.optimization_barrier((own_codes[0], all_codes, held))
        low = turn_ * ROOM
        spots = jnp.arange(own_slots)
        before = (spots[:, None] < spots[None, :]).astype(BF)
        to_owner = (own >= 0)[:, None] & (own[:, None] // table_rows == jnp.arange(size))
        rank = tn(before, to_owner.astype(BF)).astype(jnp.int32) - low
        sent = (rank[:, :, None] == jnp.arange(ROOM)) & to_owner[:, :, None]
        sent = sent.astype(BF).reshape(own_slots, size * ROOM)
        mine = (every >= 0) & (every // table_rows == me)
        rank = dot(mine.astype(BF), before).astype(jnp.int32) - low
        hit = (rank[:, None, :] == jnp.arange(ROOM)[None, :, None]) & mine[:, None, :]
        asked = jnp.sum(jnp.where(hit, every[:, None, :] - me * table_rows + 1, 0), axis=2) - 1
        hot = (asked[:, :, None] == jnp.arange(table_rows)).astype(BF)
        hot = hot.reshape(size, cores, ROOM, table_rows)
        turned = [
            lax.dynamic_index_in_dim(hot, (core + cores - k) % cores, 1, keepdims=False)
            for k in range(cores)
        ]
        return sent, [t.reshape(size * ROOM, table_rows) for t in turned], held

    def more_rows(turn_, held):
        sent, later, held = round_of(turn_, held)
        got = dot(later[0], embed_table).astype(BF).reshape(size, ROOM, width)
        got = lax.all_to_all(got, "dp", 0, 0).reshape(size * ROOM, width)
        return held + dot(sent, got)

    new_rows = lax.fori_loop(1, rounds, more_rows, dot(sent_hot, found))
    new_rows = in_core_order(from_cores(new_rows.astype(BF)))

    qkv_here, qkv_there = spread_last(qkv_near)
    out_in_near = spread_near(out_in_far)
    down_far = spread_far(down_shard)
    new_rows, qkv_here, qkv_there, out_in_near, down_far = together(
        new_rows, qkv_here, qkv_there, out_in_near, down_far
    )

    qkv_pieces = in_order(qkv_here, qkv_there)
    embedded, low, query, key, value, s_embedded, s_low, s_query, s_attended = enter(
        turned_tokens, new_rows, turn, line, column, bias, qkv_pieces, pages
    )
    out_in_here, out_in_there = spread_last(out_in_near)
    down_near = spread_near(down_far)
    s_attended, query, out_in_here, out_in_there, down_near = together(
        s_attended, query, out_in_here, out_in_there, down_near
    )

    out_in_pieces = in_order(out_in_here, out_in_there)
    down_here, down_there = spread_last(down_near)
    s_parts = from_cores(out_part(s_attended, out_in_pieces, F32))
    attended = attend_all(query, key, value, pages)
    s_parts, attended, down_here, down_there = together(s_parts, attended, down_here, down_there)

    down_pieces = in_order(down_here, down_there)
    unit1, scale1, middle_low, hidden, slope, s_part = slot_forward(
        s_parts, s_embedded, vectors, bias, out_in_pieces, down_pieces
    )
    s_parts = from_cores(s_part)
    rows_part = out_part(attended, out_in_pieces, BF)
    s_parts, rows_part = together(s_parts, rows_part)

    *grad_down, grad_r2, grad_hidden_in, small2, grad_in_bias, s_part = slot_turn(
        s_parts, hidden, slope, unit1, grad_final, vectors, out_in_pieces, down_pieces
    )
    s_parts = from_cores(s_part)
    rows_parts = from_cores(rows_part)
    down_sum = sum_first(grad_down)
    grad_in = in_grad(middle_low, grad_hidden_in, [p.shape[0] for p in down_pieces])
    in_sum = sum_first(grad_in)
    s_parts, grad_in, rows_parts = together(s_parts, grad_in, rows_parts)

    *grad_qkv_out, grad_r1, grad_query, grad_key, grad_value, small1, small0 = slot_back(
        s_parts,
        grad_r2,
        unit1,
        scale1,
        s_attended,
        s_query,
        key,
        value,
        s_low,
        low,
        vectors,
        out_in_pieces,
        pages,
    )
    down_sum, grad_qkv_out, grad_key = together(down_sum, grad_qkv_out, grad_key)

    down_sum = sum_second(down_sum)
    part = leave_part(grad_query, grad_key, grad_value, line, qkv_pieces, pages)
    parts = from_cores(part)
    middle, rows_part = rows_forward(
        rows_parts, embedded, vectors, bias, out_in_pieces, down_pieces
    )
    down_sum, in_sum, parts, rows_part = together(down_sum, in_sum, parts, rows_part)

    in_sum = sum_second(in_sum)
    down_sum = sum_far(down_sum)
    qkv_out_sum = sum_first(grad_qkv_out)
    rows_parts = from_cores(rows_part)
    grad_input, moved = leave(
        parts,
        grad_r1,
        line,
        own_column,
        turn,
        held_rows,
        sent_hot,
        [small1, small2, small0, grad_in_bias],
        size,
        pages,
    )
    in_sum, down_sum, qkv_out_sum, rows_parts, grad_input, moved = together(
        in_sum, down_sum, qkv_out_sum, rows_parts, grad_input, moved
    )

    gots = lax.all_to_all(moved, "dp", 0, 0)
    in_sum = sum_far(in_sum)
    qkv_out_sum = sum_second(qkv_out_sum)
    output = rows_end(rows_parts, middle, vectors, turn)
    down_share = add_up(down_sum).T
    gots, in_sum, qkv_out_sum, output, down_share = together(
        gots, in_sum, qkv_out_sum, output, down_share
    )

    qkv_out_sum = sum_far(qkv_out_sum)
    in_share = add_up(in_sum)
    grad_table, totals = collect(hots, from_cores(gots))
    qkv_out_sum, in_share, grad_table, totals = together(
        qkv_out_sum, in_share, grad_table, totals
    )
    qkv_out_share = add_up(qkv_out_sum)
    qkv_share = qkv_out_share[:, : 3 * head_cols].reshape(shard_rows, 3, head_cols)
    out_share = qkv_out_share[:, 3 * head_cols :].T
    grad_rows = grad_input

    def more_table(turn_, held):
        sent, later, held = round_of(turn_, held)
        rows_here, held = together(grad_rows, held)
        slot_grad = jnp.take(rows_here, own_column[:, 0], axis=0).astype(BF)
        got = tn(sent, slot_grad).astype(BF).reshape(size, ROOM, width)
        for hot, block in zip(later, from_cores(lax.all_to_all(got, "dp", 0, 0))):
            held = held + tn(hot, block.reshape(size * ROOM, width))
        return held

    grad_table = lax.fori_loop(1, rounds, more_table, grad_table)

    def piece(row, block, count):
        return totals[row, block * 128 : block * 128 + count]

    vec = [piece(0, k, shard_rows) for k in range(6)]
    own = [
        piece(1, 0, head_cols // size),
        piece(1, 1, head_cols // size),
        piece(1, 2, hidden_cols // size),
    ]

    return (
        output,
        grad_input,
        grad_table,
        qkv_share,
        jnp.stack([own[0], own[1]])[:, None, :],
        out_share,
        vec[0],
        vec[1],
        vec[2],
        in_share,
        own[2][None],
        down_share,
        vec[3],
        vec[4],
        vec[5],
    )


def solution(mesh):
    in_specs = (
        P("dp", None),
        P("dp", None),
        P("dp", None, "mp"),
        P(None, "mp"),
        P("mp", "dp"),
        P(),
        P(),
        P(),
        P("dp", "mp"),
        P("mp"),
        P("mp", "dp"),
        P(),
        P(),
        P(),
        P("dp", None),
        P("dp", None),
        P("dp"),
        P("dp", None, None),
    )
    out_specs = (
        P("dp", None),
        P("dp", None),
        P("dp", None),
        P("dp", None, "mp"),
        P(None, "mp", "dp"),
        P("mp", "dp"),
        P("dp"),
        P("dp"),
        P("dp"),
        P("dp", "mp"),
        P("mp", "dp"),
        P("mp", "dp"),
        P("dp"),
        P("dp"),
        P("dp"),
    )
    return jax.shard_map(
        per_device, mesh=mesh, in_specs=in_specs, out_specs=out_specs, check_vma=False
    )
```

```python
import jax
import jax.numpy as jnp
import numpy as np
from jax import lax
from jax.experimental import pallas as pl
from jax.experimental.pallas import tpu as pltpu
from jax.sharding import PartitionSpec as P

HEAD = 64
EPSILON = 1e-05
ROOM = 16
EXTRA = 8

BF = jnp.bfloat16
F32 = jnp.float32


def dot(a, b, dims=((1,), (0,)), **kw):
    return lax.dot_general(a, b, (dims, ((), ())), preferred_element_type=F32, **kw)


def nt(a, b):
    return dot(a, b, ((1,), (1,)))


def tn(a, b):
    return dot(a, b, ((0,), (0,)))


def split_two(values):
    high = values.astype(BF)
    return high, (values - high.astype(F32)).astype(BF)


def far_digits(size):
    found = []
    stride, rest = 4, size // 4
    while rest > 1:
        radix = next(r for r in (4, 2, 3, 5, 7, rest) if rest % r == 0)
        found.append((radix, stride))
        stride, rest = stride * radix, rest // radix
    return found


NEAR = ((2, 1), (2, 2))


def shift(size, digit, step):
    radix, stride = digit
    pairs = []
    for src in range(size):
        own = (src // stride) % radix
        pairs.append((src, src + ((own + step) % radix - own) * stride))
    return pairs


def send(values, size, digit, step):
    return lax.ppermute(values, "dp", shift(size, digit, step))


def held_order(size, rows, me):
    blocks = size // 8
    place = jnp.arange(size * rows)
    second = place >= size * rows // 2
    slot, row = (place % (size * rows // 2)) // rows, place % rows
    block = slot % blocks + jnp.where(second, blocks, 0)
    low, high = (slot // blocks) % 2, slot // blocks // 2
    owner = jnp.zeros_like(place)
    for radix, stride in far_digits(size):
        owner = owner + ((me // stride - block % radix) % radix) * stride
        block = block // radix
    x_step, y_step = jnp.where(second, high, low), jnp.where(second, low, high)
    owner = owner + (me - x_step) % 2 + ((me // 2 - y_step) % 2) * 2
    return owner * rows + row


VMEM_LIMIT = 56 * 1024 * 1024


def kernel_call(body, outs, inputs, far_count=0, scratch=(), flops=0, grid=None, specs=None):
    near = len(inputs) - far_count
    in_specs, out_specs = specs or (
        [pl.BlockSpec(memory_space=pltpu.VMEM)] * near,
        [pl.BlockSpec(memory_space=pltpu.VMEM)] * len(outs),
    )
    return pl.pallas_call(
        body,
        grid=grid or (),
        out_shape=outs,
        in_specs=[*in_specs, *([pl.BlockSpec(memory_space=pl.ANY)] * far_count)],
        out_specs=out_specs,
        scratch_shapes=scratch,
        compiler_params=pltpu.CompilerParams(vmem_limit_bytes=VMEM_LIMIT),
        cost_estimate=pl.CostEstimate(flops=1, bytes_accessed=1, transcendentals=0),
    )(*inputs)


def shape(rows, cols, dtype):
    return jax.ShapeDtypeStruct((rows, cols), dtype)


def fill(pieces, held, sems, start=0):
    copies, at = [], 0
    for i, piece in enumerate(pieces):
        rows = piece.shape[0]
        source = piece.at[:, pl.ds(start, held.shape[1])]
        copy = pltpu.make_async_copy(source, held.at[pl.ds(at, rows)], sems.at[i])
        copy.start()
        copies.append(copy)
        at += rows

    def wait():
        for copy in copies:
            copy.wait()

    return wait


def held_scratch(pieces, cols=None):
    rows = sum(p.shape[0] for p in pieces)
    return [
        pltpu.VMEM((rows, cols or pieces[0].shape[1]), BF),
        pltpu.SemaphoreType.DMA((len(pieces),)),
    ]


def norm_stats(values):
    row_mean = jnp.mean(values, axis=-1, keepdims=True)
    centered = values - row_mean
    scale = lax.rsqrt(jnp.mean(centered * centered, axis=-1, keepdims=True) + EPSILON)
    return centered * scale, scale


def norm_back(grad, unit, scale, gain):
    inner = grad * gain
    mean_inner = jnp.mean(inner, axis=-1, keepdims=True)
    mean_unit = jnp.mean(inner * unit, axis=-1, keepdims=True)
    return (
        scale * (inner - mean_inner - unit * mean_unit),
        jnp.sum(grad * unit, axis=0, keepdims=True),
        jnp.sum(grad, axis=0, keepdims=True),
    )


def gelu(values):
    return values * (0.5 + 0.5 * lax.erf(values * (0.5**0.5)))


def gelu_both(values):
    normal = 0.5 + 0.5 * lax.erf(values * (0.5**0.5))
    bell = jnp.exp(-0.5 * values * values) * (0.5 / np.pi) ** 0.5
    return values * normal, normal + values * bell


def head_masks(dtype):
    lane = lax.broadcasted_iota(jnp.int32, (1, 2 * HEAD), 1)
    return [(lane // HEAD == h).astype(dtype) for h in range(2)]


def attend_pair(query, key, value):
    outs = []
    for mask in head_masks(BF):
        scores = nt(query * mask, key)
        powers = jnp.exp(scores - jnp.max(scores, axis=-1, keepdims=True))
        prob = powers * (1.0 / jnp.sum(powers, axis=-1, keepdims=True))
        outs.append(dot(prob.astype(BF), value))
    first, second = head_masks(F32)
    return (outs[0] * first + outs[1] * second).astype(BF)


def one_hot_rows(row_of_line, rows):
    at = lax.broadcasted_iota(jnp.int32, (rows, row_of_line.shape[1]), 0)
    return (at == row_of_line).astype(F32).astype(BF)


def one_hot_slots(row_of_column, rows):
    at = lax.broadcasted_iota(jnp.int32, (row_of_column.shape[0], rows), 1)
    return (at == row_of_column).astype(F32).astype(BF)


def as_column(line):
    count = line.shape[1]
    square = (count, count)
    same = lax.broadcasted_iota(jnp.int32, square, 0) == lax.broadcasted_iota(jnp.int32, square, 1)
    return jnp.sum(jnp.where(same, line.astype(F32), 0.0), axis=1, keepdims=True)


def floor_by(values, divisor):
    return jnp.floor((values + 0.5) * (1.0 / divisor))


def iota(dims, axis):
    return lax.broadcasted_iota(jnp.int32, dims, axis).astype(F32)


def serve(places, codes, table, size, cores):
    table_rows, width = table.shape
    devices, slots = codes.shape
    count = size * ROOM

    def body(place, code, tab, *outs):
        *hots, found, most = outs
        me, core = place[0], place[1]
        line = code[...].astype(F32)
        local = line - (me * table_rows).astype(F32)
        mine = (local >= 0) & (local < table_rows)
        before = (iota((slots, slots), 0) < iota((slots, slots), 1)).astype(BF)
        rank = dot(mine.astype(F32).astype(BF), before)
        rank = jnp.where(mine & (rank < ROOM), rank, 255.0).astype(BF)
        local = jnp.where(mine, local, 0.0)
        local_high = floor_by(local, 256)
        local_low = (local - 256 * local_high).astype(BF)
        local_high = local_high.astype(BF)
        source = floor_by(iota((count, 1), 0), ROOM)
        room = iota((count, 1), 0) - ROOM * source
        for k in range(cores):
            which = lax.rem(core + cores - k, cores).astype(F32)
            pick = (iota((count, devices), 1) == source * cores + which).astype(F32).astype(BF)
            hit = dot(pick, rank) == room
            at = 256 * dot(pick, local_high) + dot(pick, local_low) + 1.0
            asked = jnp.sum(jnp.where(hit, at, 0.0), axis=1, keepdims=True) - 1.0
            hots[k][...] = (iota((count, table_rows), 1) == asked).astype(F32).astype(BF)
        found[...] = dot(hots[0][...], tab[...]).astype(BF)
        owner = floor_by(line, table_rows)
        fullest = jnp.zeros((devices, 1), F32)
        for o in range(size):
            here = jnp.sum(jnp.where(owner == o, 1.0, 0.0), axis=1, keepdims=True)
            fullest = jnp.maximum(fullest, here)
        fullest = jnp.max(fullest, axis=0, keepdims=True)
        most[...] = fullest.astype(jnp.int32)

    smem, vmem = pl.BlockSpec(memory_space=pltpu.SMEM), pl.BlockSpec(memory_space=pltpu.VMEM)
    return kernel_call(
        body,
        [
            *[shape(count, table_rows, BF)] * cores,
            shape(count, width, BF),
            shape(1, 1, jnp.int32),
        ],
        [places, codes, table],
        flops=2 * count * table_rows * width,
        specs=([smem, vmem, vmem], [vmem] * (cores + 2)),
    )


def by_owner(values, owner, place, size):
    count = values.shape[1]
    hit = (iota((size, count), 0) == owner).astype(F32)
    rows = jnp.concatenate([hit * values[r : r + 1] for r in range(values.shape[0])], axis=0)
    hot = (iota((128, count), 0) == place).astype(F32).astype(BF)
    total, rest = 0.0, rows
    for _ in range(3):
        high = rest.astype(BF)
        rest = rest - high.astype(F32)
        total = total + nt(high, hot)
    return total


def prepare(tokens, cotangent, vectors, order, codes, own_codes, size, table_rows):
    rows, width = tokens.shape
    slots = own_codes.shape[1]
    pages, per = codes.shape

    def body(tok, cot, vec, order_, code, own, turn, tok_out, cot_out, vec_out, sent):
        turn[...] = (
            (lax.broadcasted_iota(jnp.int32, (width, width), 0) == order_[...])
            .astype(F32)
            .astype(BF)
        )
        tok_out[...] = dot(tok[...], turn[...]).astype(BF)
        line = own[...].astype(F32)
        column = as_column(line)
        owner_line, owner = floor_by(line, table_rows), floor_by(column, table_rows)
        square = (slots, slots)
        earlier = (iota(square, 1) < iota(square, 0)) & (owner_line == owner)
        rank = jnp.sum(jnp.where(earlier, 1.0, 0.0), axis=1, keepdims=True)
        target = jnp.where((column >= 0) & (rank < ROOM), owner * ROOM + rank, -1.0)
        sent[...] = (iota((slots, size * ROOM), 1) == target).astype(F32).astype(BF)
        for g in range(pages):
            here = slice(g * per, (g + 1) * per)
            used = (as_column(code[g : g + 1]) >= 0).astype(F32).astype(BF)
            cot_out[here] = dot(cot[here] * used, turn[...]).astype(BF)
        rest, total = vec[...], 0.0
        for _ in range(3):
            high = rest.astype(BF)
            rest = rest - high.astype(F32)
            total = total + dot(high, turn[...])
        vec_out[...] = total

    return kernel_call(
        body,
        [
            shape(width, width, BF),
            shape(rows, width, BF),
            shape(pages * per, width, BF),
            shape(vectors.shape[0], width, F32),
            shape(slots, size * ROOM, BF),
        ],
        [tokens, cotangent, vectors, order, codes, own_codes],
    )


def enter(tokens, new_rows, turn, pos, qv_bias, pieces):
    rows, width = tokens.shape
    pages, per = pos.shape
    slots = pages * per
    cols = qv_bias.shape[1]
    length = rows // pages

    def body(*refs):
        tok, found, turn_, pos_, bias_ = refs[:5]
        piece_refs = refs[5 : 5 + len(pieces)]
        emb, low, q, k, v, s_emb, s_low, s_q, s_att, s_out, held, sems = refs[5 + len(pieces) :]
        wait = fill(piece_refs, held, sems)
        new = dot(found[...].astype(BF), turn_[...]).astype(BF)
        hots = []
        for g in range(pages):
            page, here = slice(g * length, (g + 1) * length), slice(g * per, (g + 1) * per)
            placed = one_hot_rows(pos_[g : g + 1], length)
            hot = one_hot_slots(as_column(pos_[g : g + 1]), length)
            hots.append(hot)
            exact = tok[page].astype(F32) + dot(placed, new[here])
            emb[page] = exact
            low[page] = exact.astype(BF)
            s_emb[here] = dot(hot, tok[page]) + new[here].astype(F32)
        s_low[...] = s_emb[...].astype(BF)
        wait()
        for g in range(pages):
            page, here = slice(g * length, (g + 1) * length), slice(g * per, (g + 1) * per)
            q[page] = (dot(low[page], held[:, :cols]) + bias_[0:1]).astype(BF)
            k[page] = dot(low[page], held[:, cols : 2 * cols]).astype(BF)
            v[page] = (dot(low[page], held[:, 2 * cols : 3 * cols]) + bias_[1:2]).astype(BF)
            s_q[here] = dot(hots[g], q[page]).astype(BF)
            for j in range(0, cols, 2 * HEAD):
                at = slice(j, j + 2 * HEAD)
                s_att[here, at] = attend_pair(s_q[here, at] * HEAD**-0.5, k[page, at], v[page, at])
        s_out[...] = nt(s_att[...], held[:, 3 * cols :])

    outs = [
        shape(rows, width, F32),
        shape(rows, width, BF),
        *[shape(rows, cols, BF)] * 3,
        shape(slots, width, F32),
        shape(slots, width, BF),
        *[shape(slots, cols, BF)] * 2,
        shape(slots, width, F32),
    ]
    return kernel_call(
        body,
        outs,
        [tokens, new_rows, turn, pos, qv_bias, *pieces],
        len(pieces),
        held_scratch(pieces),
    )


def attend_all(query, key, value, pieces, pages):
    rows, cols = query.shape
    length, pairs = rows // pages, cols // (2 * HEAD)
    width = sum(p.shape[0] for p in pieces)

    def body(q, k, v, *refs):
        out, total, held, sems = refs[len(pieces) :]
        first, pair = pl.program_id(0) == 0, pl.program_id(1)

        @pl.when(first & (pair == 0))
        def _():
            fill(refs[: len(pieces)], held, sems, 3 * cols)()

        half = length // 2
        for part in range(2):
            here = slice(part * half, (part + 1) * half)
            attended = attend_pair(q[here] * HEAD**-0.5, k[...], v[...])
            at = pl.ds(pl.multiple_of(pair * 2 * HEAD, 2 * HEAD), 2 * HEAD)
            total[here, at] = attended

        @pl.when(pair == pairs - 1)
        def _():
            out[...] = nt(total[...], held[...]).astype(BF)

    spec = pl.BlockSpec((length, 2 * HEAD), lambda g, j: (g, j))
    return kernel_call(
        body,
        [shape(rows, width, BF)],
        [query, key, value, *pieces],
        len(pieces),
        [pltpu.VMEM((length, cols), BF), *held_scratch(pieces, cols)],
        grid=(pages, pairs),
        specs=([spec] * 3, [pl.BlockSpec((length, width), lambda g, j: (g, 0))]),
    )[0]


def slot_forward(parts, embedded, vectors, bias, in_pieces, down_pieces):
    slots, width = embedded.shape
    wide = in_pieces[0].shape[1]
    count = len(in_pieces)

    def body(first, second, emb, vec, bias_, *refs):
        unit1, scale1, mid_low, hid, slope, part, held, sems, held2, sems2 = refs[2 * count :]
        wait = fill(refs[:count], held, sems)
        wait2 = fill(refs[count : 2 * count], held2, sems2)
        unit, scale = norm_stats(emb[...] + vec[0:1] + (first[...] + second[...]))
        unit1[...] = unit
        scale1[...] = jnp.broadcast_to(scale, scale1.shape)
        mid_low[...] = (unit * vec[1:2] + vec[2:3]).astype(BF)
        wait()
        value, rate = gelu_both(dot(mid_low[...], held[...]) + bias_[...])
        hid[...] = value.astype(BF)
        slope[...] = rate
        wait2()
        part[...] = nt(hid[...], held2[...])

    outs = [
        shape(slots, width, F32),
        shape(slots, 128, F32),
        shape(slots, width, BF),
        shape(slots, wide, BF),
        shape(slots, wide, F32),
        shape(slots, width, F32),
    ]
    return kernel_call(
        body,
        outs,
        [*parts, embedded, vectors, bias, *in_pieces, *down_pieces],
        2 * count,
        [*held_scratch(in_pieces), *held_scratch(down_pieces)],
    )


def put_rows(outs, start, values):
    at = 0
    for out in outs:
        rows = out.shape[0]
        out[:, start : start + values.shape[1]] = values[at : at + rows].astype(BF)
        at += rows


def slot_turn(parts, hidden, slope, unit1, mid_low, grad_final, vectors, in_pieces, down_pieces):
    slots, width = unit1.shape
    wide = hidden.shape[1]
    count = len(in_pieces)

    def body(first, second, hid, slp, un1, mid_, final, vec, *refs):
        (*grads, grad2, small, in_small, mid, held, sems, held2, sems2) = refs[2 * count :]
        wait = fill(refs[:count], held, sems)
        wait2 = fill(refs[count : 2 * count], held2, sems2)
        total = un1[...] * vec[1:2] + vec[2:3] + vec[3:4] + (first[...] + second[...])
        unit, scale = norm_stats(total)
        grad, gain, bias = norm_back(final[...].astype(F32), unit, scale, vec[4:5])
        grad2[...] = grad
        grad_low = grad.astype(BF)
        small[0:1] = jnp.sum(grad_low.astype(F32), axis=0, keepdims=True)
        small[1:2] = gain
        small[2:3] = bias
        small[3:8] = jnp.zeros((5, width), F32)
        wait2()
        back = (dot(grad_low, held2[...]) * slp[...]).astype(BF)
        in_small[...] = jnp.sum(back.astype(F32), axis=0, keepdims=True)
        wait()
        mid[...] = nt(back, held[...])
        put_rows(grads[:count], 0, tn(grad_low, hid[...]))
        put_rows(grads[count:], 0, tn(mid_[...], back))

    outs = [
        *[shape(p.shape[0], wide, BF) for p in (*down_pieces, *in_pieces)],
        shape(slots, width, F32),
        shape(8, width, F32),
        shape(1, wide, F32),
        shape(slots, width, F32),
    ]
    return kernel_call(
        body,
        outs,
        [*parts, hidden, slope, unit1, mid_low, grad_final, vectors, *in_pieces, *down_pieces],
        2 * count,
        [*held_scratch(in_pieces), *held_scratch(down_pieces)],
    )


def slot_back(parts, grad2, unit1, scale1, attended, s_query, key, value, s_low, low, vectors, pos, pieces):
    slots, width = unit1.shape
    rows, cols = key.shape
    pages, per = pos.shape
    length = rows // pages
    scale = HEAD**-0.5

    def body(first, second, g2, un1, sc1, att, sq, k, v, sl, lo, vec, pos_, *refs):
        (*grads, grad1, part, small, small_heads, gq, gk, gv, held, sems) = refs[len(pieces) :]
        wait = fill(refs[: len(pieces)], held, sems)
        total = g2[...] + (first[...] + second[...])
        grad, gain, bias = norm_back(total, un1[...], sc1[:, :1], vec[1:2])
        grad1[...] = grad
        grad_low = grad.astype(BF)
        small[0:1] = jnp.sum(grad_low.astype(F32), axis=0, keepdims=True)
        small[1:2] = gain
        small[2:3] = bias
        small[3:8] = jnp.zeros((5, width), F32)
        put_rows(grads, 3 * cols, tn(grad_low, att[...]))
        wait()
        gatt = dot(grad_low, held[:, 3 * cols :]).astype(BF)
        masks = head_masks(BF)
        left_lanes, right_lanes = head_masks(F32)
        for g in range(pages):
            here, page = slice(g * per, (g + 1) * per), slice(g * length, (g + 1) * length)
            for j in range(0, cols, 2 * HEAD):
                at = slice(j, j + 2 * HEAD)
                query, back = sq[here, at], gatt[here, at]
                keys, values = k[page, at], v[page, at]
                got = []
                for mask in masks:
                    scores = nt(query * mask * scale, keys)
                    powers = jnp.exp(scores - jnp.max(scores, axis=-1, keepdims=True))
                    prob = powers * (1.0 / jnp.sum(powers, axis=-1, keepdims=True))
                    grad_prob = nt(back * mask, values)
                    inner = jnp.sum(prob * grad_prob, axis=-1, keepdims=True)
                    grad_scores = (prob * (grad_prob - inner)).astype(BF)
                    got.append(
                        (
                            dot(grad_scores, keys),
                            tn(grad_scores, query),
                            tn(prob.astype(BF), back),
                        )
                    )
                left, right = got
                gq[here, at] = ((left[0] * left_lanes + right[0] * right_lanes) * scale).astype(BF)
                gk[page, at] = ((left[1] * left_lanes + right[1] * right_lanes) * scale).astype(BF)
                gv[page, at] = (left[2] * left_lanes + right[2] * right_lanes).astype(BF)
        small_heads[0:1] = jnp.sum(gq[...].astype(F32), axis=0, keepdims=True)
        small_heads[1:2] = jnp.sum(gv[...].astype(F32), axis=0, keepdims=True)
        small_heads[2:8] = jnp.zeros((6, cols), F32)
        put_rows(grads, 0, tn(sl[...], gq[...]))
        put_rows(grads, cols, tn(lo[...], gk[...]))
        put_rows(grads, 2 * cols, tn(lo[...], gv[...]))
        high, rest = split_two(nt(gq[...], held[:, :cols]))
        for g in range(pages):
            here, page = slice(g * per, (g + 1) * per), slice(g * length, (g + 1) * length)
            placed = one_hot_rows(pos_[g : g + 1], length)
            total = nt(gk[page], held[:, cols : 2 * cols]) + nt(gv[page], held[:, 2 * cols : 3 * cols])
            total = total + dot(placed, high[here]) + dot(placed, rest[here])
            part[page] = total.astype(BF)

    outs = [
        *[shape(p.shape[0], 4 * cols, BF) for p in pieces],
        shape(slots, width, F32),
        shape(rows, width, BF),
        shape(8, width, F32),
        shape(8, cols, F32),
    ]
    return kernel_call(
        body,
        outs,
        [*parts, grad2, unit1, scale1, attended, s_query, key, value, s_low, low, vectors, pos, *pieces],
        len(pieces),
        [
            pltpu.VMEM((slots, cols), BF),
            *[pltpu.VMEM((rows, cols), BF)] * 2,
            *held_scratch(pieces),
        ],
    )


def leave(places, parts, grad1, pos, turn, order, sent_hot, smalls, size):
    rows, width = parts[0].shape
    pages, per = pos.shape
    length = rows // pages
    own = sent_hot.shape[0] // per
    cols, wide = smalls[2].shape[1], smalls[3].shape[1]

    def body(place_, first, second, g1, pos_, turn_, order_, hot, sm1, sm2, smq, smh, out, moved, mine):
        high, low = split_two(g1[...])
        for g in range(pages):
            page, here = slice(g * length, (g + 1) * length), slice(g * per, (g + 1) * per)
            placed = one_hot_rows(pos_[g : g + 1], length)
            total = first[page].astype(F32) + second[page].astype(F32)
            total = total + dot(placed, high[here]) + dot(placed, low[here])
            near, rest = split_two(total)
            out[page] = nt(near, turn_[...]) + nt(rest, turn_[...])

        place = order_[...].astype(F32)
        owner = floor_by(place, width // size)
        vec = jnp.concatenate([sm1[0:3], sm2[0:3]], axis=0)
        vec = by_owner(vec, owner, place - owner * (width // size), size)
        vec = jnp.concatenate([vec[r * size : (r + 1) * size] for r in range(6)], axis=1)
        at = iota((1, cols), 1)
        owner = floor_by(at, cols // size)
        head = by_owner(smq[0:2], owner, at - owner * (cols // size), size)
        at = iota((1, wide), 1)
        owner = floor_by(at, wide // size)
        unit = by_owner(smh[...], owner, at - owner * (wide // size), size)
        others = jnp.concatenate([head[:size], head[size:], unit], axis=1)
        filler = jnp.zeros((size, width - others.shape[1]), F32)
        others = jnp.concatenate([others, filler], axis=1)
        tails = [p.astype(F32) for values in (vec, others) for p in split_two(values)]
        going = 0.0
        for i in range(own):
            page = place_[1] * own + i
            slot_hot = one_hot_slots(as_column(pos_[pl.ds(page, 1)]), length)
            here = out[pl.ds(pl.multiple_of(page * length, length), length)]
            picked = dot(slot_hot, here.astype(BF)).astype(BF)
            mine[i * per : (i + 1) * per] = picked
            going = going + tn(hot[i * per : (i + 1) * per], picked)
        for s in range(size):
            moved[s, :ROOM] = going[s * ROOM : (s + 1) * ROOM].astype(BF)
            tail = [t[s : s + 1] for t in tails] + [jnp.zeros((EXTRA - len(tails), width), F32)]
            moved[s, ROOM:] = jnp.concatenate(tail, axis=0).astype(BF)

    return kernel_call(
        body,
        [
            shape(rows, width, F32),
            jax.ShapeDtypeStruct((size, ROOM + EXTRA, width), BF),
            shape(own * per, width, BF),
        ],
        [places, *parts, grad1, pos, turn, order, sent_hot, *smalls],
        specs=(
            [
                pl.BlockSpec(memory_space=pltpu.SMEM),
                *([pl.BlockSpec(memory_space=pltpu.VMEM)] * 11),
            ],
            [pl.BlockSpec(memory_space=pltpu.VMEM)] * 3,
        ),
    )


def collect(hots, gots):
    cores, (count, table_rows) = len(hots), hots[0].shape
    size, held, width = gots[0].shape

    def body(*refs):
        hot, got = refs[:cores], refs[cores : 2 * cores]
        table, sums = refs[2 * cores :]
        value = 0.0
        for k in range(cores):
            rows = jnp.concatenate([got[k][s, :ROOM] for s in range(size)], axis=0)
            value = value + tn(hot[k][...], rows)
        table[...] = value
        tail = jnp.zeros((held - ROOM, width), F32)
        for s in range(size):
            tail = tail + got[0][s, ROOM:].astype(F32)
        sums[...] = jnp.concatenate(
            [tail[0:1] + tail[1:2], tail[2:3] + tail[3:4], jnp.zeros((6, width), F32)], axis=0
        )

    return kernel_call(
        body,
        [shape(table_rows, width, F32), shape(8, width, F32)],
        [*hots, *gots],
    )


def rows_forward(parts, embedded, vectors, bias, in_pieces, down_pieces):
    rows, width = embedded.shape
    wide = in_pieces[0].shape[1]
    block = 256 if rows % 256 == 0 else rows
    count = len(in_pieces)

    def body(first, second, emb, vec, bias_, *refs):
        middle, part, held, sems, held2, sems2 = refs[2 * count :]

        @pl.when(pl.program_id(0) == 0)
        def _():
            wait = fill(refs[:count], held, sems)
            wait2 = fill(refs[count : 2 * count], held2, sems2)
            wait()
            wait2()

        total = emb[...] + vec[0:1] + (first[...].astype(F32) + second[...].astype(F32))
        value = norm_stats(total)[0] * vec[1:2] + vec[2:3]
        middle[...] = value
        hidden = dot(value.astype(BF), held[...]) + bias_[...]
        part[...] = nt(gelu(hidden).astype(BF), held2[...]).astype(BF)

    whole = pl.BlockSpec(memory_space=pltpu.VMEM)
    by_rows = pl.BlockSpec((block, width), lambda i: (i, 0))
    return kernel_call(
        body,
        [shape(rows, width, F32), shape(rows, width, BF)],
        [*parts, embedded, vectors, bias, *in_pieces, *down_pieces],
        2 * count,
        [*held_scratch(in_pieces), *held_scratch(down_pieces)],
        grid=(rows // block,),
        specs=([by_rows, by_rows, by_rows, whole, whole], [by_rows, by_rows]),
    )


def rows_end(parts, middle, vectors, turn):
    rows, width = middle.shape
    block = 256 if rows % 256 == 0 else rows

    def body(first, second, mid, vec, turn_, out):
        total = mid[...] + vec[3:4] + (first[...].astype(F32) + second[...].astype(F32))
        final = norm_stats(total)[0] * vec[4:5] + vec[5:6]
        out[...] = nt(final.astype(BF), turn_[...]).astype(BF)

    whole = pl.BlockSpec(memory_space=pltpu.VMEM)
    by_rows = pl.BlockSpec((block, width), lambda i: (i, 0))
    return kernel_call(
        body,
        [shape(rows, width, BF)],
        [*parts, middle, vectors, turn],
        grid=(rows // block,),
        specs=([by_rows, by_rows, by_rows, whole, whole], [by_rows]),
    )[0]


def together(*values):
    return lax.optimization_barrier(values)


def per_device(
    tokens,
    embed_table,
    qkv_weight,
    qv_bias,
    out_weight,
    out_bias,
    norm1_gain,
    norm1_bias,
    in_weight,
    in_bias,
    down_weight,
    down_bias,
    norm2_gain,
    norm2_bias,
    masked_pos,
    replace_ids,
    masked_count,
    cotangent,
):
    size, cores = lax.axis_size("dp"), lax.axis_size("mp")
    me, core = lax.axis_index("dp"), lax.axis_index("mp")
    page_count, slot_count = masked_pos.shape
    length = tokens.shape[0] // page_count
    width = tokens.shape[1]
    shard_rows = width // size
    cut = size // 8
    table_rows = embed_table.shape[0]
    pages = page_count
    rows = pages * length
    own_slots = page_count // cores * slot_count
    slots = pages * slot_count
    head_cols = qkv_weight.shape[2]
    hidden_cols = in_weight.shape[1]
    far = far_digits(size)

    def to_core(values, step):
        pairs = [(c, (c + step) % cores) for c in range(cores)]
        return lax.ppermute(values, "mp", pairs)

    def from_cores(values):
        return [values] + [to_core(values, k) for k in range(1, cores)]

    def in_core_order(parts):
        whole = jnp.concatenate([parts[-k % cores] for k in range(cores)], axis=0)
        for at in range(1, cores):
            turned = jnp.concatenate([parts[(at - k) % cores] for k in range(cores)], axis=0)
            whole = jnp.where(core == at, turned, whole)
        return whole

    def own_pages(values):
        per = values.shape[0] // cores
        return lax.dynamic_slice_in_dim(values, core * per, per, 0)

    def spread_far(shard):
        blocks = [shard]
        for digit in far:
            packed = blocks[0] if len(blocks) == 1 else jnp.concatenate(blocks, axis=0)
            count = len(blocks)
            for step in range(1, digit[0]):
                got = send(packed, size, digit, step)
                blocks = blocks + [
                    got[k * shard_rows : (k + 1) * shard_rows] for k in range(count)
                ]
        return blocks

    def spread_near(blocks):
        halves = []
        for half, digit in enumerate(NEAR):
            packed = jnp.concatenate(blocks[half * cut : (half + 1) * cut], axis=0)
            halves.append((packed, send(packed, size, digit, 1)))
        return halves

    def spread_last(halves):
        here, there = [], []
        for half, pair in enumerate(halves):
            packed = jnp.concatenate(pair, axis=0)
            here.append(packed)
            there.append(send(packed, size, NEAR[1 - half], 1))
        return here, there

    def in_order(here, there):
        return [p for pair in zip(here, there) for p in pair]

    def halved(parts):
        middle = parts[0].shape[0] // 2
        sums = []
        for at in (slice(0, middle), slice(middle, None)):
            total = parts[0][at].astype(F32)
            for part in parts[1:]:
                total = total + part[at].astype(F32)
            sums.append(total.astype(BF))
        return sums

    def sum_first(pieces):
        return [
            (pieces[2 * half], send(pieces[2 * half + 1], size, NEAR[1 - half], 1))
            for half in range(2)
        ]

    def sum_second(*sums):
        done = []
        for half in range(2):
            both = zip(*[halved(halves[half]) for halves in sums])
            stay, leave_ = (jnp.concatenate(parts, axis=1) for parts in both)
            done.append((stay, send(leave_, size, NEAR[half], 1)))
        return done

    def sum_far(halves):
        blocks = []
        for stay, came in halves:
            for k in range(cut):
                here = slice(k * shard_rows, (k + 1) * shard_rows)
                blocks.append((stay[here].astype(F32) + came[here].astype(F32)).astype(BF))
        for digit in far[:0:-1]:
            blocks = [add_up(terms).astype(BF) for terms in spread_fold(blocks, digit)]
        return spread_fold(blocks, far[0])[0]

    def spread_fold(blocks, digit):
        radix = digit[0]
        inner = len(blocks) // radix
        terms = [[block] for block in blocks[:inner]]
        for step in range(1, radix):
            group = blocks[step * inner : (step + 1) * inner]
            packed = group[0] if inner == 1 else jnp.concatenate(group, axis=0)
            got = send(packed, size, digit, radix - step)
            for k in range(inner):
                terms[k].append(got[k * shard_rows : (k + 1) * shard_rows])
        return terms

    def add_up(terms):
        total = terms[0].astype(F32)
        for term in terms[1:]:
            total = total + term.astype(F32)
        return total

    pad = -(slot_count + 1) % 128
    packed_ids = jnp.concatenate(
        [replace_ids, masked_count[:, None], jnp.zeros((page_count, pad), jnp.int32)], axis=1
    )
    packed_ids = jnp.broadcast_to(packed_ids[None], (size, *packed_ids.shape))
    heads_shard = jnp.concatenate(
        [qkv_weight.reshape(shard_rows, 3 * head_cols), out_weight.T], axis=1
    )
    heads_far = spread_far(heads_shard)

    places = jnp.stack([me, core])
    used = jnp.arange(slot_count)[None, :] < masked_count[:, None]
    codes = jnp.where(used, replace_ids, -1)
    own_codes = own_pages(codes).reshape(1, own_slots)
    held_rows = held_order(size, shard_rows, me)[None, :]
    vectors = jnp.stack(
        [out_bias, norm1_gain, norm1_bias, down_bias, norm2_gain, norm2_bias] + [out_bias] * 2
    )
    turn, turned_tokens, grad_final, vectors, sent_hot = prepare(
        tokens,
        cotangent.reshape(slots, width),
        vectors,
        held_rows,
        codes,
        own_codes,
        size,
        table_rows,
    )
    packed_ids, turned_tokens, sent_hot, heads_far, in_shard = together(
        packed_ids, turned_tokens, sent_hot, heads_far, in_weight
    )

    all_ids = lax.all_to_all(packed_ids, "dp", 0, 0)
    heads_near = spread_near(heads_far)
    in_far = spread_far(in_shard)
    down_shard = down_weight.T
    hidden_bias = in_bias[None]
    all_ids, heads_near, in_far, down_shard = together(all_ids, heads_near, in_far, down_shard)

    is_used = jnp.arange(slot_count)[None, None, :] < all_ids[:, :, slot_count : slot_count + 1]
    all_codes = jnp.where(is_used, all_ids[:, :, :slot_count], -1)
    all_codes = all_codes.reshape(size * cores, own_slots)
    *hots, found, fullest = serve(places, all_codes, embed_table, size, cores)
    found = lax.all_to_all(found.reshape(size, ROOM, width), "dp", 0, 0)
    found = found.reshape(size * ROOM, width)
    heads_here, heads_there = spread_last(heads_near)
    down_far = spread_far(down_shard)
    in_near = spread_near(in_far)
    found, fullest, hots, heads_here, heads_there, down_far, in_near = together(
        found, fullest, hots, heads_here, heads_there, down_far, in_near
    )

    rounds = (fullest.reshape(()) + ROOM - 1) // ROOM

    def round_of(turn_, held):
        own, every, held = lax.optimization_barrier((own_codes[0], all_codes, held))
        low = turn_ * ROOM
        spots = jnp.arange(own_slots)
        before = (spots[:, None] < spots[None, :]).astype(BF)
        to_owner = (own >= 0)[:, None] & (own[:, None] // table_rows == jnp.arange(size))
        rank = tn(before, to_owner.astype(BF)).astype(jnp.int32) - low
        sent = (rank[:, :, None] == jnp.arange(ROOM)) & to_owner[:, :, None]
        sent = sent.astype(BF).reshape(own_slots, size * ROOM)
        mine = (every >= 0) & (every // table_rows == me)
        rank = dot(mine.astype(BF), before).astype(jnp.int32) - low
        hit = (rank[:, None, :] == jnp.arange(ROOM)[None, :, None]) & mine[:, None, :]
        asked = jnp.sum(jnp.where(hit, every[:, None, :] - me * table_rows + 1, 0), axis=2) - 1
        hot = (asked[:, :, None] == jnp.arange(table_rows)).astype(BF)
        hot = hot.reshape(size, cores, ROOM, table_rows)
        turned = [
            lax.dynamic_index_in_dim(hot, (core + cores - k) % cores, 1, keepdims=False)
            for k in range(cores)
        ]
        return sent, [t.reshape(size * ROOM, table_rows) for t in turned], held

    def more_rows(turn_, held):
        sent, later, held = round_of(turn_, held)
        got = dot(later[0], embed_table).astype(BF).reshape(size, ROOM, width)
        got = lax.all_to_all(got, "dp", 0, 0).reshape(size * ROOM, width)
        return held + dot(sent, got)

    new_rows = lax.fori_loop(1, rounds, more_rows, dot(sent_hot, found))
    new_rows = in_core_order(from_cores(new_rows.astype(BF)))

    heads_pieces = in_order(heads_here, heads_there)
    embedded, low, query, key, value, s_embedded, s_low, s_query, s_attended, s_part = enter(
        turned_tokens, new_rows, turn, masked_pos, qv_bias, heads_pieces
    )
    down_near = spread_near(down_far)
    in_here, in_there = spread_last(in_near)
    s_part, down_near, in_here, in_there, query = together(
        s_part, down_near, in_here, in_there, query
    )

    down_here, down_there = spread_last(down_near)
    s_parts = from_cores(s_part)
    rows_part = attend_all(query, key, value, heads_pieces, pages)
    s_parts, down_here, down_there, rows_part = together(
        s_parts, down_here, down_there, rows_part
    )

    in_pieces, down_pieces = in_order(in_here, in_there), in_order(down_here, down_there)
    unit1, scale1, middle_low, hidden, slope, s_part = slot_forward(
        s_parts, s_embedded, vectors, hidden_bias, in_pieces, down_pieces
    )
    s_parts = from_cores(s_part)
    *grads, grad_r2, small2, grad_in_bias, s_part = slot_turn(
        s_parts, hidden, slope, unit1, middle_low, grad_final, vectors, in_pieces, down_pieces
    )
    s_part, *grads = together(s_part, *grads)

    s_parts = from_cores(s_part)
    rows_parts = from_cores(rows_part)
    down_sum = sum_first(grads[: len(down_pieces)])
    in_sum = sum_first(grads[len(down_pieces) :])
    *grad_heads, grad_r1, part, small1, small0 = slot_back(
        s_parts,
        grad_r2,
        unit1,
        scale1,
        s_attended,
        s_query,
        key,
        value,
        s_low,
        low,
        vectors,
        masked_pos,
        heads_pieces,
    )
    down_sum, in_sum, grad_heads, part, rows_parts = together(
        down_sum, in_sum, grad_heads, part, rows_parts
    )

    heads_sum = sum_first(grad_heads)
    units_sum = sum_second(down_sum, in_sum)
    grad_input, moved, own_grad = leave(
        places,
        from_cores(part),
        grad_r1,
        masked_pos,
        turn,
        held_rows,
        sent_hot,
        [small1, small2, small0, grad_in_bias],
        size,
    )
    middle, rows_part = rows_forward(
        rows_parts, embedded, vectors, hidden_bias, in_pieces, down_pieces
    )
    units_sum, heads_sum, grad_input, moved, rows_part = together(
        units_sum, heads_sum, grad_input, moved, rows_part
    )

    gots = lax.all_to_all(moved, "dp", 0, 0)
    units_sum = sum_far(units_sum)
    heads_sum = sum_second(heads_sum)
    output = rows_end(from_cores(rows_part), middle, vectors, turn)
    units_sum, heads_sum, output, gots = together(units_sum, heads_sum, output, gots)

    heads_sum = sum_far(heads_sum)
    grad_table, totals = collect(hots, from_cores(gots))
    units_share = add_up(units_sum)
    down_share, in_share = units_share[:, :hidden_cols].T, units_share[:, hidden_cols:]
    def more_table(turn_, held):
        sent, later, held = round_of(turn_, held)
        got = tn(sent, own_grad).astype(BF).reshape(size, ROOM, width)
        for hot, block in zip(later, from_cores(lax.all_to_all(got, "dp", 0, 0))):
            held = held + tn(hot, block.reshape(size * ROOM, width))
        return held

    grad_table = lax.fori_loop(1, rounds, more_table, grad_table)
    def piece(row, block, count):
        return totals[row, block * 128 : block * 128 + count]

    vec = [piece(0, k, shard_rows) for k in range(6)]
    own = [
        piece(1, 0, head_cols // size),
        piece(1, 1, head_cols // size),
        piece(1, 2, hidden_cols // size),
    ]
    heads_sum, in_share, down_share, grad_table, vec, own = together(
        heads_sum, in_share, down_share, grad_table, vec, own
    )
    heads_share = add_up(heads_sum)
    qkv_share = heads_share[:, : 3 * head_cols].reshape(shard_rows, 3, head_cols)
    out_share = heads_share[:, 3 * head_cols :].T


    return (
        output,
        grad_input,
        grad_table,
        qkv_share,
        jnp.stack([own[0], own[1]])[:, None, :],
        out_share,
        vec[0],
        vec[1],
        vec[2],
        in_share,
        own[2][None],
        down_share,
        vec[3],
        vec[4],
        vec[5],
    )


def solution(mesh):
    in_specs = (
        P("dp", None),
        P("dp", None),
        P("dp", None, "mp"),
        P(None, "mp"),
        P("mp", "dp"),
        P(),
        P(),
        P(),
        P("dp", "mp"),
        P("mp"),
        P("mp", "dp"),
        P(),
        P(),
        P(),
        P("dp", None),
        P("dp", None),
        P("dp"),
        P("dp", None, None),
    )
    out_specs = (
        P("dp", None),
        P("dp", None),
        P("dp", None),
        P("dp", None, "mp"),
        P(None, "mp", "dp"),
        P("mp", "dp"),
        P("dp"),
        P("dp"),
        P("dp"),
        P("dp", "mp"),
        P("mp", "dp"),
        P("mp", "dp"),
        P("dp"),
        P("dp"),
        P("dp"),
    )
    return jax.shard_map(
        per_device, mesh=mesh, in_specs=in_specs, out_specs=out_specs, check_vma=False
    )
```

```python
import jax
import jax.numpy as jnp
import numpy as np
from jax import lax
from jax.experimental import pallas as pl
from jax.experimental.pallas import tpu as pltpu
from jax.sharding import PartitionSpec as P

HEAD = 64
EPSILON = 1e-05
ROOM = 16
EXTRA = 8

BF = jnp.bfloat16
F32 = jnp.float32


def dot(a, b, dims=((1,), (0,)), **kw):
    return lax.dot_general(a, b, (dims, ((), ())), preferred_element_type=F32, **kw)


def nt(a, b):
    return dot(a, b, ((1,), (1,)))


def tn(a, b):
    return dot(a, b, ((0,), (0,)))


def split_two(values):
    high = values.astype(BF)
    return high, (values - high.astype(F32)).astype(BF)


def far_digits(size):
    found = []
    stride, rest = 4, size // 4
    while rest > 1:
        radix = next(r for r in (4, 2, 3, 5, 7, rest) if rest % r == 0)
        found.append((radix, stride))
        stride, rest = stride * radix, rest // radix
    return found


NEAR = ((2, 1), (2, 2))


def shift(size, digit, step):
    radix, stride = digit
    pairs = []
    for src in range(size):
        own = (src // stride) % radix
        pairs.append((src, src + ((own + step) % radix - own) * stride))
    return pairs


def send(values, size, digit, step):
    return lax.ppermute(values, "dp", shift(size, digit, step))


def held_order(size, rows, me):
    blocks = size // 8
    place = jnp.arange(size * rows)
    second = place >= size * rows // 2
    slot, row = (place % (size * rows // 2)) // rows, place % rows
    block = slot % blocks + jnp.where(second, blocks, 0)
    low, high = (slot // blocks) % 2, slot // blocks // 2
    owner = jnp.zeros_like(place)
    for radix, stride in far_digits(size):
        owner = owner + ((me // stride - block % radix) % radix) * stride
        block = block // radix
    x_step, y_step = jnp.where(second, high, low), jnp.where(second, low, high)
    owner = owner + (me - x_step) % 2 + ((me // 2 - y_step) % 2) * 2
    return owner * rows + row


VMEM_LIMIT = 20 * 1024 * 1024


def kernel_call(body, outs, inputs, far_count=0, scratch=(), flops=0, grid=None, specs=None):
    near = len(inputs) - far_count
    in_specs, out_specs = specs or (
        [pl.BlockSpec(memory_space=pltpu.VMEM)] * near,
        [pl.BlockSpec(memory_space=pltpu.VMEM)] * len(outs),
    )
    return pl.pallas_call(
        body,
        grid=grid or (),
        out_shape=outs,
        in_specs=[*in_specs, *([pl.BlockSpec(memory_space=pl.ANY)] * far_count)],
        out_specs=out_specs,
        scratch_shapes=scratch,
        compiler_params=pltpu.CompilerParams(vmem_limit_bytes=VMEM_LIMIT),
        cost_estimate=pl.CostEstimate(flops=1, bytes_accessed=1, transcendentals=0),
    )(*inputs)


def shape(rows, cols, dtype):
    return jax.ShapeDtypeStruct((rows, cols), dtype)


def fill(pieces, held, sems, start=0):
    copies, at = [], 0
    for i, piece in enumerate(pieces):
        rows = piece.shape[0]
        source = piece.at[:, pl.ds(start, held.shape[1])]
        copy = pltpu.make_async_copy(source, held.at[pl.ds(at, rows)], sems.at[i])
        copy.start()
        copies.append(copy)
        at += rows

    def wait():
        for copy in copies:
            copy.wait()

    return wait


def held_scratch(pieces, cols=None):
    rows = sum(p.shape[0] for p in pieces)
    return [
        pltpu.VMEM((rows, cols or pieces[0].shape[1]), BF),
        pltpu.SemaphoreType.DMA((len(pieces),)),
    ]


def norm_stats(values):
    row_mean = jnp.mean(values, axis=-1, keepdims=True)
    centered = values - row_mean
    scale = lax.rsqrt(jnp.mean(centered * centered, axis=-1, keepdims=True) + EPSILON)
    return centered * scale, scale


def norm_back(grad, unit, scale, gain):
    inner = grad * gain
    mean_inner = jnp.mean(inner, axis=-1, keepdims=True)
    mean_unit = jnp.mean(inner * unit, axis=-1, keepdims=True)
    return (
        scale * (inner - mean_inner - unit * mean_unit),
        jnp.sum(grad * unit, axis=0, keepdims=True),
        jnp.sum(grad, axis=0, keepdims=True),
    )


def gelu(values):
    return values * (0.5 + 0.5 * lax.erf(values * (0.5**0.5)))


def gelu_both(values):
    normal = 0.5 + 0.5 * lax.erf(values * (0.5**0.5))
    bell = jnp.exp(-0.5 * values * values) * (0.5 / np.pi) ** 0.5
    return values * normal, normal + values * bell


def head_masks(dtype):
    lane = lax.broadcasted_iota(jnp.int32, (1, 2 * HEAD), 1)
    return [(lane // HEAD == h).astype(dtype) for h in range(2)]


def attend_pair(query, key, value):
    lanes = value.shape[1]
    wider = jnp.concatenate([value, jnp.ones_like(value)], axis=1)
    outs = []
    for mask in head_masks(BF):
        scores = nt(query * mask, key)
        powers = jnp.exp(scores - jnp.max(scores, axis=-1, keepdims=True))
        both = dot(powers.astype(BF), wider)
        outs.append(both[:, :lanes] / both[:, lanes:])
    first, second = head_masks(F32)
    return (outs[0] * first + outs[1] * second).astype(BF)


def one_hot_rows(row_of_line, rows):
    at = lax.broadcasted_iota(jnp.int32, (rows, row_of_line.shape[1]), 0)
    return (at == row_of_line).astype(F32).astype(BF)


def one_hot_slots(row_of_column, rows):
    at = lax.broadcasted_iota(jnp.int32, (row_of_column.shape[0], rows), 1)
    return (at == row_of_column).astype(F32).astype(BF)


def as_column(line):
    count = line.shape[1]
    square = (count, count)
    same = lax.broadcasted_iota(jnp.int32, square, 0) == lax.broadcasted_iota(jnp.int32, square, 1)
    return jnp.sum(jnp.where(same, line.astype(F32), 0.0), axis=1, keepdims=True)


def floor_by(values, divisor):
    return jnp.floor((values + 0.5) * (1.0 / divisor))


def iota(dims, axis):
    return lax.broadcasted_iota(jnp.int32, dims, axis).astype(F32)


def serve(places, codes, table, size, cores):
    table_rows, width = table.shape
    devices, slots = codes.shape
    count = size * ROOM

    def body(place, code, tab, *outs):
        *hots, found, most = outs
        me, core = place[0], place[1]
        line = code[...].astype(F32)
        local = line - (me * table_rows).astype(F32)
        mine = (local >= 0) & (local < table_rows)
        before = (iota((slots, slots), 0) < iota((slots, slots), 1)).astype(BF)
        rank = dot(mine.astype(F32).astype(BF), before)
        rank = jnp.where(mine & (rank < ROOM), rank, 255.0).astype(BF)
        local = jnp.where(mine, local, 0.0)
        local_high = floor_by(local, 256)
        local_low = (local - 256 * local_high).astype(BF)
        local_high = local_high.astype(BF)
        source = floor_by(iota((count, 1), 0), ROOM)
        room = iota((count, 1), 0) - ROOM * source
        for k in range(cores):
            which = lax.rem(core + cores - k, cores).astype(F32)
            pick = (iota((count, devices), 1) == source * cores + which).astype(F32).astype(BF)
            hit = dot(pick, rank) == room
            at = 256 * dot(pick, local_high) + dot(pick, local_low) + 1.0
            asked = jnp.sum(jnp.where(hit, at, 0.0), axis=1, keepdims=True) - 1.0
            hots[k][...] = (iota((count, table_rows), 1) == asked).astype(F32).astype(BF)
        found[...] = dot(hots[0][...], tab[...]).astype(BF)
        owner = floor_by(line, table_rows)
        fullest = jnp.zeros((devices, 1), F32)
        for o in range(size):
            here = jnp.sum(jnp.where(owner == o, 1.0, 0.0), axis=1, keepdims=True)
            fullest = jnp.maximum(fullest, here)
        fullest = jnp.max(fullest, axis=0, keepdims=True)
        most[...] = fullest.astype(jnp.int32)

    smem, vmem = pl.BlockSpec(memory_space=pltpu.SMEM), pl.BlockSpec(memory_space=pltpu.VMEM)
    return kernel_call(
        body,
        [
            *[shape(count, table_rows, BF)] * cores,
            shape(count, width, BF),
            shape(1, 1, jnp.int32),
        ],
        [places, codes, table],
        flops=2 * count * table_rows * width,
        specs=([smem, vmem, vmem], [vmem] * (cores + 2)),
    )


def by_owner(values, owner, place, size):
    count = values.shape[1]
    hit = (iota((size, count), 0) == owner).astype(F32)
    rows = jnp.concatenate([hit * values[r : r + 1] for r in range(values.shape[0])], axis=0)
    hot = (iota((128, count), 0) == place).astype(F32).astype(BF)
    total, rest = 0.0, rows
    for _ in range(3):
        high = rest.astype(BF)
        rest = rest - high.astype(F32)
        total = total + nt(high, hot)
    return total


def stack_rows(groups):
    if any(part.shape[0] % 16 for group in groups for part in group):
        return [jnp.concatenate(group, axis=0) for group in groups]

    def body(*refs):
        at = 0
        for out, group in zip(refs[len(refs) - len(groups) :], groups):
            start = 0
            for part in group:
                out[start : start + part.shape[0]] = refs[at][...]
                start, at = start + part.shape[0], at + 1

    outs = [shape(sum(p.shape[0] for p in group), group[0].shape[1], BF) for group in groups]
    return kernel_call(body, outs, [part for group in groups for part in group])


def prepare(tokens, order, codes, size, table_rows):
    rows, width = tokens.shape
    slots = codes.shape[1]

    def body(tok, order_, code, turn, tok_out, sent):
        turn[...] = (
            (lax.broadcasted_iota(jnp.int32, (width, width), 0) == order_[...])
            .astype(F32)
            .astype(BF)
        )
        line = code[...].astype(F32)
        column = as_column(line)
        owner_line, owner = floor_by(line, table_rows), floor_by(column, table_rows)
        square = (slots, slots)
        earlier = (iota(square, 1) < iota(square, 0)) & (owner_line == owner)
        rank = jnp.sum(jnp.where(earlier, 1.0, 0.0), axis=1, keepdims=True)
        target = jnp.where((column >= 0) & (rank < ROOM), owner * ROOM + rank, -1.0)
        sent[...] = (iota((slots, size * ROOM), 1) == target).astype(F32).astype(BF)
        tok_out[...] = dot(tok[...], turn[...]).astype(BF)

    return kernel_call(
        body,
        [shape(width, width, BF), shape(rows, width, BF), shape(slots, size * ROOM, BF)],
        [tokens, order, codes],
    )


def turn_small(cotangent, codes, vectors, turn):
    slots, width = cotangent.shape

    def body(cot, code, vec, turn_, cot_out, vec_out):
        pages, per = code.shape
        for g in range(pages):
            here = slice(g * per, (g + 1) * per)
            used = (as_column(code[g : g + 1]) >= 0).astype(F32).astype(BF)
            cot_out[here] = dot(cot[here] * used, turn_[...]).astype(BF)
        rest, total = vec[...], 0.0
        for _ in range(3):
            high = rest.astype(BF)
            rest = rest - high.astype(F32)
            total = total + dot(high, turn_[...])
        vec_out[...] = total

    return kernel_call(
        body,
        [shape(slots, width, BF), shape(vectors.shape[0], width, F32)],
        [cotangent, codes, vectors, turn],
    )


def enter(places, tokens, founds, sents, more, turn, pos, qv_bias, pieces):
    rows, width = tokens.shape
    pages, per = pos.shape
    slots, cores = pages * per, len(founds)
    own = sents[0].shape[0]
    near = 6 + 2 * cores
    cols = qv_bias.shape[1]
    length = rows // pages

    def body(*refs):
        place_, tok, more_, turn_, pos_, bias_ = refs[:6]
        found, sent = refs[6 : 6 + cores], refs[6 + cores : near]
        piece_refs = refs[near : near + len(pieces)]
        (
            emb,
            low,
            q,
            k,
            v,
            s_emb,
            s_low,
            s_q,
            s_att,
            s_out,
            fetched,
            held,
            sems,
        ) = refs[near + len(pieces) :]
        wait = fill(piece_refs, held, sems)
        for c in range(cores):
            start = pl.multiple_of(lax.rem(place_[1] + cores - c, cores) * own, own)
            fetched[pl.ds(start, own)] = dot(sent[c][...], found[c][...])
        fetched[...] += more_[...]
        new = dot(fetched[...].astype(BF), turn_[...]).astype(BF)
        hots = []
        for g in range(pages):
            page, here = slice(g * length, (g + 1) * length), slice(g * per, (g + 1) * per)
            placed = one_hot_rows(pos_[g : g + 1], length)
            hot = one_hot_slots(as_column(pos_[g : g + 1]), length)
            hots.append(hot)
            exact = tok[page].astype(F32) + dot(placed, new[here])
            emb[page] = exact
            low[page] = exact.astype(BF)
            s_emb[here] = dot(hot, tok[page]) + new[here].astype(F32)
        s_low[...] = s_emb[...].astype(BF)
        wait()
        for g in range(pages):
            page, here = slice(g * length, (g + 1) * length), slice(g * per, (g + 1) * per)
            q[page] = (dot(low[page], held[:, :cols]) + bias_[0:1]).astype(BF)
            k[page] = dot(low[page], held[:, cols : 2 * cols]).astype(BF)
            v[page] = (dot(low[page], held[:, 2 * cols : 3 * cols]) + bias_[1:2]).astype(BF)
            s_q[here] = dot(hots[g], q[page]).astype(BF)
            for j in range(0, cols, 2 * HEAD):
                at = slice(j, j + 2 * HEAD)
                s_att[here, at] = attend_pair(s_q[here, at] * HEAD**-0.5, k[page, at], v[page, at])
        s_out[...] = nt(s_att[...], held[:, 3 * cols :])

    outs = [
        shape(rows, width, F32),
        shape(rows, width, BF),
        *[shape(rows, cols, BF)] * 3,
        shape(slots, width, F32),
        shape(slots, width, BF),
        *[shape(slots, cols, BF)] * 2,
        shape(slots, width, F32),
    ]
    return kernel_call(
        body,
        outs,
        [places, tokens, more, turn, pos, qv_bias, *founds, *sents, *pieces],
        len(pieces),
        [pltpu.VMEM((slots, width), F32), *held_scratch(pieces)],
        specs=(
            [
                pl.BlockSpec(memory_space=pltpu.SMEM),
                *([pl.BlockSpec(memory_space=pltpu.VMEM)] * (near - 1)),
            ],
            [pl.BlockSpec(memory_space=pltpu.VMEM)] * len(outs),
        ),
    )


def attend_all(query, key, value, pieces, pages):
    rows, cols = query.shape
    length, pairs = rows // pages, cols // (2 * HEAD)
    width = sum(p.shape[0] for p in pieces)

    def body(q, k, v, *refs):
        out, total, held, sems = refs[len(pieces) :]
        first, pair = pl.program_id(0) == 0, pl.program_id(1)

        @pl.when(first & (pair == 0))
        def _():
            fill(refs[: len(pieces)], held, sems, 3 * cols)()

        half = length // 2
        for part in range(2):
            here = slice(part * half, (part + 1) * half)
            attended = attend_pair(q[here] * HEAD**-0.5, k[...], v[...])
            at = pl.ds(pl.multiple_of(pair * 2 * HEAD, 2 * HEAD), 2 * HEAD)
            total[here, at] = attended

        @pl.when(pair == pairs - 1)
        def _():
            out[...] = nt(total[...], held[...]).astype(BF)

    spec = pl.BlockSpec((length, 2 * HEAD), lambda g, j: (g, j))
    return kernel_call(
        body,
        [shape(rows, width, BF)],
        [query, key, value, *pieces],
        len(pieces),
        [pltpu.VMEM((length, cols), BF), *held_scratch(pieces, cols)],
        grid=(pages, pairs),
        specs=([spec] * 3, [pl.BlockSpec((length, width), lambda g, j: (g, 0))]),
    )[0]


def slot_forward(parts, embedded, vectors, bias, in_pieces, down_pieces):
    slots, width = embedded.shape
    wide = in_pieces[0].shape[1]
    count, total_count = len(in_pieces), len(in_pieces) + len(down_pieces)

    def body(first, second, emb, vec, bias_, *refs):
        unit1, scale1, mid_low, hid, slope, part, held, sems, held2, sems2 = refs[total_count:]
        wait = fill(refs[:count], held, sems)
        wait2 = fill(refs[count:total_count], held2, sems2)
        unit, scale = norm_stats(emb[...] + vec[0:1] + (first[...] + second[...]))
        unit1[...] = unit
        scale1[...] = jnp.broadcast_to(scale, scale1.shape)
        mid_low[...] = (unit * vec[1:2] + vec[2:3]).astype(BF)
        wait()
        value, rate = gelu_both(dot(mid_low[...], held[...]) + bias_[...])
        hid[...] = value.astype(BF)
        slope[...] = rate
        wait2()
        part[...] = nt(hid[...], held2[...])

    outs = [
        shape(slots, width, F32),
        shape(slots, 128, F32),
        shape(slots, width, BF),
        shape(slots, wide, BF),
        shape(slots, wide, F32),
        shape(slots, width, F32),
    ]
    return kernel_call(
        body,
        outs,
        [*parts, embedded, vectors, bias, *in_pieces, *down_pieces],
        total_count,
        [*held_scratch(in_pieces), *held_scratch(down_pieces)],
    )


def put_rows(outs, start, values):
    at = 0
    for out in outs:
        rows = out.shape[0]
        out[:, start : start + values.shape[1]] = values[at : at + rows].astype(BF)
        at += rows


def slot_turn(parts, hidden, slope, unit1, grad_final, vectors, in_pieces, down_pieces):
    slots, width = unit1.shape
    wide = hidden.shape[1]
    count, total_count = len(in_pieces), len(in_pieces) + len(down_pieces)

    def body(first, second, hid, slp, un1, final, vec, *refs):
        (*grads, grad2, ghin, small, in_small, mid, held, sems, held2, sems2) = refs[total_count:]
        wait = fill(refs[:count], held, sems)
        wait2 = fill(refs[count:total_count], held2, sems2)
        total = un1[...] * vec[1:2] + vec[2:3] + vec[3:4] + (first[...] + second[...])
        unit, scale = norm_stats(total)
        grad, gain, bias = norm_back(final[...].astype(F32), unit, scale, vec[4:5])
        grad2[...] = grad
        grad_low = grad.astype(BF)
        small[0:1] = jnp.sum(grad_low.astype(F32), axis=0, keepdims=True)
        small[1:2] = gain
        small[2:3] = bias
        small[3:8] = jnp.zeros((5, width), F32)
        wait2()
        back = (dot(grad_low, held2[...]) * slp[...]).astype(BF)
        ghin[...] = back
        in_small[...] = jnp.sum(back.astype(F32), axis=0, keepdims=True)
        wait()
        mid[...] = nt(back, held[...])
        put_rows(grads, 0, tn(grad_low, hid[...]))

    outs = [
        *[shape(p.shape[0], wide, BF) for p in in_pieces],
        shape(slots, width, F32),
        shape(slots, wide, BF),
        shape(8, width, F32),
        shape(1, wide, F32),
        shape(slots, width, F32),
    ]
    return kernel_call(
        body,
        outs,
        [*parts, hidden, slope, unit1, grad_final, vectors, *in_pieces, *down_pieces],
        total_count,
        [*held_scratch(in_pieces), *held_scratch(down_pieces)],
    )


def in_grad(mid_low, ghin, heights):
    def body(mid, gh, *grads):
        put_rows(grads, 0, tn(mid[...], gh[...]))

    return kernel_call(body, [shape(r, ghin.shape[1], BF) for r in heights], [mid_low, ghin])


def slot_back(parts, grad2, unit1, scale1, attended, s_query, key, value, s_low, low, vectors, pos, pieces):
    slots, width = unit1.shape
    rows, cols = key.shape
    pages, per = pos.shape
    length = rows // pages
    scale = HEAD**-0.5

    def body(first, second, g2, un1, sc1, att, sq, k, v, sl, lo, vec, pos_, *refs):
        (*grads, grad1, part, small, small_heads, gq, gk, gv, held, sems) = refs[len(pieces) :]
        wait = fill(refs[: len(pieces)], held, sems)
        total = g2[...] + (first[...] + second[...])
        grad, gain, bias = norm_back(total, un1[...], sc1[:, :1], vec[1:2])
        grad1[...] = grad
        grad_low = grad.astype(BF)
        small[0:1] = jnp.sum(grad_low.astype(F32), axis=0, keepdims=True)
        small[1:2] = gain
        small[2:3] = bias
        small[3:8] = jnp.zeros((5, width), F32)
        put_rows(grads, 3 * cols, tn(grad_low, att[...]))
        wait()
        gatt = dot(grad_low, held[:, 3 * cols :]).astype(BF)
        masks = head_masks(BF)
        left_lanes, right_lanes = head_masks(F32)
        for g in range(pages):
            here, page = slice(g * per, (g + 1) * per), slice(g * length, (g + 1) * length)
            for j in range(0, cols, 2 * HEAD):
                at = slice(j, j + 2 * HEAD)
                query, back = sq[here, at], gatt[here, at]
                keys, values = k[page, at], v[page, at]
                got = []
                for mask in masks:
                    scores = nt(query * mask * scale, keys)
                    powers = jnp.exp(scores - jnp.max(scores, axis=-1, keepdims=True))
                    prob = powers * (1.0 / jnp.sum(powers, axis=-1, keepdims=True))
                    grad_prob = nt(back * mask, values)
                    inner = jnp.sum(prob * grad_prob, axis=-1, keepdims=True)
                    grad_scores = (prob * (grad_prob - inner)).astype(BF)
                    got.append(
                        (
                            dot(grad_scores, keys),
                            tn(grad_scores, query),
                            tn(prob.astype(BF), back),
                        )
                    )
                left, right = got
                gq[here, at] = ((left[0] * left_lanes + right[0] * right_lanes) * scale).astype(BF)
                gk[page, at] = ((left[1] * left_lanes + right[1] * right_lanes) * scale).astype(BF)
                gv[page, at] = (left[2] * left_lanes + right[2] * right_lanes).astype(BF)
        small_heads[0:1] = jnp.sum(gq[...].astype(F32), axis=0, keepdims=True)
        small_heads[1:2] = jnp.sum(gv[...].astype(F32), axis=0, keepdims=True)
        small_heads[2:8] = jnp.zeros((6, cols), F32)
        put_rows(grads, 0, tn(sl[...], gq[...]))
        put_rows(grads, cols, tn(lo[...], gk[...]))
        put_rows(grads, 2 * cols, tn(lo[...], gv[...]))
        high, rest = split_two(nt(gq[...], held[:, :cols]))
        for g in range(pages):
            here, page = slice(g * per, (g + 1) * per), slice(g * length, (g + 1) * length)
            placed = one_hot_rows(pos_[g : g + 1], length)
            total = nt(gk[page], held[:, cols : 2 * cols]) + nt(gv[page], held[:, 2 * cols : 3 * cols])
            total = total + dot(placed, high[here]) + dot(placed, rest[here])
            part[page] = total.astype(BF)

    outs = [
        *[shape(p.shape[0], 4 * cols, BF) for p in pieces],
        shape(slots, width, F32),
        shape(rows, width, BF),
        shape(8, width, F32),
        shape(8, cols, F32),
    ]
    return kernel_call(
        body,
        outs,
        [*parts, grad2, unit1, scale1, attended, s_query, key, value, s_low, low, vectors, pos, *pieces],
        len(pieces),
        [
            pltpu.VMEM((slots, cols), BF),
            *[pltpu.VMEM((rows, cols), BF)] * 2,
            *held_scratch(pieces),
        ],
    )


def leave(places, parts, grad1, pos, turn, order, sent_hot, smalls, size):
    rows, width = parts[0].shape
    pages, per = pos.shape
    length = rows // pages
    own = sent_hot.shape[0] // per
    cols, wide = smalls[2].shape[1], smalls[3].shape[1]

    def body(place_, first, second, g1, pos_, turn_, order_, hot, sm1, sm2, smq, smh, out, moved, mine):
        high, low = split_two(g1[...])
        for g in range(pages):
            page, here = slice(g * length, (g + 1) * length), slice(g * per, (g + 1) * per)
            placed = one_hot_rows(pos_[g : g + 1], length)
            total = first[page].astype(F32) + second[page].astype(F32)
            total = total + dot(placed, high[here]) + dot(placed, low[here])
            near, rest = split_two(total)
            out[page] = nt(near, turn_[...]) + nt(rest, turn_[...])

        place = order_[...].astype(F32)
        owner = floor_by(place, width // size)
        vec = jnp.concatenate([sm1[0:3], sm2[0:3]], axis=0)
        vec = by_owner(vec, owner, place - owner * (width // size), size)
        vec = jnp.concatenate([vec[r * size : (r + 1) * size] for r in range(6)], axis=1)
        at = iota((1, cols), 1)
        owner = floor_by(at, cols // size)
        head = by_owner(smq[0:2], owner, at - owner * (cols // size), size)
        at = iota((1, wide), 1)
        owner = floor_by(at, wide // size)
        unit = by_owner(smh[...], owner, at - owner * (wide // size), size)
        others = jnp.concatenate([head[:size], head[size:], unit], axis=1)
        filler = jnp.zeros((size, width - others.shape[1]), F32)
        others = jnp.concatenate([others, filler], axis=1)
        tails = [p.astype(F32) for values in (vec, others) for p in split_two(values)]
        going = 0.0
        for i in range(own):
            page = place_[1] * own + i
            slot_hot = one_hot_slots(as_column(pos_[pl.ds(page, 1)]), length)
            here = out[pl.ds(pl.multiple_of(page * length, length), length)]
            picked = dot(slot_hot, here.astype(BF)).astype(BF)
            mine[i * per : (i + 1) * per] = picked
            going = going + tn(hot[i * per : (i + 1) * per], picked)
        for s in range(size):
            moved[s, :ROOM] = going[s * ROOM : (s + 1) * ROOM].astype(BF)
            tail = [t[s : s + 1] for t in tails] + [jnp.zeros((EXTRA - len(tails), width), F32)]
            moved[s, ROOM:] = jnp.concatenate(tail, axis=0).astype(BF)

    return kernel_call(
        body,
        [
            shape(rows, width, F32),
            jax.ShapeDtypeStruct((size, ROOM + EXTRA, width), BF),
            shape(own * per, width, BF),
        ],
        [places, *parts, grad1, pos, turn, order, sent_hot, *smalls],
        specs=(
            [
                pl.BlockSpec(memory_space=pltpu.SMEM),
                *([pl.BlockSpec(memory_space=pltpu.VMEM)] * 11),
            ],
            [pl.BlockSpec(memory_space=pltpu.VMEM)] * 3,
        ),
    )


def collect(hots, gots):
    cores, (count, table_rows) = len(hots), hots[0].shape
    size, held, width = gots[0].shape

    def body(*refs):
        hot, got = refs[:cores], refs[cores : 2 * cores]
        table, sums = refs[2 * cores :]
        value = 0.0
        for k in range(cores):
            rows = jnp.concatenate([got[k][s, :ROOM] for s in range(size)], axis=0)
            value = value + tn(hot[k][...], rows)
        table[...] = value
        tail = jnp.zeros((held - ROOM, width), F32)
        for s in range(size):
            tail = tail + got[0][s, ROOM:].astype(F32)
        sums[...] = jnp.concatenate(
            [tail[0:1] + tail[1:2], tail[2:3] + tail[3:4], jnp.zeros((6, width), F32)], axis=0
        )

    return kernel_call(
        body,
        [shape(table_rows, width, F32), shape(8, width, F32)],
        [*hots, *gots],
    )


def rows_forward(parts, embedded, vectors, bias, in_pieces, down_pieces):
    rows, width = embedded.shape
    wide = in_pieces[0].shape[1]
    block = 256 if rows % 256 == 0 else rows
    count, total_count = len(in_pieces), len(in_pieces) + len(down_pieces)

    def body(first, second, emb, vec, bias_, *refs):
        middle, part, held, sems, held2, sems2 = refs[total_count:]

        @pl.when(pl.program_id(0) == 0)
        def _():
            wait = fill(refs[:count], held, sems)
            wait2 = fill(refs[count:total_count], held2, sems2)
            wait()
            wait2()

        total = emb[...] + vec[0:1] + (first[...].astype(F32) + second[...].astype(F32))
        value = norm_stats(total)[0] * vec[1:2] + vec[2:3]
        middle[...] = value
        hidden = dot(value.astype(BF), held[...]) + bias_[...]
        part[...] = nt(gelu(hidden).astype(BF), held2[...]).astype(BF)

    whole = pl.BlockSpec(memory_space=pltpu.VMEM)
    by_rows = pl.BlockSpec((block, width), lambda i: (i, 0))
    return kernel_call(
        body,
        [shape(rows, width, F32), shape(rows, width, BF)],
        [*parts, embedded, vectors, bias, *in_pieces, *down_pieces],
        total_count,
        [*held_scratch(in_pieces), *held_scratch(down_pieces)],
        grid=(rows // block,),
        specs=([by_rows, by_rows, by_rows, whole, whole], [by_rows, by_rows]),
    )


def rows_end(parts, middle, vectors, turn):
    rows, width = middle.shape
    block = 256 if rows % 256 == 0 else rows

    def body(first, second, mid, vec, turn_, out):
        total = mid[...] + vec[3:4] + (first[...].astype(F32) + second[...].astype(F32))
        final = norm_stats(total)[0] * vec[4:5] + vec[5:6]
        out[...] = nt(final.astype(BF), turn_[...]).astype(BF)

    whole = pl.BlockSpec(memory_space=pltpu.VMEM)
    by_rows = pl.BlockSpec((block, width), lambda i: (i, 0))
    return kernel_call(
        body,
        [shape(rows, width, BF)],
        [*parts, middle, vectors, turn],
        grid=(rows // block,),
        specs=([by_rows, by_rows, by_rows, whole, whole], [by_rows]),
    )[0]


def together(*values):
    return lax.optimization_barrier(values)


def per_device(
    tokens,
    embed_table,
    qkv_weight,
    qv_bias,
    out_weight,
    out_bias,
    norm1_gain,
    norm1_bias,
    in_weight,
    in_bias,
    down_weight,
    down_bias,
    norm2_gain,
    norm2_bias,
    masked_pos,
    replace_ids,
    masked_count,
    cotangent,
):
    size, cores = lax.axis_size("dp"), lax.axis_size("mp")
    me, core = lax.axis_index("dp"), lax.axis_index("mp")
    page_count, slot_count = masked_pos.shape
    length = tokens.shape[0] // page_count
    width = tokens.shape[1]
    shard_rows = width // size
    cut = size // 8
    table_rows = embed_table.shape[0]
    pages = page_count
    rows = pages * length
    own_slots = page_count // cores * slot_count
    slots = pages * slot_count
    head_cols = qkv_weight.shape[2]
    hidden_cols = in_weight.shape[1]
    far = far_digits(size)

    def to_core(values, step):
        pairs = [(c, (c + step) % cores) for c in range(cores)]
        return lax.ppermute(values, "mp", pairs)

    def from_cores(values):
        return [values] + [to_core(values, k) for k in range(1, cores)]

    def in_core_order(parts):
        whole = jnp.concatenate([parts[-k % cores] for k in range(cores)], axis=0)
        for at in range(1, cores):
            turned = jnp.concatenate([parts[(at - k) % cores] for k in range(cores)], axis=0)
            whole = jnp.where(core == at, turned, whole)
        return whole

    def own_pages(values):
        per = values.shape[0] // cores
        return lax.dynamic_slice_in_dim(values, core * per, per, 0)

    def spread_far(shard):
        blocks = [shard]
        for digit in far:
            packed = blocks[0] if len(blocks) == 1 else jnp.concatenate(blocks, axis=0)
            count = len(blocks)
            for step in range(1, digit[0]):
                got = send(packed, size, digit, step)
                blocks = blocks + [
                    got[k * shard_rows : (k + 1) * shard_rows] for k in range(count)
                ]
        return blocks

    def last_of(halves):
        pieces = []
        for half, pair in enumerate(halves):
            pieces += [*pair, *[send(part, size, NEAR[1 - half], 1) for part in pair]]
        return pieces

    def spread_near(blocks):
        halves = stack_rows([blocks[:cut], blocks[cut:]])
        return [(part, send(part, size, digit, 1)) for part, digit in zip(halves, NEAR)]

    def spread_last(halves):
        here = stack_rows([list(pair) for pair in halves])
        return here, [send(here[half], size, NEAR[1 - half], 1) for half in range(2)]

    def in_order(here, there):
        return [p for pair in zip(here, there) for p in pair]

    def halved(parts):
        middle = parts[0].shape[0] // 2
        sums = []
        for at in (slice(0, middle), slice(middle, None)):
            total = parts[0][at].astype(F32)
            for part in parts[1:]:
                total = total + part[at].astype(F32)
            sums.append(total.astype(BF))
        return sums

    def sum_first(pieces):
        return [
            (pieces[2 * half], send(pieces[2 * half + 1], size, NEAR[1 - half], 1))
            for half in range(2)
        ]

    def sum_second(*sums):
        done = []
        for half in range(2):
            both = zip(*[halved(halves[half]) for halves in sums])
            stay, leave_ = (jnp.concatenate(parts, axis=1) for parts in both)
            done.append((stay, send(leave_, size, NEAR[half], 1)))
        return done

    def sum_far(halves):
        blocks = []
        for stay, came in halves:
            for k in range(cut):
                here = slice(k * shard_rows, (k + 1) * shard_rows)
                blocks.append((stay[here].astype(F32) + came[here].astype(F32)).astype(BF))
        for digit in far[:0:-1]:
            blocks = [add_up(terms).astype(BF) for terms in spread_fold(blocks, digit)]
        return spread_fold(blocks, far[0])[0]

    def spread_fold(blocks, digit):
        radix = digit[0]
        inner = len(blocks) // radix
        terms = [[block] for block in blocks[:inner]]
        for step in range(1, radix):
            group = blocks[step * inner : (step + 1) * inner]
            packed = group[0] if inner == 1 else jnp.concatenate(group, axis=0)
            got = send(packed, size, digit, radix - step)
            for k in range(inner):
                terms[k].append(got[k * shard_rows : (k + 1) * shard_rows])
        return terms

    def add_up(terms):
        total = terms[0].astype(F32)
        for term in terms[1:]:
            total = total + term.astype(F32)
        return total

    pad = -(slot_count + 1) % 128
    packed_ids = jnp.concatenate(
        [replace_ids, masked_count[:, None], jnp.zeros((page_count, pad), jnp.int32)], axis=1
    )
    packed_ids = jnp.broadcast_to(packed_ids[None], (size, *packed_ids.shape))
    heads_shard = jnp.concatenate(
        [qkv_weight.reshape(shard_rows, 3 * head_cols), out_weight.T], axis=1
    )
    heads_far = spread_far(heads_shard)

    places = jnp.stack([me, core])
    used = jnp.arange(slot_count)[None, :] < masked_count[:, None]
    codes = jnp.where(used, replace_ids, -1)
    own_codes = own_pages(codes).reshape(1, own_slots)
    held_rows = held_order(size, shard_rows, me)[None, :]
    turn, turned_tokens, sent_hot = prepare(tokens, held_rows, own_codes, size, table_rows)
    packed_ids, turned_tokens, sent_hot, heads_far, in_shard = together(
        packed_ids, turned_tokens, sent_hot, heads_far, in_weight
    )

    all_ids = lax.all_to_all(packed_ids, "dp", 0, 0)
    heads_near = spread_near(heads_far)
    in_far = spread_far(in_shard)
    down_shard = down_weight.T
    vectors = jnp.stack(
        [out_bias, norm1_gain, norm1_bias, down_bias, norm2_gain, norm2_bias] + [out_bias] * 2
    )
    round_turn, _ = together(turn, in_shard)
    sents = from_cores(sent_hot)
    grad_final, vectors = turn_small(
        cotangent.reshape(slots, width), codes, vectors, round_turn
    )
    hidden_bias = in_bias[None]
    all_ids, heads_near, in_far, down_shard, grad_final = together(
        all_ids, heads_near, in_far, down_shard, grad_final
    )

    is_used = jnp.arange(slot_count)[None, None, :] < all_ids[:, :, slot_count : slot_count + 1]
    all_codes = jnp.where(is_used, all_ids[:, :, :slot_count], -1)
    all_codes = all_codes.reshape(size * cores, own_slots)
    *hots, found, fullest = serve(places, all_codes, embed_table, size, cores)
    found, heads_near, in_far = together(found, heads_near, in_far)
    found = lax.all_to_all(found.reshape(size, ROOM, width), "dp", 0, 0)
    found = found.reshape(size * ROOM, width)
    heads_here, heads_there = spread_last(heads_near)
    down_far = spread_far(down_shard)
    in_near = spread_near(in_far)
    found, fullest, hots, heads_here, heads_there, down_far, in_near = together(
        found, fullest, hots, heads_here, heads_there, down_far, in_near
    )

    rounds = (fullest.reshape(()) + ROOM - 1) // ROOM

    def round_of(turn_, held):
        own, every, held = lax.optimization_barrier((own_codes[0], all_codes, held))
        low = turn_ * ROOM
        spots = jnp.arange(own_slots)
        before = (spots[:, None] < spots[None, :]).astype(BF)
        to_owner = (own >= 0)[:, None] & (own[:, None] // table_rows == jnp.arange(size))
        rank = tn(before, to_owner.astype(BF)).astype(jnp.int32) - low
        sent = (rank[:, :, None] == jnp.arange(ROOM)) & to_owner[:, :, None]
        sent = sent.astype(BF).reshape(own_slots, size * ROOM)
        mine = (every >= 0) & (every // table_rows == me)
        rank = dot(mine.astype(BF), before).astype(jnp.int32) - low
        hit = (rank[:, None, :] == jnp.arange(ROOM)[None, :, None]) & mine[:, None, :]
        asked = jnp.sum(jnp.where(hit, every[:, None, :] - me * table_rows + 1, 0), axis=2) - 1
        hot = (asked[:, :, None] == jnp.arange(table_rows)).astype(BF)
        hot = hot.reshape(size, cores, ROOM, table_rows)
        turned = [
            lax.dynamic_index_in_dim(hot, (core + cores - k) % cores, 1, keepdims=False)
            for k in range(cores)
        ]
        return sent, [t.reshape(size * ROOM, table_rows) for t in turned], held

    def more_rows(turn_, held):
        sent, later, held = round_of(turn_, held)
        got = dot(later[0], embed_table).astype(BF).reshape(size, ROOM, width)
        got = lax.all_to_all(got, "dp", 0, 0).reshape(size * ROOM, width)
        return held + in_core_order(from_cores(dot(sent, got).astype(BF)))

    more = lax.fori_loop(1, rounds, more_rows, jnp.zeros((slots, width), F32))
    founds = from_cores(found)
    heads_pieces = in_order(heads_here, heads_there)
    embedded, low, query, key, value, s_embedded, s_low, s_query, s_attended, s_part = enter(
        places,
        turned_tokens,
        founds,
        sents,
        more,
        turn,
        masked_pos,
        qv_bias,
        heads_pieces,
    )
    down_near = spread_near(down_far)
    in_here, in_there = spread_last(in_near)
    s_part, down_near, in_here, in_there, query = together(
        s_part, down_near, in_here, in_there, query
    )

    down_pieces = last_of(down_near)
    s_parts = from_cores(s_part)
    rows_part = attend_all(query, key, value, heads_pieces, pages)
    s_parts, down_pieces, rows_part = together(s_parts, down_pieces, rows_part)

    in_pieces = in_order(in_here, in_there)
    unit1, scale1, middle_low, hidden, slope, s_part = slot_forward(
        s_parts, s_embedded, vectors, hidden_bias, in_pieces, down_pieces
    )
    s_parts = from_cores(s_part)
    *grad_down, grad_r2, grad_hidden_in, small2, grad_in_bias, s_part = slot_turn(
        s_parts, hidden, slope, unit1, grad_final, vectors, in_pieces, down_pieces
    )
    s_part, rows_part = together(s_part, rows_part)

    s_parts = from_cores(s_part)
    rows_parts = from_cores(rows_part)
    down_sum = sum_first(grad_down)
    grad_in = in_grad(middle_low, grad_hidden_in, [p.shape[0] for p in in_pieces])
    s_parts, grad_in = together(s_parts, grad_in)

    in_sum = sum_first(grad_in)
    *grad_heads, grad_r1, part, small1, small0 = slot_back(
        s_parts,
        grad_r2,
        unit1,
        scale1,
        s_attended,
        s_query,
        key,
        value,
        s_low,
        low,
        vectors,
        masked_pos,
        heads_pieces,
    )
    down_sum, in_sum, grad_heads, part, rows_parts = together(
        down_sum, in_sum, grad_heads, part, rows_parts
    )

    heads_sum = sum_first(grad_heads)
    units_sum = sum_second(down_sum, in_sum)
    parts = from_cores(part)
    middle, rows_part = rows_forward(
        rows_parts, embedded, vectors, hidden_bias, in_pieces, down_pieces
    )
    parts, rows_part = together(parts, rows_part)
    grad_input, moved, own_grad = leave(
        places,
        parts,
        grad_r1,
        masked_pos,
        turn,
        held_rows,
        sent_hot,
        [small1, small2, small0, grad_in_bias],
        size,
    )
    units_sum, heads_sum, grad_input, moved, rows_part = together(
        units_sum, heads_sum, grad_input, moved, rows_part
    )

    gots = lax.all_to_all(moved, "dp", 0, 0)
    units_sum = sum_far(units_sum)
    heads_sum = sum_second(heads_sum)
    output = rows_end(from_cores(rows_part), middle, vectors, turn)
    units_sum, heads_sum, output, gots = together(units_sum, heads_sum, output, gots)

    heads_sum = sum_far(heads_sum)
    grad_table, totals = collect(hots, from_cores(gots))
    units_share = add_up(units_sum)
    down_share, in_share = units_share[:, :hidden_cols].T, units_share[:, hidden_cols:]
    def more_table(turn_, held):
        sent, later, held = round_of(turn_, held)
        got = tn(sent, own_grad).astype(BF).reshape(size, ROOM, width)
        for hot, block in zip(later, from_cores(lax.all_to_all(got, "dp", 0, 0))):
            held = held + tn(hot, block.reshape(size * ROOM, width))
        return held

    grad_table = lax.fori_loop(1, rounds, more_table, grad_table)
    def piece(row, block, count):
        return totals[row, block * 128 : block * 128 + count]

    vec = [piece(0, k, shard_rows) for k in range(6)]
    own = [
        piece(1, 0, head_cols // size),
        piece(1, 1, head_cols // size),
        piece(1, 2, hidden_cols // size),
    ]
    heads_sum, in_share, down_share, grad_table, vec, own = together(
        heads_sum, in_share, down_share, grad_table, vec, own
    )
    heads_share = add_up(heads_sum)
    qkv_share = heads_share[:, : 3 * head_cols].reshape(shard_rows, 3, head_cols)
    out_share = heads_share[:, 3 * head_cols :].T


    return (
        output,
        grad_input,
        grad_table,
        qkv_share,
        jnp.stack([own[0], own[1]])[:, None, :],
        out_share,
        vec[0],
        vec[1],
        vec[2],
        in_share,
        own[2][None],
        down_share,
        vec[3],
        vec[4],
        vec[5],
    )


def solution(mesh):
    in_specs = (
        P("dp", None),
        P("dp", None),
        P("dp", None, "mp"),
        P(None, "mp"),
        P("mp", "dp"),
        P(),
        P(),
        P(),
        P("dp", "mp"),
        P("mp"),
        P("mp", "dp"),
        P(),
        P(),
        P(),
        P("dp", None),
        P("dp", None),
        P("dp"),
        P("dp", None, None),
    )
    out_specs = (
        P("dp", None),
        P("dp", None),
        P("dp", None),
        P("dp", None, "mp"),
        P(None, "mp", "dp"),
        P("mp", "dp"),
        P("dp"),
        P("dp"),
        P("dp"),
        P("dp", "mp"),
        P("mp", "dp"),
        P("mp", "dp"),
        P("dp"),
        P("dp"),
        P("dp"),
    )
    return jax.shard_map(
        per_device, mesh=mesh, in_specs=in_specs, out_specs=out_specs, check_vma=False
    )
```

```python
import jax
import jax.numpy as jnp
import numpy as np
from jax import lax
from jax.experimental import pallas as pl
from jax.experimental.pallas import tpu as pltpu
from jax.sharding import PartitionSpec as P

HEAD = 64
EPSILON = 1e-05
ROOM = 16
EXTRA = 8

BF = jnp.bfloat16
F32 = jnp.float32


def dot(a, b, dims=((1,), (0,)), **kw):
    return lax.dot_general(a, b, (dims, ((), ())), preferred_element_type=F32, **kw)


def nt(a, b):
    return dot(a, b, ((1,), (1,)))


def tn(a, b):
    return dot(a, b, ((0,), (0,)))


def split_two(values):
    high = values.astype(BF)
    return high, (values - high.astype(F32)).astype(BF)


def far_digits(size):
    found = []
    stride, rest = 4, size // 4
    while rest > 1:
        radix = next(r for r in (4, 2, 3, 5, 7, rest) if rest % r == 0)
        found.append((radix, stride))
        stride, rest = stride * radix, rest // radix
    return found


NEAR = ((2, 1), (2, 2))


def shift(size, digit, step):
    radix, stride = digit
    pairs = []
    for src in range(size):
        own = (src // stride) % radix
        pairs.append((src, src + ((own + step) % radix - own) * stride))
    return pairs


def send(values, size, digit, step):
    return lax.ppermute(values, "dp", shift(size, digit, step))


def held_order(size, rows, me):
    blocks = size // 8
    place = jnp.arange(size * rows)
    second = place >= size * rows // 2
    slot, row = (place % (size * rows // 2)) // rows, place % rows
    block = slot % blocks + jnp.where(second, blocks, 0)
    low, high = (slot // blocks) % 2, slot // blocks // 2
    owner = jnp.zeros_like(place)
    for radix, stride in far_digits(size):
        owner = owner + ((me // stride - block % radix) % radix) * stride
        block = block // radix
    x_step, y_step = jnp.where(second, high, low), jnp.where(second, low, high)
    owner = owner + (me - x_step) % 2 + ((me // 2 - y_step) % 2) * 2
    return owner * rows + row


VMEM_LIMIT = 20 * 1024 * 1024


def kernel_call(body, outs, inputs, far_count=0, scratch=(), flops=0, grid=None, specs=None):
    near = len(inputs) - far_count
    in_specs, out_specs = specs or (
        [pl.BlockSpec(memory_space=pltpu.VMEM)] * near,
        [pl.BlockSpec(memory_space=pltpu.VMEM)] * len(outs),
    )
    return pl.pallas_call(
        body,
        grid=grid or (),
        out_shape=outs,
        in_specs=[*in_specs, *([pl.BlockSpec(memory_space=pl.ANY)] * far_count)],
        out_specs=out_specs,
        scratch_shapes=scratch,
        compiler_params=pltpu.CompilerParams(vmem_limit_bytes=VMEM_LIMIT),
        cost_estimate=pl.CostEstimate(flops=1, bytes_accessed=1, transcendentals=0),
    )(*inputs)


def shape(rows, cols, dtype):
    return jax.ShapeDtypeStruct((rows, cols), dtype)


def fill(pieces, held, sems, start=0):
    copies, at = [], 0
    for i, piece in enumerate(pieces):
        rows = piece.shape[0]
        source = piece.at[:, pl.ds(start, held.shape[1])]
        copy = pltpu.make_async_copy(source, held.at[pl.ds(at, rows)], sems.at[i])
        copy.start()
        copies.append(copy)
        at += rows

    def wait():
        for copy in copies:
            copy.wait()

    return wait


def held_scratch(pieces, cols=None):
    rows = sum(p.shape[0] for p in pieces)
    return [
        pltpu.VMEM((rows, cols or pieces[0].shape[1]), BF),
        pltpu.SemaphoreType.DMA((len(pieces),)),
    ]


def norm_stats(values):
    row_mean = jnp.mean(values, axis=-1, keepdims=True)
    centered = values - row_mean
    scale = lax.rsqrt(jnp.mean(centered * centered, axis=-1, keepdims=True) + EPSILON)
    return centered * scale, scale


def norm_back(grad, unit, scale, gain):
    inner = grad * gain
    mean_inner = jnp.mean(inner, axis=-1, keepdims=True)
    mean_unit = jnp.mean(inner * unit, axis=-1, keepdims=True)
    return (
        scale * (inner - mean_inner - unit * mean_unit),
        jnp.sum(grad * unit, axis=0, keepdims=True),
        jnp.sum(grad, axis=0, keepdims=True),
    )


def gelu(values):
    return values * (0.5 + 0.5 * lax.erf(values * (0.5**0.5)))


def gelu_both(values):
    normal = 0.5 + 0.5 * lax.erf(values * (0.5**0.5))
    bell = jnp.exp(-0.5 * values * values) * (0.5 / np.pi) ** 0.5
    return values * normal, normal + values * bell


def head_masks(dtype):
    lane = lax.broadcasted_iota(jnp.int32, (1, 2 * HEAD), 1)
    return [(lane // HEAD == h).astype(dtype) for h in range(2)]


def attend_pair(query, key, value):
    lanes = value.shape[1]
    wider = jnp.concatenate([value, jnp.ones_like(value)], axis=1)
    outs = []
    for mask in head_masks(BF):
        scores = nt(query * mask, key)
        powers = jnp.exp(scores - jnp.max(scores, axis=-1, keepdims=True))
        both = dot(powers.astype(BF), wider)
        outs.append(both[:, :lanes] / both[:, lanes:])
    first, second = head_masks(F32)
    return (outs[0] * first + outs[1] * second).astype(BF)


def one_hot_rows(row_of_line, rows):
    at = lax.broadcasted_iota(jnp.int32, (rows, row_of_line.shape[1]), 0)
    return (at == row_of_line).astype(F32).astype(BF)


def one_hot_slots(row_of_column, rows):
    at = lax.broadcasted_iota(jnp.int32, (row_of_column.shape[0], rows), 1)
    return (at == row_of_column).astype(F32).astype(BF)


def as_column(line):
    count = line.shape[1]
    square = (count, count)
    same = lax.broadcasted_iota(jnp.int32, square, 0) == lax.broadcasted_iota(jnp.int32, square, 1)
    return jnp.sum(jnp.where(same, line.astype(F32), 0.0), axis=1, keepdims=True)


def floor_by(values, divisor):
    return jnp.floor((values + 0.5) * (1.0 / divisor))


def iota(dims, axis):
    return lax.broadcasted_iota(jnp.int32, dims, axis).astype(F32)


def serve(places, codes, table, size, cores):
    table_rows, width = table.shape
    devices, slots = codes.shape
    count = size * ROOM

    def body(place, code, tab, *outs):
        *hots, found, most = outs
        me, core = place[0], place[1]
        line = code[...].astype(F32)
        local = line - (me * table_rows).astype(F32)
        mine = (local >= 0) & (local < table_rows)
        before = (iota((slots, slots), 0) < iota((slots, slots), 1)).astype(BF)
        rank = dot(mine.astype(F32).astype(BF), before)
        rank = jnp.where(mine & (rank < ROOM), rank, 255.0).astype(BF)
        local = jnp.where(mine, local, 0.0)
        local_high = floor_by(local, 256)
        local_low = (local - 256 * local_high).astype(BF)
        local_high = local_high.astype(BF)
        source = floor_by(iota((count, 1), 0), ROOM)
        room = iota((count, 1), 0) - ROOM * source
        for k in range(cores):
            which = lax.rem(core + cores - k, cores).astype(F32)
            pick = (iota((count, devices), 1) == source * cores + which).astype(F32).astype(BF)
            hit = dot(pick, rank) == room
            at = 256 * dot(pick, local_high) + dot(pick, local_low) + 1.0
            asked = jnp.sum(jnp.where(hit, at, 0.0), axis=1, keepdims=True) - 1.0
            hots[k][...] = (iota((count, table_rows), 1) == asked).astype(F32).astype(BF)
        found[...] = dot(hots[0][...], tab[...]).astype(BF)
        owner = floor_by(line, table_rows)
        fullest = jnp.zeros((devices, 1), F32)
        for o in range(size):
            here = jnp.sum(jnp.where(owner == o, 1.0, 0.0), axis=1, keepdims=True)
            fullest = jnp.maximum(fullest, here)
        fullest = jnp.max(fullest, axis=0, keepdims=True)
        most[...] = fullest.astype(jnp.int32)

    smem, vmem = pl.BlockSpec(memory_space=pltpu.SMEM), pl.BlockSpec(memory_space=pltpu.VMEM)
    return kernel_call(
        body,
        [
            *[shape(count, table_rows, BF)] * cores,
            shape(count, width, BF),
            shape(1, 1, jnp.int32),
        ],
        [places, codes, table],
        flops=2 * count * table_rows * width,
        specs=([smem, vmem, vmem], [vmem] * (cores + 2)),
    )


def by_owner(values, owner, place, size):
    count = values.shape[1]
    hit = (iota((size, count), 0) == owner).astype(F32)
    rows = jnp.concatenate([hit * values[r : r + 1] for r in range(values.shape[0])], axis=0)
    hot = (iota((128, count), 0) == place).astype(F32).astype(BF)
    total, rest = 0.0, rows
    for _ in range(3):
        high = rest.astype(BF)
        rest = rest - high.astype(F32)
        total = total + nt(high, hot)
    return total


def stack_rows(groups):
    if any(part.shape[0] % 16 for group in groups for part in group):
        return [jnp.concatenate(group, axis=0) for group in groups]

    def body(*refs):
        at = 0
        for out, group in zip(refs[len(refs) - len(groups) :], groups):
            start = 0
            for part in group:
                out[start : start + part.shape[0]] = refs[at][...]
                start, at = start + part.shape[0], at + 1

    outs = [shape(sum(p.shape[0] for p in group), group[0].shape[1], BF) for group in groups]
    return kernel_call(body, outs, [part for group in groups for part in group])


def prepare(tokens, order, codes, size, table_rows):
    rows, width = tokens.shape
    slots = codes.shape[1]

    def body(tok, order_, code, turn, tok_out, sent):
        turn[...] = (
            (lax.broadcasted_iota(jnp.int32, (width, width), 0) == order_[...])
            .astype(F32)
            .astype(BF)
        )
        line = code[...].astype(F32)
        column = as_column(line)
        owner_line, owner = floor_by(line, table_rows), floor_by(column, table_rows)
        square = (slots, slots)
        earlier = (iota(square, 1) < iota(square, 0)) & (owner_line == owner)
        rank = jnp.sum(jnp.where(earlier, 1.0, 0.0), axis=1, keepdims=True)
        target = jnp.where((column >= 0) & (rank < ROOM), owner * ROOM + rank, -1.0)
        sent[...] = (iota((slots, size * ROOM), 1) == target).astype(F32).astype(BF)
        tok_out[...] = dot(tok[...], turn[...]).astype(BF)

    return kernel_call(
        body,
        [shape(width, width, BF), shape(rows, width, BF), shape(slots, size * ROOM, BF)],
        [tokens, order, codes],
    )


def turn_small(cotangent, codes, vectors, turn):
    slots, width = cotangent.shape

    def body(cot, code, vec, turn_, cot_out, vec_out):
        pages, per = code.shape
        for g in range(pages):
            here = slice(g * per, (g + 1) * per)
            used = (as_column(code[g : g + 1]) >= 0).astype(F32).astype(BF)
            cot_out[here] = dot(cot[here] * used, turn_[...]).astype(BF)
        rest, total = vec[...], 0.0
        for _ in range(3):
            high = rest.astype(BF)
            rest = rest - high.astype(F32)
            total = total + dot(high, turn_[...])
        vec_out[...] = total

    return kernel_call(
        body,
        [shape(slots, width, BF), shape(vectors.shape[0], width, F32)],
        [cotangent, codes, vectors, turn],
    )


def enter(places, tokens, founds, sents, more, turn, pos, qv_bias, pieces):
    rows, width = tokens.shape
    pages, per = pos.shape
    slots, cores = pages * per, len(founds)
    own = sents[0].shape[0]
    near = 6 + 2 * cores
    cols = qv_bias.shape[1]
    length = rows // pages

    def body(*refs):
        place_, tok, more_, turn_, pos_, bias_ = refs[:6]
        found, sent = refs[6 : 6 + cores], refs[6 + cores : near]
        piece_refs = refs[near : near + len(pieces)]
        (
            emb,
            low,
            q,
            k,
            v,
            s_emb,
            s_low,
            s_q,
            s_att,
            s_out,
            fetched,
            held,
            sems,
        ) = refs[near + len(pieces) :]
        wait = fill(piece_refs, held, sems)
        for c in range(cores):
            start = pl.multiple_of(lax.rem(place_[1] + cores - c, cores) * own, own)
            fetched[pl.ds(start, own)] = dot(sent[c][...], found[c][...])
        fetched[...] += more_[...]
        new = dot(fetched[...].astype(BF), turn_[...]).astype(BF)
        hots = []
        for g in range(pages):
            page, here = slice(g * length, (g + 1) * length), slice(g * per, (g + 1) * per)
            placed = one_hot_rows(pos_[g : g + 1], length)
            hot = one_hot_slots(as_column(pos_[g : g + 1]), length)
            hots.append(hot)
            exact = tok[page].astype(F32) + dot(placed, new[here])
            emb[page] = exact
            low[page] = exact.astype(BF)
            s_emb[here] = dot(hot, tok[page]) + new[here].astype(F32)
        s_low[...] = s_emb[...].astype(BF)
        wait()
        for g in range(pages):
            page, here = slice(g * length, (g + 1) * length), slice(g * per, (g + 1) * per)
            q[page] = (dot(low[page], held[:, :cols]) + bias_[0:1]).astype(BF)
            k[page] = dot(low[page], held[:, cols : 2 * cols]).astype(BF)
            v[page] = (dot(low[page], held[:, 2 * cols : 3 * cols]) + bias_[1:2]).astype(BF)
            s_q[here] = dot(hots[g], q[page]).astype(BF)
            for j in range(0, cols, 2 * HEAD):
                at = slice(j, j + 2 * HEAD)
                s_att[here, at] = attend_pair(s_q[here, at] * HEAD**-0.5, k[page, at], v[page, at])
        s_out[...] = nt(s_att[...], held[:, 3 * cols :])

    outs = [
        shape(rows, width, F32),
        shape(rows, width, BF),
        *[shape(rows, cols, BF)] * 3,
        shape(slots, width, F32),
        shape(slots, width, BF),
        *[shape(slots, cols, BF)] * 2,
        shape(slots, width, F32),
    ]
    return kernel_call(
        body,
        outs,
        [places, tokens, more, turn, pos, qv_bias, *founds, *sents, *pieces],
        len(pieces),
        [pltpu.VMEM((slots, width), F32), *held_scratch(pieces)],
        specs=(
            [
                pl.BlockSpec(memory_space=pltpu.SMEM),
                *([pl.BlockSpec(memory_space=pltpu.VMEM)] * (near - 1)),
            ],
            [pl.BlockSpec(memory_space=pltpu.VMEM)] * len(outs),
        ),
    )


def attend_all(query, key, value, pieces, pages):
    rows, cols = query.shape
    length, pairs = rows // pages, cols // (2 * HEAD)
    width = sum(p.shape[0] for p in pieces)

    def body(q, k, v, *refs):
        out, total, held, sems = refs[len(pieces) :]
        first, pair = pl.program_id(0) == 0, pl.program_id(1)

        @pl.when(first & (pair == 0))
        def _():
            fill(refs[: len(pieces)], held, sems, 3 * cols)()

        half = length // 2
        for part in range(2):
            here = slice(part * half, (part + 1) * half)
            attended = attend_pair(q[here] * HEAD**-0.5, k[...], v[...])
            at = pl.ds(pl.multiple_of(pair * 2 * HEAD, 2 * HEAD), 2 * HEAD)
            total[here, at] = attended

        @pl.when(pair == pairs - 1)
        def _():
            out[...] = nt(total[...], held[...]).astype(BF)

    spec = pl.BlockSpec((length, 2 * HEAD), lambda g, j: (g, j))
    return kernel_call(
        body,
        [shape(rows, width, BF)],
        [query, key, value, *pieces],
        len(pieces),
        [pltpu.VMEM((length, cols), BF), *held_scratch(pieces, cols)],
        grid=(pages, pairs),
        specs=([spec] * 3, [pl.BlockSpec((length, width), lambda g, j: (g, 0))]),
    )[0]


def slot_forward(parts, embedded, vectors, bias, in_pieces, down_pieces):
    slots, width = embedded.shape
    wide = in_pieces[0].shape[1]
    count, total_count = len(in_pieces), len(in_pieces) + len(down_pieces)

    def body(first, second, emb, vec, bias_, *refs):
        unit1, scale1, mid_low, hid, slope, part, held, sems, held2, sems2 = refs[total_count:]
        wait = fill(refs[:count], held, sems)
        wait2 = fill(refs[count:total_count], held2, sems2)
        unit, scale = norm_stats(emb[...] + vec[0:1] + (first[...] + second[...]))
        unit1[...] = unit
        scale1[...] = jnp.broadcast_to(scale, scale1.shape)
        mid_low[...] = (unit * vec[1:2] + vec[2:3]).astype(BF)
        wait()
        value, rate = gelu_both(dot(mid_low[...], held[...]) + bias_[...])
        hid[...] = value.astype(BF)
        slope[...] = rate
        wait2()
        part[...] = nt(hid[...], held2[...])

    outs = [
        shape(slots, width, F32),
        shape(slots, 128, F32),
        shape(slots, width, BF),
        shape(slots, wide, BF),
        shape(slots, wide, F32),
        shape(slots, width, F32),
    ]
    return kernel_call(
        body,
        outs,
        [*parts, embedded, vectors, bias, *in_pieces, *down_pieces],
        total_count,
        [*held_scratch(in_pieces), *held_scratch(down_pieces)],
    )


def put_rows(outs, start, values):
    at = 0
    for out in outs:
        rows = out.shape[0]
        out[:, start : start + values.shape[1]] = values[at : at + rows].astype(BF)
        at += rows


def slot_turn(parts, hidden, slope, unit1, grad_final, vectors, in_pieces, down_pieces):
    slots, width = unit1.shape
    wide = hidden.shape[1]
    count, total_count = len(in_pieces), len(in_pieces) + len(down_pieces)

    def body(first, second, hid, slp, un1, final, vec, *refs):
        (*grads, grad2, ghin, small, in_small, mid, held, sems, held2, sems2) = refs[total_count:]
        wait = fill(refs[:count], held, sems)
        wait2 = fill(refs[count:total_count], held2, sems2)
        total = un1[...] * vec[1:2] + vec[2:3] + vec[3:4] + (first[...] + second[...])
        unit, scale = norm_stats(total)
        grad, gain, bias = norm_back(final[...].astype(F32), unit, scale, vec[4:5])
        grad2[...] = grad
        grad_low = grad.astype(BF)
        small[0:1] = jnp.sum(grad_low.astype(F32), axis=0, keepdims=True)
        small[1:2] = gain
        small[2:3] = bias
        small[3:8] = jnp.zeros((5, width), F32)
        wait2()
        back = (dot(grad_low, held2[...]) * slp[...]).astype(BF)
        ghin[...] = back
        in_small[...] = jnp.sum(back.astype(F32), axis=0, keepdims=True)
        wait()
        mid[...] = nt(back, held[...])
        put_rows(grads, 0, tn(grad_low, hid[...]))

    outs = [
        *[shape(p.shape[0], wide, BF) for p in in_pieces],
        shape(slots, width, F32),
        shape(slots, wide, BF),
        shape(8, width, F32),
        shape(1, wide, F32),
        shape(slots, width, F32),
    ]
    return kernel_call(
        body,
        outs,
        [*parts, hidden, slope, unit1, grad_final, vectors, *in_pieces, *down_pieces],
        total_count,
        [*held_scratch(in_pieces), *held_scratch(down_pieces)],
    )


def in_grad(mid_low, ghin, heights):
    def body(mid, gh, *grads):
        put_rows(grads, 0, tn(mid[...], gh[...]))

    return kernel_call(body, [shape(r, ghin.shape[1], BF) for r in heights], [mid_low, ghin])


def slot_back(parts, grad2, unit1, scale1, attended, s_query, key, value, s_low, low, vectors, pos, pieces):
    slots, width = unit1.shape
    rows, cols = key.shape
    pages, per = pos.shape
    length = rows // pages
    scale = HEAD**-0.5

    def body(first, second, g2, un1, sc1, att, sq, k, v, sl, lo, vec, pos_, *refs):
        (*grads, grad1, part, small, small_heads, gq, gk, gv, held, sems) = refs[len(pieces) :]
        wait = fill(refs[: len(pieces)], held, sems)
        total = g2[...] + (first[...] + second[...])
        grad, gain, bias = norm_back(total, un1[...], sc1[:, :1], vec[1:2])
        grad1[...] = grad
        grad_low = grad.astype(BF)
        small[0:1] = jnp.sum(grad_low.astype(F32), axis=0, keepdims=True)
        small[1:2] = gain
        small[2:3] = bias
        small[3:8] = jnp.zeros((5, width), F32)
        put_rows(grads, 3 * cols, tn(grad_low, att[...]))
        wait()
        gatt = dot(grad_low, held[:, 3 * cols :]).astype(BF)
        masks = head_masks(BF)
        left_lanes, right_lanes = head_masks(F32)
        for g in range(pages):
            here, page = slice(g * per, (g + 1) * per), slice(g * length, (g + 1) * length)
            for j in range(0, cols, 2 * HEAD):
                at = slice(j, j + 2 * HEAD)
                query, back = sq[here, at], gatt[here, at]
                keys, values = k[page, at], v[page, at]
                got = []
                for mask in masks:
                    scores = nt(query * mask * scale, keys)
                    powers = jnp.exp(scores - jnp.max(scores, axis=-1, keepdims=True))
                    prob = powers * (1.0 / jnp.sum(powers, axis=-1, keepdims=True))
                    grad_prob = nt(back * mask, values)
                    inner = jnp.sum(prob * grad_prob, axis=-1, keepdims=True)
                    grad_scores = (prob * (grad_prob - inner)).astype(BF)
                    got.append(
                        (
                            dot(grad_scores, keys),
                            tn(grad_scores, query),
                            tn(prob.astype(BF), back),
                        )
                    )
                left, right = got
                gq[here, at] = ((left[0] * left_lanes + right[0] * right_lanes) * scale).astype(BF)
                gk[page, at] = ((left[1] * left_lanes + right[1] * right_lanes) * scale).astype(BF)
                gv[page, at] = (left[2] * left_lanes + right[2] * right_lanes).astype(BF)
        small_heads[0:1] = jnp.sum(gq[...].astype(F32), axis=0, keepdims=True)
        small_heads[1:2] = jnp.sum(gv[...].astype(F32), axis=0, keepdims=True)
        small_heads[2:8] = jnp.zeros((6, cols), F32)
        put_rows(grads, 0, tn(sl[...], gq[...]))
        put_rows(grads, cols, tn(lo[...], gk[...]))
        put_rows(grads, 2 * cols, tn(lo[...], gv[...]))
        high, rest = split_two(nt(gq[...], held[:, :cols]))
        for g in range(pages):
            here, page = slice(g * per, (g + 1) * per), slice(g * length, (g + 1) * length)
            placed = one_hot_rows(pos_[g : g + 1], length)
            total = nt(gk[page], held[:, cols : 2 * cols]) + nt(gv[page], held[:, 2 * cols : 3 * cols])
            total = total + dot(placed, high[here]) + dot(placed, rest[here])
            part[page] = total.astype(BF)

    outs = [
        *[shape(p.shape[0], 4 * cols, BF) for p in pieces],
        shape(slots, width, F32),
        shape(rows, width, BF),
        shape(8, width, F32),
        shape(8, cols, F32),
    ]
    return kernel_call(
        body,
        outs,
        [*parts, grad2, unit1, scale1, attended, s_query, key, value, s_low, low, vectors, pos, *pieces],
        len(pieces),
        [
            pltpu.VMEM((slots, cols), BF),
            *[pltpu.VMEM((rows, cols), BF)] * 2,
            *held_scratch(pieces),
        ],
    )


def leave(places, parts, grad1, pos, turn, order, sent_hot, smalls, size):
    rows, width = parts[0].shape
    pages, per = pos.shape
    length = rows // pages
    own = sent_hot.shape[0] // per
    cols, wide = smalls[2].shape[1], smalls[3].shape[1]

    def body(place_, first, second, g1, pos_, turn_, order_, hot, sm1, sm2, smq, smh, out, moved, mine):
        high, low = split_two(g1[...])
        for g in range(pages):
            page, here = slice(g * length, (g + 1) * length), slice(g * per, (g + 1) * per)
            placed = one_hot_rows(pos_[g : g + 1], length)
            total = first[page].astype(F32) + second[page].astype(F32)
            total = total + dot(placed, high[here]) + dot(placed, low[here])
            near, rest = split_two(total)
            out[page] = nt(near, turn_[...]) + nt(rest, turn_[...])

        place = order_[...].astype(F32)
        owner = floor_by(place, width // size)
        vec = jnp.concatenate([sm1[0:3], sm2[0:3]], axis=0)
        vec = by_owner(vec, owner, place - owner * (width // size), size)
        vec = jnp.concatenate([vec[r * size : (r + 1) * size] for r in range(6)], axis=1)
        at = iota((1, cols), 1)
        owner = floor_by(at, cols // size)
        head = by_owner(smq[0:2], owner, at - owner * (cols // size), size)
        at = iota((1, wide), 1)
        owner = floor_by(at, wide // size)
        unit = by_owner(smh[...], owner, at - owner * (wide // size), size)
        others = jnp.concatenate([head[:size], head[size:], unit], axis=1)
        filler = jnp.zeros((size, width - others.shape[1]), F32)
        others = jnp.concatenate([others, filler], axis=1)
        tails = [p.astype(F32) for values in (vec, others) for p in split_two(values)]
        going = 0.0
        for i in range(own):
            page = place_[1] * own + i
            slot_hot = one_hot_slots(as_column(pos_[pl.ds(page, 1)]), length)
            here = out[pl.ds(pl.multiple_of(page * length, length), length)]
            picked = dot(slot_hot, here.astype(BF)).astype(BF)
            mine[i * per : (i + 1) * per] = picked
            going = going + tn(hot[i * per : (i + 1) * per], picked)
        for s in range(size):
            moved[s, :ROOM] = going[s * ROOM : (s + 1) * ROOM].astype(BF)
            tail = [t[s : s + 1] for t in tails] + [jnp.zeros((EXTRA - len(tails), width), F32)]
            moved[s, ROOM:] = jnp.concatenate(tail, axis=0).astype(BF)

    return kernel_call(
        body,
        [
            shape(rows, width, F32),
            jax.ShapeDtypeStruct((size, ROOM + EXTRA, width), BF),
            shape(own * per, width, BF),
        ],
        [places, *parts, grad1, pos, turn, order, sent_hot, *smalls],
        specs=(
            [
                pl.BlockSpec(memory_space=pltpu.SMEM),
                *([pl.BlockSpec(memory_space=pltpu.VMEM)] * 11),
            ],
            [pl.BlockSpec(memory_space=pltpu.VMEM)] * 3,
        ),
    )


def collect(hots, gots):
    cores, (count, table_rows) = len(hots), hots[0].shape
    size, held, width = gots[0].shape

    def body(*refs):
        hot, got = refs[:cores], refs[cores : 2 * cores]
        table, sums = refs[2 * cores :]
        value = 0.0
        for k in range(cores):
            rows = jnp.concatenate([got[k][s, :ROOM] for s in range(size)], axis=0)
            value = value + tn(hot[k][...], rows)
        table[...] = value
        tail = jnp.zeros((held - ROOM, width), F32)
        for s in range(size):
            tail = tail + got[0][s, ROOM:].astype(F32)
        sums[...] = jnp.concatenate(
            [tail[0:1] + tail[1:2], tail[2:3] + tail[3:4], jnp.zeros((6, width), F32)], axis=0
        )

    return kernel_call(
        body,
        [shape(table_rows, width, F32), shape(8, width, F32)],
        [*hots, *gots],
    )


def rows_forward(parts, embedded, vectors, bias, in_pieces, down_pieces):
    rows, width = embedded.shape
    wide = in_pieces[0].shape[1]
    block = 256 if rows % 256 == 0 else rows
    count, total_count = len(in_pieces), len(in_pieces) + len(down_pieces)

    def body(first, second, emb, vec, bias_, *refs):
        middle, part, held, sems, held2, sems2 = refs[total_count:]

        @pl.when(pl.program_id(0) == 0)
        def _():
            wait = fill(refs[:count], held, sems)
            wait2 = fill(refs[count:total_count], held2, sems2)
            wait()
            wait2()

        total = emb[...] + vec[0:1] + (first[...].astype(F32) + second[...].astype(F32))
        value = norm_stats(total)[0] * vec[1:2] + vec[2:3]
        middle[...] = value
        hidden = dot(value.astype(BF), held[...]) + bias_[...]
        part[...] = nt(gelu(hidden).astype(BF), held2[...]).astype(BF)

    whole = pl.BlockSpec(memory_space=pltpu.VMEM)
    by_rows = pl.BlockSpec((block, width), lambda i: (i, 0))
    return kernel_call(
        body,
        [shape(rows, width, F32), shape(rows, width, BF)],
        [*parts, embedded, vectors, bias, *in_pieces, *down_pieces],
        total_count,
        [*held_scratch(in_pieces), *held_scratch(down_pieces)],
        grid=(rows // block,),
        specs=([by_rows, by_rows, by_rows, whole, whole], [by_rows, by_rows]),
    )


def rows_end(parts, middle, vectors, turn):
    rows, width = middle.shape
    block = 256 if rows % 256 == 0 else rows

    def body(first, second, mid, vec, turn_, out):
        total = mid[...] + vec[3:4] + (first[...].astype(F32) + second[...].astype(F32))
        final = norm_stats(total)[0] * vec[4:5] + vec[5:6]
        out[...] = nt(final.astype(BF), turn_[...]).astype(BF)

    whole = pl.BlockSpec(memory_space=pltpu.VMEM)
    by_rows = pl.BlockSpec((block, width), lambda i: (i, 0))
    return kernel_call(
        body,
        [shape(rows, width, BF)],
        [*parts, middle, vectors, turn],
        grid=(rows // block,),
        specs=([by_rows, by_rows, by_rows, whole, whole], [by_rows]),
    )[0]


def together(*values):
    return lax.optimization_barrier(values)


def per_device(
    tokens,
    embed_table,
    qkv_weight,
    qv_bias,
    out_weight,
    out_bias,
    norm1_gain,
    norm1_bias,
    in_weight,
    in_bias,
    down_weight,
    down_bias,
    norm2_gain,
    norm2_bias,
    masked_pos,
    replace_ids,
    masked_count,
    cotangent,
):
    size, cores = lax.axis_size("dp"), lax.axis_size("mp")
    me, core = lax.axis_index("dp"), lax.axis_index("mp")
    page_count, slot_count = masked_pos.shape
    length = tokens.shape[0] // page_count
    width = tokens.shape[1]
    shard_rows = width // size
    cut = size // 8
    table_rows = embed_table.shape[0]
    pages = page_count
    rows = pages * length
    own_slots = page_count // cores * slot_count
    slots = pages * slot_count
    head_cols = qkv_weight.shape[2]
    hidden_cols = in_weight.shape[1]
    far = far_digits(size)

    def to_core(values, step):
        pairs = [(c, (c + step) % cores) for c in range(cores)]
        return lax.ppermute(values, "mp", pairs)

    def from_cores(values):
        return [values] + [to_core(values, k) for k in range(1, cores)]

    def in_core_order(parts):
        whole = jnp.concatenate([parts[-k % cores] for k in range(cores)], axis=0)
        for at in range(1, cores):
            turned = jnp.concatenate([parts[(at - k) % cores] for k in range(cores)], axis=0)
            whole = jnp.where(core == at, turned, whole)
        return whole

    def own_pages(values):
        per = values.shape[0] // cores
        return lax.dynamic_slice_in_dim(values, core * per, per, 0)

    def spread_far(shard):
        blocks = [shard]
        for digit in far:
            packed = blocks[0] if len(blocks) == 1 else jnp.concatenate(blocks, axis=0)
            count = len(blocks)
            for step in range(1, digit[0]):
                got = send(packed, size, digit, step)
                blocks = blocks + [
                    got[k * shard_rows : (k + 1) * shard_rows] for k in range(count)
                ]
        return blocks

    def last_of(halves):
        pieces = []
        for half, pair in enumerate(halves):
            pieces += [*pair, *[send(part, size, NEAR[1 - half], 1) for part in pair]]
        return pieces

    def spread_near(blocks):
        halves = stack_rows([blocks[:cut], blocks[cut:]])
        return [(part, send(part, size, digit, 1)) for part, digit in zip(halves, NEAR)]

    def spread_last(halves):
        here = stack_rows([list(pair) for pair in halves])
        return here, [send(here[half], size, NEAR[1 - half], 1) for half in range(2)]

    def in_order(here, there):
        return [p for pair in zip(here, there) for p in pair]

    def halved(parts):
        middle = parts[0].shape[0] // 2
        sums = []
        for at in (slice(0, middle), slice(middle, None)):
            total = parts[0][at].astype(F32)
            for part in parts[1:]:
                total = total + part[at].astype(F32)
            sums.append(total.astype(BF))
        return sums

    def sum_first(pieces):
        return [
            (pieces[2 * half], send(pieces[2 * half + 1], size, NEAR[1 - half], 1))
            for half in range(2)
        ]

    def sum_second(*sums):
        done = []
        for half in range(2):
            both = zip(*[halved(halves[half]) for halves in sums])
            stay, leave_ = (jnp.concatenate(parts, axis=1) for parts in both)
            done.append((stay, send(leave_, size, NEAR[half], 1)))
        return done

    def sum_far(halves):
        blocks = []
        for stay, came in halves:
            for k in range(cut):
                here = slice(k * shard_rows, (k + 1) * shard_rows)
                blocks.append((stay[here].astype(F32) + came[here].astype(F32)).astype(BF))
        for digit in far[:0:-1]:
            blocks = [add_up(terms).astype(BF) for terms in spread_fold(blocks, digit)]
        return spread_fold(blocks, far[0])[0]

    def spread_fold(blocks, digit):
        radix = digit[0]
        inner = len(blocks) // radix
        terms = [[block] for block in blocks[:inner]]
        for step in range(1, radix):
            group = blocks[step * inner : (step + 1) * inner]
            packed = group[0] if inner == 1 else jnp.concatenate(group, axis=0)
            got = send(packed, size, digit, radix - step)
            for k in range(inner):
                terms[k].append(got[k * shard_rows : (k + 1) * shard_rows])
        return terms

    def add_up(terms):
        total = terms[0].astype(F32)
        for term in terms[1:]:
            total = total + term.astype(F32)
        return total

    pad = -(slot_count + 1) % 128
    packed_ids = jnp.concatenate(
        [replace_ids, masked_count[:, None], jnp.zeros((page_count, pad), jnp.int32)], axis=1
    )
    packed_ids = jnp.broadcast_to(packed_ids[None], (size, *packed_ids.shape))
    heads_shard = jnp.concatenate(
        [qkv_weight.reshape(shard_rows, 3 * head_cols), out_weight.T], axis=1
    )
    heads_far = spread_far(heads_shard)

    places = jnp.stack([me, core])
    used = jnp.arange(slot_count)[None, :] < masked_count[:, None]
    codes = jnp.where(used, replace_ids, -1)
    own_codes = own_pages(codes).reshape(1, own_slots)
    held_rows = held_order(size, shard_rows, me)[None, :]
    turn, turned_tokens, sent_hot = prepare(tokens, held_rows, own_codes, size, table_rows)
    packed_ids, turned_tokens, sent_hot, heads_far, in_shard = together(
        packed_ids, turned_tokens, sent_hot, heads_far, in_weight
    )

    all_ids = lax.all_to_all(packed_ids, "dp", 0, 0)
    heads_near = spread_near(heads_far)
    in_far = spread_far(in_shard)
    down_shard = down_weight.T
    vectors = jnp.stack(
        [out_bias, norm1_gain, norm1_bias, down_bias, norm2_gain, norm2_bias] + [out_bias] * 2
    )
    round_turn, _ = together(turn, in_shard)
    sents = from_cores(sent_hot)
    grad_final, vectors = turn_small(
        cotangent.reshape(slots, width), codes, vectors, round_turn
    )
    hidden_bias = in_bias[None]
    all_ids, heads_near, in_far, down_shard, grad_final = together(
        all_ids, heads_near, in_far, down_shard, grad_final
    )

    is_used = jnp.arange(slot_count)[None, None, :] < all_ids[:, :, slot_count : slot_count + 1]
    all_codes = jnp.where(is_used, all_ids[:, :, :slot_count], -1)
    all_codes = all_codes.reshape(size * cores, own_slots)
    *hots, found, fullest = serve(places, all_codes, embed_table, size, cores)
    found, heads_near, in_far = together(found, heads_near, in_far)
    found = lax.all_to_all(found.reshape(size, ROOM, width), "dp", 0, 0)
    found = found.reshape(size * ROOM, width)
    heads_here, heads_there = spread_last(heads_near)
    down_far = spread_far(down_shard)
    in_near = spread_near(in_far)

    rounds = (fullest.reshape(()) + ROOM - 1) // ROOM

    def round_of(turn_, held):
        own, every, held = lax.optimization_barrier((own_codes[0], all_codes, held))
        low = turn_ * ROOM
        spots = jnp.arange(own_slots)
        before = (spots[:, None] < spots[None, :]).astype(BF)
        to_owner = (own >= 0)[:, None] & (own[:, None] // table_rows == jnp.arange(size))
        rank = tn(before, to_owner.astype(BF)).astype(jnp.int32) - low
        sent = (rank[:, :, None] == jnp.arange(ROOM)) & to_owner[:, :, None]
        sent = sent.astype(BF).reshape(own_slots, size * ROOM)
        mine = (every >= 0) & (every // table_rows == me)
        rank = dot(mine.astype(BF), before).astype(jnp.int32) - low
        hit = (rank[:, None, :] == jnp.arange(ROOM)[None, :, None]) & mine[:, None, :]
        asked = jnp.sum(jnp.where(hit, every[:, None, :] - me * table_rows + 1, 0), axis=2) - 1
        hot = (asked[:, :, None] == jnp.arange(table_rows)).astype(BF)
        hot = hot.reshape(size, cores, ROOM, table_rows)
        turned = [
            lax.dynamic_index_in_dim(hot, (core + cores - k) % cores, 1, keepdims=False)
            for k in range(cores)
        ]
        return sent, [t.reshape(size * ROOM, table_rows) for t in turned], held

    def more_rows(turn_, held):
        sent, later, held = round_of(turn_, held)
        got = dot(later[0], embed_table).astype(BF).reshape(size, ROOM, width)
        got = lax.all_to_all(got, "dp", 0, 0).reshape(size * ROOM, width)
        return held + in_core_order(from_cores(dot(sent, got).astype(BF)))

    more = lax.fori_loop(1, rounds, more_rows, jnp.zeros((slots, width), F32))
    founds = from_cores(found)
    heads_pieces = in_order(heads_here, heads_there)
    embedded, low, query, key, value, s_embedded, s_low, s_query, s_attended, s_part = enter(
        places,
        turned_tokens,
        founds,
        sents,
        more,
        turn,
        masked_pos,
        qv_bias,
        heads_pieces,
    )
    down_near = spread_near(down_far)
    in_here, in_there = spread_last(in_near)
    s_part, down_near, in_here, in_there, query = together(
        s_part, down_near, in_here, in_there, query
    )

    down_pieces = last_of(down_near)
    s_parts = from_cores(s_part)
    rows_part = attend_all(query, key, value, heads_pieces, pages)
    s_parts, down_pieces, rows_part = together(s_parts, down_pieces, rows_part)

    in_pieces = in_order(in_here, in_there)
    unit1, scale1, middle_low, hidden, slope, s_part = slot_forward(
        s_parts, s_embedded, vectors, hidden_bias, in_pieces, down_pieces
    )
    s_parts = from_cores(s_part)
    *grad_down, grad_r2, grad_hidden_in, small2, grad_in_bias, s_part = slot_turn(
        s_parts, hidden, slope, unit1, grad_final, vectors, in_pieces, down_pieces
    )
    s_part, rows_part = together(s_part, rows_part)

    s_parts = from_cores(s_part)
    rows_parts = from_cores(rows_part)
    down_sum = sum_first(grad_down)
    grad_in = in_grad(middle_low, grad_hidden_in, [p.shape[0] for p in in_pieces])
    s_parts, grad_in = together(s_parts, grad_in)

    in_sum = sum_first(grad_in)
    *grad_heads, grad_r1, part, small1, small0 = slot_back(
        s_parts,
        grad_r2,
        unit1,
        scale1,
        s_attended,
        s_query,
        key,
        value,
        s_low,
        low,
        vectors,
        masked_pos,
        heads_pieces,
    )
    down_sum, in_sum, grad_heads, part, rows_parts = together(
        down_sum, in_sum, grad_heads, part, rows_parts
    )

    heads_sum = sum_first(grad_heads)
    units_sum = sum_second(down_sum, in_sum)
    parts = from_cores(part)
    middle, rows_part = rows_forward(
        rows_parts, embedded, vectors, hidden_bias, in_pieces, down_pieces
    )
    parts, rows_part = together(parts, rows_part)
    grad_input, moved, own_grad = leave(
        places,
        parts,
        grad_r1,
        masked_pos,
        turn,
        held_rows,
        sent_hot,
        [small1, small2, small0, grad_in_bias],
        size,
    )

    gots = lax.all_to_all(moved, "dp", 0, 0)
    units_sum = sum_far(units_sum)
    heads_sum = sum_second(heads_sum)
    output = rows_end(from_cores(rows_part), middle, vectors, turn)
    units_sum, heads_sum, output, gots = together(units_sum, heads_sum, output, gots)

    heads_sum = sum_far(heads_sum)
    grad_table, totals = collect(hots, from_cores(gots))
    units_share = add_up(units_sum)
    down_share, in_share = units_share[:, :hidden_cols].T, units_share[:, hidden_cols:]
    def more_table(turn_, held):
        sent, later, held = round_of(turn_, held)
        got = tn(sent, own_grad).astype(BF).reshape(size, ROOM, width)
        for hot, block in zip(later, from_cores(lax.all_to_all(got, "dp", 0, 0))):
            held = held + tn(hot, block.reshape(size * ROOM, width))
        return held

    grad_table = lax.fori_loop(1, rounds, more_table, grad_table)
    def piece(row, block, count):
        return totals[row, block * 128 : block * 128 + count]

    vec = [piece(0, k, shard_rows) for k in range(6)]
    own = [
        piece(1, 0, head_cols // size),
        piece(1, 1, head_cols // size),
        piece(1, 2, hidden_cols // size),
    ]
    heads_sum, in_share, down_share, grad_table, vec, own = together(
        heads_sum, in_share, down_share, grad_table, vec, own
    )
    heads_share = add_up(heads_sum)
    qkv_share = heads_share[:, : 3 * head_cols].reshape(shard_rows, 3, head_cols)
    out_share = heads_share[:, 3 * head_cols :].T


    return (
        output,
        grad_input,
        grad_table,
        qkv_share,
        jnp.stack([own[0], own[1]])[:, None, :],
        out_share,
        vec[0],
        vec[1],
        vec[2],
        in_share,
        own[2][None],
        down_share,
        vec[3],
        vec[4],
        vec[5],
    )


def solution(mesh):
    in_specs = (
        P("dp", None),
        P("dp", None),
        P("dp", None, "mp"),
        P(None, "mp"),
        P("mp", "dp"),
        P(),
        P(),
        P(),
        P("dp", "mp"),
        P("mp"),
        P("mp", "dp"),
        P(),
        P(),
        P(),
        P("dp", None),
        P("dp", None),
        P("dp"),
        P("dp", None, None),
    )
    out_specs = (
        P("dp", None),
        P("dp", None),
        P("dp", None),
        P("dp", None, "mp"),
        P(None, "mp", "dp"),
        P("mp", "dp"),
        P("dp"),
        P("dp"),
        P("dp"),
        P("dp", "mp"),
        P("mp", "dp"),
        P("mp", "dp"),
        P("dp"),
        P("dp"),
        P("dp"),
    )
    return jax.shard_map(
        per_device, mesh=mesh, in_specs=in_specs, out_specs=out_specs, check_vma=False
    )
```

```python
import jax
import jax.numpy as jnp
import numpy as np
from jax import lax
from jax.experimental import pallas as pl
from jax.experimental.pallas import tpu as pltpu
from jax.sharding import PartitionSpec as P

HEAD = 64
EPSILON = 1e-05
ROOM = 16
EXTRA = 8

BF = jnp.bfloat16
F32 = jnp.float32


def dot(a, b, dims=((1,), (0,)), **kw):
    return lax.dot_general(a, b, (dims, ((), ())), preferred_element_type=F32, **kw)


def nt(a, b):
    return dot(a, b, ((1,), (1,)))


def tn(a, b):
    return dot(a, b, ((0,), (0,)))


def split_two(values):
    high = values.astype(BF)
    return high, (values - high.astype(F32)).astype(BF)


def far_digits(size):
    found = []
    stride, rest = 4, size // 4
    while rest > 1:
        radix = next(r for r in (4, 2, 3, 5, 7, rest) if rest % r == 0)
        found.append((radix, stride))
        stride, rest = stride * radix, rest // radix
    return found


NEAR = ((2, 1), (2, 2))


def shift(size, digit, step):
    radix, stride = digit
    pairs = []
    for src in range(size):
        own = (src // stride) % radix
        pairs.append((src, src + ((own + step) % radix - own) * stride))
    return pairs


def send(values, size, digit, step):
    return lax.ppermute(values, "dp", shift(size, digit, step))


def held_order(size, rows, me):
    blocks = size // 8
    place = jnp.arange(size * rows)
    second = place >= size * rows // 2
    slot, row = (place % (size * rows // 2)) // rows, place % rows
    block = slot % blocks + jnp.where(second, blocks, 0)
    low, high = (slot // blocks) % 2, slot // blocks // 2
    owner = jnp.zeros_like(place)
    for radix, stride in far_digits(size):
        owner = owner + ((me // stride - block % radix) % radix) * stride
        block = block // radix
    x_step, y_step = jnp.where(second, high, low), jnp.where(second, low, high)
    owner = owner + (me - x_step) % 2 + ((me // 2 - y_step) % 2) * 2
    return owner * rows + row


VMEM_LIMIT = 20 * 1024 * 1024


def kernel_call(body, outs, inputs, far_count=0, scratch=(), flops=0, grid=None, specs=None):
    near = len(inputs) - far_count
    in_specs, out_specs = specs or (
        [pl.BlockSpec(memory_space=pltpu.VMEM)] * near,
        [pl.BlockSpec(memory_space=pltpu.VMEM)] * len(outs),
    )
    return pl.pallas_call(
        body,
        grid=grid or (),
        out_shape=outs,
        in_specs=[*in_specs, *([pl.BlockSpec(memory_space=pl.ANY)] * far_count)],
        out_specs=out_specs,
        scratch_shapes=scratch,
        compiler_params=pltpu.CompilerParams(vmem_limit_bytes=VMEM_LIMIT),
        cost_estimate=pl.CostEstimate(flops=1, bytes_accessed=1, transcendentals=0),
    )(*inputs)


def shape(rows, cols, dtype):
    return jax.ShapeDtypeStruct((rows, cols), dtype)


def fill(pieces, held, sems, start=0):
    copies, at = [], 0
    for i, piece in enumerate(pieces):
        rows = piece.shape[0]
        source = piece.at[:, pl.ds(start, held.shape[1])]
        copy = pltpu.make_async_copy(source, held.at[pl.ds(at, rows)], sems.at[i])
        copy.start()
        copies.append(copy)
        at += rows

    def wait():
        for copy in copies:
            copy.wait()

    return wait


def held_scratch(pieces, cols=None):
    rows = sum(p.shape[0] for p in pieces)
    return [
        pltpu.VMEM((rows, cols or pieces[0].shape[1]), BF),
        pltpu.SemaphoreType.DMA((len(pieces),)),
    ]


def norm_stats(values):
    row_mean = jnp.mean(values, axis=-1, keepdims=True)
    centered = values - row_mean
    scale = lax.rsqrt(jnp.mean(centered * centered, axis=-1, keepdims=True) + EPSILON)
    return centered * scale, scale


def norm_back(grad, unit, scale, gain):
    inner = grad * gain
    mean_inner = jnp.mean(inner, axis=-1, keepdims=True)
    mean_unit = jnp.mean(inner * unit, axis=-1, keepdims=True)
    return (
        scale * (inner - mean_inner - unit * mean_unit),
        jnp.sum(grad * unit, axis=0, keepdims=True),
        jnp.sum(grad, axis=0, keepdims=True),
    )


def gelu(values):
    return values * (0.5 + 0.5 * lax.erf(values * (0.5**0.5)))


def gelu_both(values):
    normal = 0.5 + 0.5 * lax.erf(values * (0.5**0.5))
    bell = jnp.exp(-0.5 * values * values) * (0.5 / np.pi) ** 0.5
    return values * normal, normal + values * bell


def head_masks(dtype):
    lane = lax.broadcasted_iota(jnp.int32, (1, 2 * HEAD), 1)
    return [(lane // HEAD == h).astype(dtype) for h in range(2)]


def attend_pair(query, key, value):
    lanes = value.shape[1]
    wider = jnp.concatenate([value, jnp.ones_like(value)], axis=1)
    outs = []
    for mask in head_masks(BF):
        scores = nt(query * mask, key)
        powers = jnp.exp(scores - jnp.max(scores, axis=-1, keepdims=True))
        both = dot(powers.astype(BF), wider)
        outs.append(both[:, :lanes] / both[:, lanes:])
    first, second = head_masks(F32)
    return (outs[0] * first + outs[1] * second).astype(BF)


def one_hot_rows(row_of_line, rows):
    at = lax.broadcasted_iota(jnp.int32, (rows, row_of_line.shape[1]), 0)
    return (at == row_of_line).astype(F32).astype(BF)


def one_hot_slots(row_of_column, rows):
    at = lax.broadcasted_iota(jnp.int32, (row_of_column.shape[0], rows), 1)
    return (at == row_of_column).astype(F32).astype(BF)


def as_column(line):
    count = line.shape[1]
    square = (count, count)
    same = lax.broadcasted_iota(jnp.int32, square, 0) == lax.broadcasted_iota(jnp.int32, square, 1)
    return jnp.sum(jnp.where(same, line.astype(F32), 0.0), axis=1, keepdims=True)


def floor_by(values, divisor):
    return jnp.floor((values + 0.5) * (1.0 / divisor))


def iota(dims, axis):
    return lax.broadcasted_iota(jnp.int32, dims, axis).astype(F32)


def serve(places, codes, table, size, cores):
    table_rows, width = table.shape
    devices, slots = codes.shape
    count = size * ROOM

    def body(place, code, tab, *outs):
        *hots, found, most = outs
        me, core = place[0], place[1]
        line = code[...].astype(F32)
        local = line - (me * table_rows).astype(F32)
        mine = (local >= 0) & (local < table_rows)
        before = (iota((slots, slots), 0) < iota((slots, slots), 1)).astype(BF)
        rank = dot(mine.astype(F32).astype(BF), before)
        rank = jnp.where(mine & (rank < ROOM), rank, 255.0).astype(BF)
        local = jnp.where(mine, local, 0.0)
        local_high = floor_by(local, 256)
        local_low = (local - 256 * local_high).astype(BF)
        local_high = local_high.astype(BF)
        source = floor_by(iota((count, 1), 0), ROOM)
        room = iota((count, 1), 0) - ROOM * source
        for k in range(cores):
            which = lax.rem(core + cores - k, cores).astype(F32)
            pick = (iota((count, devices), 1) == source * cores + which).astype(F32).astype(BF)
            hit = dot(pick, rank) == room
            at = 256 * dot(pick, local_high) + dot(pick, local_low) + 1.0
            asked = jnp.sum(jnp.where(hit, at, 0.0), axis=1, keepdims=True) - 1.0
            hots[k][...] = (iota((count, table_rows), 1) == asked).astype(F32).astype(BF)
        found[...] = dot(hots[0][...], tab[...]).astype(BF)
        owner = floor_by(line, table_rows)
        fullest = jnp.zeros((devices, 1), F32)
        for o in range(size):
            here = jnp.sum(jnp.where(owner == o, 1.0, 0.0), axis=1, keepdims=True)
            fullest = jnp.maximum(fullest, here)
        fullest = jnp.max(fullest, axis=0, keepdims=True)
        most[...] = fullest.astype(jnp.int32)

    smem, vmem = pl.BlockSpec(memory_space=pltpu.SMEM), pl.BlockSpec(memory_space=pltpu.VMEM)
    return kernel_call(
        body,
        [
            *[shape(count, table_rows, BF)] * cores,
            shape(count, width, BF),
            shape(1, 1, jnp.int32),
        ],
        [places, codes, table],
        flops=2 * count * table_rows * width,
        specs=([smem, vmem, vmem], [vmem] * (cores + 2)),
    )


def by_owner(values, owner, place, size):
    count = values.shape[1]
    hit = (iota((size, count), 0) == owner).astype(F32)
    rows = jnp.concatenate([hit * values[r : r + 1] for r in range(values.shape[0])], axis=0)
    hot = (iota((128, count), 0) == place).astype(F32).astype(BF)
    total, rest = 0.0, rows
    for _ in range(3):
        high = rest.astype(BF)
        rest = rest - high.astype(F32)
        total = total + nt(high, hot)
    return total


def stack_rows(groups):
    if any(part.shape[0] % 16 for group in groups for part in group):
        return [jnp.concatenate(group, axis=0) for group in groups]

    def body(*refs):
        at = 0
        for out, group in zip(refs[len(refs) - len(groups) :], groups):
            start = 0
            for part in group:
                out[start : start + part.shape[0]] = refs[at][...]
                start, at = start + part.shape[0], at + 1

    outs = [shape(sum(p.shape[0] for p in group), group[0].shape[1], BF) for group in groups]
    return kernel_call(body, outs, [part for group in groups for part in group])


def prepare(tokens, order, codes, size, table_rows):
    rows, width = tokens.shape
    slots = codes.shape[1]

    def body(tok, order_, code, turn, tok_out, sent):
        turn[...] = (
            (lax.broadcasted_iota(jnp.int32, (width, width), 0) == order_[...])
            .astype(F32)
            .astype(BF)
        )
        line = code[...].astype(F32)
        column = as_column(line)
        owner_line, owner = floor_by(line, table_rows), floor_by(column, table_rows)
        square = (slots, slots)
        earlier = (iota(square, 1) < iota(square, 0)) & (owner_line == owner)
        rank = jnp.sum(jnp.where(earlier, 1.0, 0.0), axis=1, keepdims=True)
        target = jnp.where((column >= 0) & (rank < ROOM), owner * ROOM + rank, -1.0)
        sent[...] = (iota((slots, size * ROOM), 1) == target).astype(F32).astype(BF)
        tok_out[...] = dot(tok[...], turn[...]).astype(BF)

    return kernel_call(
        body,
        [shape(width, width, BF), shape(rows, width, BF), shape(slots, size * ROOM, BF)],
        [tokens, order, codes],
    )


def turn_small(cotangent, codes, vectors, turn):
    slots, width = cotangent.shape

    def body(cot, code, vec, turn_, cot_out, vec_out):
        pages, per = code.shape
        for g in range(pages):
            here = slice(g * per, (g + 1) * per)
            used = (as_column(code[g : g + 1]) >= 0).astype(F32).astype(BF)
            cot_out[here] = dot(cot[here] * used, turn_[...]).astype(BF)
        rest, total = vec[...], 0.0
        for _ in range(3):
            high = rest.astype(BF)
            rest = rest - high.astype(F32)
            total = total + dot(high, turn_[...])
        vec_out[...] = total

    return kernel_call(
        body,
        [shape(slots, width, BF), shape(vectors.shape[0], width, F32)],
        [cotangent, codes, vectors, turn],
    )


def enter(places, tokens, founds, sents, more, turn, pos, qv_bias, pieces):
    rows, width = tokens.shape
    pages, per = pos.shape
    slots, cores = pages * per, len(founds)
    own = sents[0].shape[0]
    near = 6 + 2 * cores
    cols = qv_bias.shape[1]
    length = rows // pages

    def body(*refs):
        place_, tok, more_, turn_, pos_, bias_ = refs[:6]
        found, sent = refs[6 : 6 + cores], refs[6 + cores : near]
        piece_refs = refs[near : near + len(pieces)]
        (
            emb,
            low,
            q,
            k,
            v,
            s_emb,
            s_low,
            s_q,
            s_att,
            s_out,
            fetched,
            held,
            sems,
        ) = refs[near + len(pieces) :]
        wait = fill(piece_refs, held, sems)
        for c in range(cores):
            start = pl.multiple_of(lax.rem(place_[1] + cores - c, cores) * own, own)
            fetched[pl.ds(start, own)] = dot(sent[c][...], found[c][...])
        fetched[...] += more_[...]
        new = dot(fetched[...].astype(BF), turn_[...]).astype(BF)
        hots = []
        for g in range(pages):
            page, here = slice(g * length, (g + 1) * length), slice(g * per, (g + 1) * per)
            placed = one_hot_rows(pos_[g : g + 1], length)
            hot = one_hot_slots(as_column(pos_[g : g + 1]), length)
            hots.append(hot)
            exact = tok[page].astype(F32) + dot(placed, new[here])
            emb[page] = exact
            low[page] = exact.astype(BF)
            s_emb[here] = dot(hot, tok[page]) + new[here].astype(F32)
        s_low[...] = s_emb[...].astype(BF)
        wait()
        for g in range(pages):
            page, here = slice(g * length, (g + 1) * length), slice(g * per, (g + 1) * per)
            q[page] = (dot(low[page], held[:, :cols]) + bias_[0:1]).astype(BF)
            k[page] = dot(low[page], held[:, cols : 2 * cols]).astype(BF)
            v[page] = (dot(low[page], held[:, 2 * cols : 3 * cols]) + bias_[1:2]).astype(BF)
            s_q[here] = dot(hots[g], q[page]).astype(BF)
            for j in range(0, cols, 2 * HEAD):
                at = slice(j, j + 2 * HEAD)
                s_att[here, at] = attend_pair(s_q[here, at] * HEAD**-0.5, k[page, at], v[page, at])
        s_out[...] = nt(s_att[...], held[:, 3 * cols :])

    outs = [
        shape(rows, width, F32),
        shape(rows, width, BF),
        *[shape(rows, cols, BF)] * 3,
        shape(slots, width, F32),
        shape(slots, width, BF),
        *[shape(slots, cols, BF)] * 2,
        shape(slots, width, F32),
    ]
    return kernel_call(
        body,
        outs,
        [places, tokens, more, turn, pos, qv_bias, *founds, *sents, *pieces],
        len(pieces),
        [pltpu.VMEM((slots, width), F32), *held_scratch(pieces)],
        specs=(
            [
                pl.BlockSpec(memory_space=pltpu.SMEM),
                *([pl.BlockSpec(memory_space=pltpu.VMEM)] * (near - 1)),
            ],
            [pl.BlockSpec(memory_space=pltpu.VMEM)] * len(outs),
        ),
    )


def attend_all(query, key, value, pieces, pages):
    rows, cols = query.shape
    length, pairs = rows // pages, cols // (2 * HEAD)
    width = sum(p.shape[0] for p in pieces)

    def body(q, k, v, *refs):
        out, total, held, sems = refs[len(pieces) :]
        first, pair = pl.program_id(0) == 0, pl.program_id(1)

        @pl.when(first & (pair == 0))
        def _():
            fill(refs[: len(pieces)], held, sems, 3 * cols)()

        half = length // 2
        for part in range(2):
            here = slice(part * half, (part + 1) * half)
            attended = attend_pair(q[here] * HEAD**-0.5, k[...], v[...])
            at = pl.ds(pl.multiple_of(pair * 2 * HEAD, 2 * HEAD), 2 * HEAD)
            total[here, at] = attended

        @pl.when(pair == pairs - 1)
        def _():
            out[...] = nt(total[...], held[...]).astype(BF)

    spec = pl.BlockSpec((length, 2 * HEAD), lambda g, j: (g, j))
    return kernel_call(
        body,
        [shape(rows, width, BF)],
        [query, key, value, *pieces],
        len(pieces),
        [pltpu.VMEM((length, cols), BF), *held_scratch(pieces, cols)],
        grid=(pages, pairs),
        specs=([spec] * 3, [pl.BlockSpec((length, width), lambda g, j: (g, 0))]),
    )[0]


def slot_forward(parts, embedded, vectors, bias, in_pieces, down_pieces):
    slots, width = embedded.shape
    wide = in_pieces[0].shape[1]
    count, total_count = len(in_pieces), len(in_pieces) + len(down_pieces)

    def body(first, second, emb, vec, bias_, *refs):
        unit1, scale1, mid_low, hid, slope, part, held, sems, held2, sems2 = refs[total_count:]
        wait = fill(refs[:count], held, sems)
        wait2 = fill(refs[count:total_count], held2, sems2)
        unit, scale = norm_stats(emb[...] + vec[0:1] + (first[...] + second[...]))
        unit1[...] = unit
        scale1[...] = jnp.broadcast_to(scale, scale1.shape)
        mid_low[...] = (unit * vec[1:2] + vec[2:3]).astype(BF)
        wait()
        value, rate = gelu_both(dot(mid_low[...], held[...]) + bias_[...])
        hid[...] = value.astype(BF)
        slope[...] = rate
        wait2()
        part[...] = nt(hid[...], held2[...])

    outs = [
        shape(slots, width, F32),
        shape(slots, 128, F32),
        shape(slots, width, BF),
        shape(slots, wide, BF),
        shape(slots, wide, F32),
        shape(slots, width, F32),
    ]
    return kernel_call(
        body,
        outs,
        [*parts, embedded, vectors, bias, *in_pieces, *down_pieces],
        total_count,
        [*held_scratch(in_pieces), *held_scratch(down_pieces)],
    )


def put_rows(outs, start, values):
    at = 0
    for out in outs:
        rows = out.shape[0]
        out[:, start : start + values.shape[1]] = values[at : at + rows].astype(BF)
        at += rows


def slot_turn(parts, hidden, slope, unit1, grad_final, vectors, in_pieces, down_pieces):
    slots, width = unit1.shape
    wide = hidden.shape[1]
    count, total_count = len(in_pieces), len(in_pieces) + len(down_pieces)

    def body(first, second, hid, slp, un1, final, vec, *refs):
        (*grads, grad2, ghin, small, in_small, mid, held, sems, held2, sems2) = refs[total_count:]
        wait = fill(refs[:count], held, sems)
        wait2 = fill(refs[count:total_count], held2, sems2)
        total = un1[...] * vec[1:2] + vec[2:3] + vec[3:4] + (first[...] + second[...])
        unit, scale = norm_stats(total)
        grad, gain, bias = norm_back(final[...].astype(F32), unit, scale, vec[4:5])
        grad2[...] = grad
        grad_low = grad.astype(BF)
        small[0:1] = jnp.sum(grad_low.astype(F32), axis=0, keepdims=True)
        small[1:2] = gain
        small[2:3] = bias
        small[3:8] = jnp.zeros((5, width), F32)
        wait2()
        back = (dot(grad_low, held2[...]) * slp[...]).astype(BF)
        ghin[...] = back
        in_small[...] = jnp.sum(back.astype(F32), axis=0, keepdims=True)
        wait()
        mid[...] = nt(back, held[...])
        put_rows(grads, 0, tn(grad_low, hid[...]))

    outs = [
        *[shape(p.shape[0], wide, BF) for p in in_pieces],
        shape(slots, width, F32),
        shape(slots, wide, BF),
        shape(8, width, F32),
        shape(1, wide, F32),
        shape(slots, width, F32),
    ]
    return kernel_call(
        body,
        outs,
        [*parts, hidden, slope, unit1, grad_final, vectors, *in_pieces, *down_pieces],
        total_count,
        [*held_scratch(in_pieces), *held_scratch(down_pieces)],
    )


def in_grad(mid_low, ghin, heights):
    def body(mid, gh, *grads):
        put_rows(grads, 0, tn(mid[...], gh[...]))

    return kernel_call(body, [shape(r, ghin.shape[1], BF) for r in heights], [mid_low, ghin])


def slot_back(parts, grad2, unit1, scale1, attended, s_query, key, value, s_low, low, vectors, pos, pieces):
    slots, width = unit1.shape
    rows, cols = key.shape
    pages, per = pos.shape
    length = rows // pages
    scale = HEAD**-0.5

    def body(first, second, g2, un1, sc1, att, sq, k, v, sl, lo, vec, pos_, *refs):
        (*grads, grad1, part, small, small_heads, gq, gk, gv, held, sems) = refs[len(pieces) :]
        wait = fill(refs[: len(pieces)], held, sems)
        total = g2[...] + (first[...] + second[...])
        grad, gain, bias = norm_back(total, un1[...], sc1[:, :1], vec[1:2])
        grad1[...] = grad
        grad_low = grad.astype(BF)
        small[0:1] = jnp.sum(grad_low.astype(F32), axis=0, keepdims=True)
        small[1:2] = gain
        small[2:3] = bias
        small[3:8] = jnp.zeros((5, width), F32)
        put_rows(grads, 3 * cols, tn(grad_low, att[...]))
        wait()
        gatt = dot(grad_low, held[:, 3 * cols :]).astype(BF)
        masks = head_masks(BF)
        left_lanes, right_lanes = head_masks(F32)
        for g in range(pages):
            here, page = slice(g * per, (g + 1) * per), slice(g * length, (g + 1) * length)
            for j in range(0, cols, 2 * HEAD):
                at = slice(j, j + 2 * HEAD)
                query, back = sq[here, at], gatt[here, at]
                keys, values = k[page, at], v[page, at]
                got = []
                for mask in masks:
                    scores = nt(query * mask * scale, keys)
                    powers = jnp.exp(scores - jnp.max(scores, axis=-1, keepdims=True))
                    prob = powers * (1.0 / jnp.sum(powers, axis=-1, keepdims=True))
                    grad_prob = nt(back * mask, values)
                    inner = jnp.sum(prob * grad_prob, axis=-1, keepdims=True)
                    grad_scores = (prob * (grad_prob - inner)).astype(BF)
                    got.append(
                        (
                            dot(grad_scores, keys),
                            tn(grad_scores, query),
                            tn(prob.astype(BF), back),
                        )
                    )
                left, right = got
                gq[here, at] = ((left[0] * left_lanes + right[0] * right_lanes) * scale).astype(BF)
                gk[page, at] = ((left[1] * left_lanes + right[1] * right_lanes) * scale).astype(BF)
                gv[page, at] = (left[2] * left_lanes + right[2] * right_lanes).astype(BF)
        small_heads[0:1] = jnp.sum(gq[...].astype(F32), axis=0, keepdims=True)
        small_heads[1:2] = jnp.sum(gv[...].astype(F32), axis=0, keepdims=True)
        small_heads[2:8] = jnp.zeros((6, cols), F32)
        put_rows(grads, 0, tn(sl[...], gq[...]))
        put_rows(grads, cols, tn(lo[...], gk[...]))
        put_rows(grads, 2 * cols, tn(lo[...], gv[...]))
        high, rest = split_two(nt(gq[...], held[:, :cols]))
        for g in range(pages):
            here, page = slice(g * per, (g + 1) * per), slice(g * length, (g + 1) * length)
            placed = one_hot_rows(pos_[g : g + 1], length)
            total = nt(gk[page], held[:, cols : 2 * cols]) + nt(gv[page], held[:, 2 * cols : 3 * cols])
            total = total + dot(placed, high[here]) + dot(placed, rest[here])
            part[page] = total.astype(BF)

    outs = [
        *[shape(p.shape[0], 4 * cols, BF) for p in pieces],
        shape(slots, width, F32),
        shape(rows, width, BF),
        shape(8, width, F32),
        shape(8, cols, F32),
    ]
    return kernel_call(
        body,
        outs,
        [*parts, grad2, unit1, scale1, attended, s_query, key, value, s_low, low, vectors, pos, *pieces],
        len(pieces),
        [
            pltpu.VMEM((slots, cols), BF),
            *[pltpu.VMEM((rows, cols), BF)] * 2,
            *held_scratch(pieces),
        ],
    )


def leave(places, parts, grad1, pos, turn, order, sent_hot, smalls, size):
    rows, width = parts[0].shape
    pages, per = pos.shape
    length = rows // pages
    own = sent_hot.shape[0] // per
    cols, wide = smalls[2].shape[1], smalls[3].shape[1]

    def body(place_, first, second, g1, pos_, turn_, order_, hot, sm1, sm2, smq, smh, out, moved, mine):
        high, low = split_two(g1[...])
        for g in range(pages):
            page, here = slice(g * length, (g + 1) * length), slice(g * per, (g + 1) * per)
            placed = one_hot_rows(pos_[g : g + 1], length)
            total = first[page].astype(F32) + second[page].astype(F32)
            total = total + dot(placed, high[here]) + dot(placed, low[here])
            near, rest = split_two(total)
            out[page] = nt(near, turn_[...]) + nt(rest, turn_[...])

        place = order_[...].astype(F32)
        owner = floor_by(place, width // size)
        vec = jnp.concatenate([sm1[0:3], sm2[0:3]], axis=0)
        vec = by_owner(vec, owner, place - owner * (width // size), size)
        vec = jnp.concatenate([vec[r * size : (r + 1) * size] for r in range(6)], axis=1)
        at = iota((1, cols), 1)
        owner = floor_by(at, cols // size)
        head = by_owner(smq[0:2], owner, at - owner * (cols // size), size)
        at = iota((1, wide), 1)
        owner = floor_by(at, wide // size)
        unit = by_owner(smh[...], owner, at - owner * (wide // size), size)
        others = jnp.concatenate([head[:size], head[size:], unit], axis=1)
        filler = jnp.zeros((size, width - others.shape[1]), F32)
        others = jnp.concatenate([others, filler], axis=1)
        tails = [p.astype(F32) for values in (vec, others) for p in split_two(values)]
        going = 0.0
        for i in range(own):
            page = place_[1] * own + i
            slot_hot = one_hot_slots(as_column(pos_[pl.ds(page, 1)]), length)
            here = out[pl.ds(pl.multiple_of(page * length, length), length)]
            picked = dot(slot_hot, here.astype(BF)).astype(BF)
            mine[i * per : (i + 1) * per] = picked
            going = going + tn(hot[i * per : (i + 1) * per], picked)
        for s in range(size):
            moved[s, :ROOM] = going[s * ROOM : (s + 1) * ROOM].astype(BF)
            tail = [t[s : s + 1] for t in tails] + [jnp.zeros((EXTRA - len(tails), width), F32)]
            moved[s, ROOM:] = jnp.concatenate(tail, axis=0).astype(BF)

    return kernel_call(
        body,
        [
            shape(rows, width, F32),
            jax.ShapeDtypeStruct((size, ROOM + EXTRA, width), BF),
            shape(own * per, width, BF),
        ],
        [places, *parts, grad1, pos, turn, order, sent_hot, *smalls],
        specs=(
            [
                pl.BlockSpec(memory_space=pltpu.SMEM),
                *([pl.BlockSpec(memory_space=pltpu.VMEM)] * 11),
            ],
            [pl.BlockSpec(memory_space=pltpu.VMEM)] * 3,
        ),
    )


def collect(hots, gots):
    cores, (count, table_rows) = len(hots), hots[0].shape
    size, held, width = gots[0].shape

    def body(*refs):
        hot, got = refs[:cores], refs[cores : 2 * cores]
        table, sums = refs[2 * cores :]
        value = 0.0
        for k in range(cores):
            rows = jnp.concatenate([got[k][s, :ROOM] for s in range(size)], axis=0)
            value = value + tn(hot[k][...], rows)
        table[...] = value
        tail = jnp.zeros((held - ROOM, width), F32)
        for s in range(size):
            tail = tail + got[0][s, ROOM:].astype(F32)
        sums[...] = jnp.concatenate(
            [tail[0:1] + tail[1:2], tail[2:3] + tail[3:4], jnp.zeros((6, width), F32)], axis=0
        )

    return kernel_call(
        body,
        [shape(table_rows, width, F32), shape(8, width, F32)],
        [*hots, *gots],
    )


def rows_forward(parts, embedded, vectors, bias, in_pieces, down_pieces):
    rows, width = embedded.shape
    wide = in_pieces[0].shape[1]
    block = 256 if rows % 256 == 0 else rows
    count, total_count = len(in_pieces), len(in_pieces) + len(down_pieces)

    def body(first, second, emb, vec, bias_, *refs):
        middle, part, held, sems, held2, sems2 = refs[total_count:]

        @pl.when(pl.program_id(0) == 0)
        def _():
            wait = fill(refs[:count], held, sems)
            wait2 = fill(refs[count:total_count], held2, sems2)
            wait()
            wait2()

        total = emb[...] + vec[0:1] + (first[...].astype(F32) + second[...].astype(F32))
        value = norm_stats(total)[0] * vec[1:2] + vec[2:3]
        middle[...] = value
        hidden = dot(value.astype(BF), held[...]) + bias_[...]
        part[...] = nt(gelu(hidden).astype(BF), held2[...]).astype(BF)

    whole = pl.BlockSpec(memory_space=pltpu.VMEM)
    by_rows = pl.BlockSpec((block, width), lambda i: (i, 0))
    return kernel_call(
        body,
        [shape(rows, width, F32), shape(rows, width, BF)],
        [*parts, embedded, vectors, bias, *in_pieces, *down_pieces],
        total_count,
        [*held_scratch(in_pieces), *held_scratch(down_pieces)],
        grid=(rows // block,),
        specs=([by_rows, by_rows, by_rows, whole, whole], [by_rows, by_rows]),
    )


def rows_end(parts, middle, vectors, turn):
    rows, width = middle.shape
    block = 256 if rows % 256 == 0 else rows

    def body(first, second, mid, vec, turn_, out):
        total = mid[...] + vec[3:4] + (first[...].astype(F32) + second[...].astype(F32))
        final = norm_stats(total)[0] * vec[4:5] + vec[5:6]
        out[...] = nt(final.astype(BF), turn_[...]).astype(BF)

    whole = pl.BlockSpec(memory_space=pltpu.VMEM)
    by_rows = pl.BlockSpec((block, width), lambda i: (i, 0))
    return kernel_call(
        body,
        [shape(rows, width, BF)],
        [*parts, middle, vectors, turn],
        grid=(rows // block,),
        specs=([by_rows, by_rows, by_rows, whole, whole], [by_rows]),
    )[0]


def together(*values):
    return lax.optimization_barrier(values)


def per_device(
    tokens,
    embed_table,
    qkv_weight,
    qv_bias,
    out_weight,
    out_bias,
    norm1_gain,
    norm1_bias,
    in_weight,
    in_bias,
    down_weight,
    down_bias,
    norm2_gain,
    norm2_bias,
    masked_pos,
    replace_ids,
    masked_count,
    cotangent,
):
    size, cores = lax.axis_size("dp"), lax.axis_size("mp")
    me, core = lax.axis_index("dp"), lax.axis_index("mp")
    page_count, slot_count = masked_pos.shape
    length = tokens.shape[0] // page_count
    width = tokens.shape[1]
    shard_rows = width // size
    cut = size // 8
    table_rows = embed_table.shape[0]
    pages = page_count
    rows = pages * length
    own_slots = page_count // cores * slot_count
    slots = pages * slot_count
    head_cols = qkv_weight.shape[2]
    hidden_cols = in_weight.shape[1]
    far = far_digits(size)

    def to_core(values, step):
        pairs = [(c, (c + step) % cores) for c in range(cores)]
        return lax.ppermute(values, "mp", pairs)

    def from_cores(values):
        return [values] + [to_core(values, k) for k in range(1, cores)]

    def in_core_order(parts):
        whole = jnp.concatenate([parts[-k % cores] for k in range(cores)], axis=0)
        for at in range(1, cores):
            turned = jnp.concatenate([parts[(at - k) % cores] for k in range(cores)], axis=0)
            whole = jnp.where(core == at, turned, whole)
        return whole

    def own_pages(values):
        per = values.shape[0] // cores
        return lax.dynamic_slice_in_dim(values, core * per, per, 0)

    def spread_far(shard):
        blocks = [shard]
        for digit in far:
            packed = blocks[0] if len(blocks) == 1 else jnp.concatenate(blocks, axis=0)
            count = len(blocks)
            for step in range(1, digit[0]):
                got = send(packed, size, digit, step)
                blocks = blocks + [
                    got[k * shard_rows : (k + 1) * shard_rows] for k in range(count)
                ]
        return blocks

    def last_of(halves):
        pieces = []
        for half, pair in enumerate(halves):
            pieces += [*pair, *[send(part, size, NEAR[1 - half], 1) for part in pair]]
        return pieces

    def spread_near(blocks):
        halves = stack_rows([blocks[:cut], blocks[cut:]])
        return [(part, send(part, size, digit, 1)) for part, digit in zip(halves, NEAR)]

    def spread_last(halves):
        here = stack_rows([list(pair) for pair in halves])
        return here, [send(here[half], size, NEAR[1 - half], 1) for half in range(2)]

    def in_order(here, there):
        return [p for pair in zip(here, there) for p in pair]

    def halved(parts):
        middle = parts[0].shape[0] // 2
        sums = []
        for at in (slice(0, middle), slice(middle, None)):
            total = parts[0][at].astype(F32)
            for part in parts[1:]:
                total = total + part[at].astype(F32)
            sums.append(total.astype(BF))
        return sums

    def sum_first(pieces):
        return [
            (pieces[2 * half], send(pieces[2 * half + 1], size, NEAR[1 - half], 1))
            for half in range(2)
        ]

    def sum_second(*sums):
        done = []
        for half in range(2):
            both = zip(*[halved(halves[half]) for halves in sums])
            stay, leave_ = (jnp.concatenate(parts, axis=1) for parts in both)
            done.append((stay, send(leave_, size, NEAR[half], 1)))
        return done

    def sum_far(halves):
        blocks = []
        for stay, came in halves:
            for k in range(cut):
                here = slice(k * shard_rows, (k + 1) * shard_rows)
                blocks.append((stay[here].astype(F32) + came[here].astype(F32)).astype(BF))
        for digit in far[:0:-1]:
            blocks = [add_up(terms).astype(BF) for terms in spread_fold(blocks, digit)]
        return spread_fold(blocks, far[0])[0]

    def spread_fold(blocks, digit):
        radix = digit[0]
        inner = len(blocks) // radix
        terms = [[block] for block in blocks[:inner]]
        for step in range(1, radix):
            group = blocks[step * inner : (step + 1) * inner]
            packed = group[0] if inner == 1 else jnp.concatenate(group, axis=0)
            got = send(packed, size, digit, radix - step)
            for k in range(inner):
                terms[k].append(got[k * shard_rows : (k + 1) * shard_rows])
        return terms

    def add_up(terms):
        total = terms[0].astype(F32)
        for term in terms[1:]:
            total = total + term.astype(F32)
        return total

    pad = -(slot_count + 1) % 128
    packed_ids = jnp.concatenate(
        [replace_ids, masked_count[:, None], jnp.zeros((page_count, pad), jnp.int32)], axis=1
    )
    packed_ids = jnp.broadcast_to(packed_ids[None], (size, *packed_ids.shape))
    heads_shard = jnp.concatenate(
        [qkv_weight.reshape(shard_rows, 3 * head_cols), out_weight.T], axis=1
    )
    heads_far = spread_far(heads_shard)

    places = jnp.stack([me, core])
    used = jnp.arange(slot_count)[None, :] < masked_count[:, None]
    codes = jnp.where(used, replace_ids, -1)
    own_codes = own_pages(codes).reshape(1, own_slots)
    held_rows = held_order(size, shard_rows, me)[None, :]
    turn, turned_tokens, sent_hot = prepare(tokens, held_rows, own_codes, size, table_rows)
    packed_ids, turned_tokens, sent_hot, heads_far, in_shard = together(
        packed_ids, turned_tokens, sent_hot, heads_far, in_weight
    )

    all_ids = lax.all_to_all(packed_ids, "dp", 0, 0)
    heads_near = spread_near(heads_far)
    in_far = spread_far(in_shard)
    down_shard = down_weight.T
    vectors = jnp.stack(
        [out_bias, norm1_gain, norm1_bias, down_bias, norm2_gain, norm2_bias] + [out_bias] * 2
    )
    round_turn, _ = together(turn, in_shard)
    sents = from_cores(sent_hot)
    grad_final, vectors = turn_small(
        cotangent.reshape(slots, width), codes, vectors, round_turn
    )
    hidden_bias = in_bias[None]
    all_ids, heads_near, in_far, down_shard, grad_final = together(
        all_ids, heads_near, in_far, down_shard, grad_final
    )

    is_used = jnp.arange(slot_count)[None, None, :] < all_ids[:, :, slot_count : slot_count + 1]
    all_codes = jnp.where(is_used, all_ids[:, :, :slot_count], -1)
    all_codes = all_codes.reshape(size * cores, own_slots)
    *hots, found, fullest = serve(places, all_codes, embed_table, size, cores)
    found, heads_near, in_far = together(found, heads_near, in_far)
    found = lax.all_to_all(found.reshape(size, ROOM, width), "dp", 0, 0)
    found = found.reshape(size * ROOM, width)
    heads_here, heads_there = spread_last(heads_near)
    down_far = spread_far(down_shard)
    in_near = spread_near(in_far)

    rounds = (fullest.reshape(()) + ROOM - 1) // ROOM

    def round_of(turn_, held):
        own, every, held = lax.optimization_barrier((own_codes[0], all_codes, held))
        low = turn_ * ROOM
        spots = jnp.arange(own_slots)
        before = (spots[:, None] < spots[None, :]).astype(BF)
        to_owner = (own >= 0)[:, None] & (own[:, None] // table_rows == jnp.arange(size))
        rank = tn(before, to_owner.astype(BF)).astype(jnp.int32) - low
        sent = (rank[:, :, None] == jnp.arange(ROOM)) & to_owner[:, :, None]
        sent = sent.astype(BF).reshape(own_slots, size * ROOM)
        mine = (every >= 0) & (every // table_rows == me)
        rank = dot(mine.astype(BF), before).astype(jnp.int32) - low
        hit = (rank[:, None, :] == jnp.arange(ROOM)[None, :, None]) & mine[:, None, :]
        asked = jnp.sum(jnp.where(hit, every[:, None, :] - me * table_rows + 1, 0), axis=2) - 1
        hot = (asked[:, :, None] == jnp.arange(table_rows)).astype(BF)
        hot = hot.reshape(size, cores, ROOM, table_rows)
        turned = [
            lax.dynamic_index_in_dim(hot, (core + cores - k) % cores, 1, keepdims=False)
            for k in range(cores)
        ]
        return sent, [t.reshape(size * ROOM, table_rows) for t in turned], held

    def more_rows(turn_, held):
        sent, later, held = round_of(turn_, held)
        got = dot(later[0], embed_table).astype(BF).reshape(size, ROOM, width)
        got = lax.all_to_all(got, "dp", 0, 0).reshape(size * ROOM, width)
        return held + in_core_order(from_cores(dot(sent, got).astype(BF)))

    more = lax.fori_loop(1, rounds, more_rows, jnp.zeros((slots, width), F32))
    founds = from_cores(found)
    heads_pieces = in_order(heads_here, heads_there)
    embedded, low, query, key, value, s_embedded, s_low, s_query, s_attended, s_part = enter(
        places,
        turned_tokens,
        founds,
        sents,
        more,
        turn,
        masked_pos,
        qv_bias,
        heads_pieces,
    )
    down_near = spread_near(down_far)
    in_here, in_there = spread_last(in_near)
    s_part, down_near, in_here, in_there, query = together(
        s_part, down_near, in_here, in_there, query
    )

    down_pieces = last_of(down_near)
    s_parts = from_cores(s_part)
    rows_part = attend_all(query, key, value, heads_pieces, pages)
    s_parts, down_pieces, rows_part = together(s_parts, down_pieces, rows_part)

    in_pieces = in_order(in_here, in_there)
    unit1, scale1, middle_low, hidden, slope, s_part = slot_forward(
        s_parts, s_embedded, vectors, hidden_bias, in_pieces, down_pieces
    )
    s_parts = from_cores(s_part)
    *grad_down, grad_r2, grad_hidden_in, small2, grad_in_bias, s_part = slot_turn(
        s_parts, hidden, slope, unit1, grad_final, vectors, in_pieces, down_pieces
    )

    s_parts = from_cores(s_part)
    rows_parts = from_cores(rows_part)
    down_sum = sum_first(grad_down)
    grad_in = in_grad(middle_low, grad_hidden_in, [p.shape[0] for p in in_pieces])
    s_parts, grad_in = together(s_parts, grad_in)

    in_sum = sum_first(grad_in)
    *grad_heads, grad_r1, part, small1, small0 = slot_back(
        s_parts,
        grad_r2,
        unit1,
        scale1,
        s_attended,
        s_query,
        key,
        value,
        s_low,
        low,
        vectors,
        masked_pos,
        heads_pieces,
    )
    down_sum, in_sum, grad_heads, part, rows_parts = together(
        down_sum, in_sum, grad_heads, part, rows_parts
    )

    heads_sum = sum_first(grad_heads)
    units_sum = sum_second(down_sum, in_sum)
    parts = from_cores(part)
    middle, rows_part = rows_forward(
        rows_parts, embedded, vectors, hidden_bias, in_pieces, down_pieces
    )
    grad_input, moved, own_grad = leave(
        places,
        parts,
        grad_r1,
        masked_pos,
        turn,
        held_rows,
        sent_hot,
        [small1, small2, small0, grad_in_bias],
        size,
    )

    gots = lax.all_to_all(moved, "dp", 0, 0)
    units_sum = sum_far(units_sum)
    heads_sum = sum_second(heads_sum)
    output = rows_end(from_cores(rows_part), middle, vectors, turn)
    units_sum, heads_sum, output, gots = together(units_sum, heads_sum, output, gots)

    heads_sum = sum_far(heads_sum)
    grad_table, totals = collect(hots, from_cores(gots))
    units_share = add_up(units_sum)
    down_share, in_share = units_share[:, :hidden_cols].T, units_share[:, hidden_cols:]
    def more_table(turn_, held):
        sent, later, held = round_of(turn_, held)
        got = tn(sent, own_grad).astype(BF).reshape(size, ROOM, width)
        for hot, block in zip(later, from_cores(lax.all_to_all(got, "dp", 0, 0))):
            held = held + tn(hot, block.reshape(size * ROOM, width))
        return held

    grad_table = lax.fori_loop(1, rounds, more_table, grad_table)
    def piece(row, block, count):
        return totals[row, block * 128 : block * 128 + count]

    vec = [piece(0, k, shard_rows) for k in range(6)]
    own = [
        piece(1, 0, head_cols // size),
        piece(1, 1, head_cols // size),
        piece(1, 2, hidden_cols // size),
    ]
    heads_sum, in_share, down_share, grad_table, vec, own = together(
        heads_sum, in_share, down_share, grad_table, vec, own
    )
    heads_share = add_up(heads_sum)
    qkv_share = heads_share[:, : 3 * head_cols].reshape(shard_rows, 3, head_cols)
    out_share = heads_share[:, 3 * head_cols :].T


    return (
        output,
        grad_input,
        grad_table,
        qkv_share,
        jnp.stack([own[0], own[1]])[:, None, :],
        out_share,
        vec[0],
        vec[1],
        vec[2],
        in_share,
        own[2][None],
        down_share,
        vec[3],
        vec[4],
        vec[5],
    )


def solution(mesh):
    in_specs = (
        P("dp", None),
        P("dp", None),
        P("dp", None, "mp"),
        P(None, "mp"),
        P("mp", "dp"),
        P(),
        P(),
        P(),
        P("dp", "mp"),
        P("mp"),
        P("mp", "dp"),
        P(),
        P(),
        P(),
        P("dp", None),
        P("dp", None),
        P("dp"),
        P("dp", None, None),
    )
    out_specs = (
        P("dp", None),
        P("dp", None),
        P("dp", None),
        P("dp", None, "mp"),
        P(None, "mp", "dp"),
        P("mp", "dp"),
        P("dp"),
        P("dp"),
        P("dp"),
        P("dp", "mp"),
        P("mp", "dp"),
        P("mp", "dp"),
        P("dp"),
        P("dp"),
        P("dp"),
    )
    return jax.shard_map(
        per_device, mesh=mesh, in_specs=in_specs, out_specs=out_specs, check_vma=False
    )
```
